128 devices in a mesh: slab: 16 (over z, y), angle: 8 (over x, core).
Axes of the slice: x: 4, y: 4, z: 4, core: 2. Of those that a mesh axis runs over, the one named last changes fastest.
Arguments:
- volume0: float32 [128, 512, 128], P('slab'), may hold values from -6 to 6
- weights: bfloat16 [16, 8, 3, 512, 4096], P('slab', 'angle'), as said below
- tile_block: int32 [16, 8, 3], P('slab', 'angle'), may hold values from 0 to 15, as said below
- tile_count: int32 [16, 8], P('slab', 'angle'), may hold values from 1 to 3, as said below
- owner: int32 [8, 16], P('angle'), may hold values from 0 to 15, as said below
- sino: bfloat16 [8, 16, 512, 128], P('angle', 'slab'), may hold values from -4 to 12
- weight_z: bfloat16 [128, 512, 128], P('slab'), may hold values from 0.25 to 2
- weight_y: bfloat16 [128, 512, 128], P('slab'), may hold values from 0.25 to 2
- weight_x: bfloat16 [128, 512, 128], P('slab'), may hold values from 0.25 to 2
Outputs:
- volume: float32 [128, 512, 128], P('slab', None, 'angle')
- residual: float32 [8, 16, 512, 128], P('angle', 'slab')
The draws below stay inside these ranges and needn't reach their ends.
Inputs may be any that keep to these rules, and one draw needn't show every extreme that they name: `tile_block`: slot 0 of slab s names owner[a, s]. Slot t of slab s names owner[a, (s + d) % 16] for a distance d in 0 to 2 that differs between the slots of one slab; for a live slot, s + d stays below 16. So a live tile's block is held by its own slab or by one of the 2 slabs above it, and the 3 slots of one slab name different ray blocks. Slots t with t >= tile_count[s, a] are unused; the count 3 is reached on some device. `owner`: each row names every ray block of its angle group once. `weights`: entries are positive.
All inputs are finite; a program needn't handle non-finite values.
Results may differ from the reference program's by a relative error of at most 0.013.
Values may be sent and summed in bfloat16 or wider, within the bound.
A program may use at most 128 MiB of HBM per device.

```python
import math
import jax
import jax.numpy as jnp
from jax import lax

NY = 512
CZ = 8
NX = 128
RB = 512
TPD = 3
ITERS = 3
NB = 16
NZ = 128
VOXP = 4096
N_SLAB = 16
N_ANGLE = 8


def draw_volume0(key, part):
    key_one, key_two, key_three, key_four = jax.random.split(jax.random.fold_in(key, 53), 4)
    shape_all = (NZ, NY, NX)
    y_pos = (lax.broadcasted_iota(jnp.float32, (1, NY, 1), 1) + 0.5) / NY
    x_pos = (lax.broadcasted_iota(jnp.float32, (1, 1, NX), 2) + 0.5) / NX
    amplitudes = jax.random.uniform(key_two, (3,), jnp.float32, 0.3, 0.6)
    phases = jax.random.uniform(key_three, (3,), jnp.float32, 0.0, 2.0 * math.pi)
    tilt = jax.random.uniform(key_four, (), jnp.float32, 0.0, 2.0 * math.pi)
    smooth = jnp.zeros((1, NY, 1), jnp.float32)
    for harmonic in range(3):
        smooth = smooth + amplitudes[harmonic] * jnp.cos(2.0 * math.pi * (harmonic + 1) * y_pos + phases[harmonic])
    modulation = 1.0 + 0.5 * jnp.cos(2.0 * math.pi * x_pos + tilt)
    roughness = jnp.clip(jax.random.normal(key_one, shape_all, jnp.float32), -3.0, 3.0)
    return roughness + smooth * modulation


def draw_weights(key, part):
    base_key = jax.random.fold_in(key, 11)
    spacing = NY / RB

    def one_slab(slab_index):
        slab_key = jax.random.fold_in(base_key, slab_index)
        key_one, key_two, key_three, key_four, key_five, key_six, key_seven = jax.random.split(slab_key, 7)
        shape_slab = (N_ANGLE, TPD, RB, VOXP)
        roughness = jax.random.uniform(key_two, shape_slab, jnp.float32, 0.5, 1.5)
        spread = jax.random.uniform(key_one, shape_slab, jnp.float32, 0.5, 1.5)
        offset = jax.random.uniform(key_three, (N_ANGLE, TPD, 1, 1), jnp.float32, 0.0, float(RB))
        slope = jax.random.uniform(key_four, (N_ANGLE, TPD, 1, 1), jnp.float32, -1.5, 1.5)
        low_amps = jax.random.uniform(key_seven, (6, N_ANGLE, TPD, 1, 1), jnp.float32, 0.3, 0.6)
        high_amps = jax.random.uniform(jax.random.fold_in(key_seven, 3), (6, N_ANGLE, TPD, 1, 1), jnp.float32, 0.1, 0.3)
        ray_ids = lax.broadcasted_iota(jnp.float32, (1, 1, RB, 1), 2)
        voxel_ids = lax.broadcasted_iota(jnp.int32, (1, 1, 1, VOXP), 3)
        depth = (slab_index * CZ + voxel_ids // NY).astype(jnp.float32)
        column = (voxel_ids % NY).astype(jnp.float32)
        center = ray_ids + 0.5 + offset + slope * depth
        gap_size = jnp.mod(column + 0.5 - center, float(NY))
        distance = jnp.minimum(gap_size, float(NY) - gap_size)
        peak = jnp.maximum(0.0, 1.0 - distance)
        theta = 2.0 * math.pi / NY * gap_size
        exponent = jnp.zeros(shape_slab, jnp.float32)
        for harmonic in range(6):
            amplitude = low_amps[harmonic] if harmonic < 3 else high_amps[harmonic]
            exponent = exponent + amplitude * jnp.cos((harmonic + 1) * theta)
        background = spacing / NY * jnp.exp(exponent) * spread
        row_factor = jnp.exp(jax.random.uniform(key_five, (N_ANGLE, TPD, RB, 1), jnp.float32, 0.0, math.log(10.0)))
        col_factor = jnp.exp(jax.random.uniform(key_six, (N_ANGLE, 1, 1, VOXP), jnp.float32, 0.0, math.log(10.0)))
        base_scale = 1.0 / (8.0 * CZ)
        return base_scale * (peak * roughness + background) * row_factor * col_factor
    return lax.map(one_slab, jnp.arange(N_SLAB, dtype=jnp.int32)).astype(jnp.bfloat16)


def angle_orders(key):
    angle_keys = jax.random.split(jax.random.fold_in(key, 23), N_ANGLE)
    return jax.vmap(lambda single_key: jax.random.permutation(single_key, NB))(angle_keys).astype(jnp.int32)


def slot_distances(key):
    scores = jax.random.randint(jax.random.fold_in(key, 29), (N_SLAB, N_ANGLE, TPD - 1), 0, 1 << 20, jnp.int32)
    distinct = scores * TPD + jnp.arange(TPD - 1, dtype=jnp.int32)[None, None, :]
    ordering = jnp.argsort(distinct, axis=2).astype(jnp.int32) + 1
    return jnp.concatenate([jnp.zeros((N_SLAB, N_ANGLE, 1), jnp.int32), ordering], axis=2).astype(jnp.int32)


def draw_owner(key, part):
    return angle_orders(key)


def draw_tile_block(key, part):
    table = angle_orders(key)
    slab_ids = jnp.arange(N_SLAB, dtype=jnp.int32)[:, None, None]
    held = ((slab_ids + slot_distances(key)) % N_SLAB).astype(jnp.int32)
    broad = jnp.broadcast_to(table[None, :, :], (N_SLAB, N_ANGLE, NB))
    return jnp.take_along_axis(broad, held, axis=2).astype(jnp.int32)


def draw_tile_count(key, part):
    slab_ids = jnp.arange(N_SLAB, dtype=jnp.int32)[:, None, None]
    valid = (slab_ids + slot_distances(key) < N_SLAB).astype(jnp.int32)
    limit = jnp.sum(jnp.cumprod(valid, axis=2), axis=2).astype(jnp.int32)
    key_one, key_two, key_three = jax.random.split(jax.random.fold_in(key, 37), 3)
    counts = jax.random.randint(key_one, (N_SLAB, N_ANGLE), 1, TPD + 1, jnp.int32)
    counts = jnp.minimum(counts, limit)
    chosen_slab = jax.random.randint(key_two, (), 0, N_SLAB - TPD + 1, jnp.int32)
    chosen_angle = jax.random.randint(key_three, (), 0, N_ANGLE, jnp.int32)
    slab_grid = lax.broadcasted_iota(jnp.int32, (N_SLAB, N_ANGLE), 0)
    angle_grid = lax.broadcasted_iota(jnp.int32, (N_SLAB, N_ANGLE), 1)
    hit = (slab_grid == chosen_slab) & (angle_grid == chosen_angle)
    return jnp.where(hit, TPD, counts).astype(jnp.int32)


def draw_sino(key, part):
    key_one, key_two, key_three, key_four, key_five = jax.random.split(jax.random.fold_in(key, 41), 5)
    shape_all = (N_ANGLE, NB, RB, NX)
    ray_pos = lax.broadcasted_iota(jnp.float32, (1, 1, RB, 1), 2) / RB
    col_pos = lax.broadcasted_iota(jnp.float32, (1, 1, 1, NX), 3) / NX
    phase_one = jax.random.uniform(key_one, (N_ANGLE, NB, 1, 1), jnp.float32, 0.0, 2.0 * math.pi)
    phase_two = jax.random.uniform(key_two, (N_ANGLE, NB, 1, 1), jnp.float32, 0.0, 2.0 * math.pi)
    freq_ray = jax.random.uniform(key_three, (N_ANGLE, NB, 1, 1), jnp.float32, 1.0, 3.0)
    freq_col = jax.random.uniform(key_four, (N_ANGLE, NB, 1, 1), jnp.float32, 1.0, 3.0)
    smooth = jnp.sin(2.0 * math.pi * freq_ray * ray_pos + phase_one) * jnp.cos(2.0 * math.pi * freq_col * col_pos + phase_two)
    roughness = 0.5 * jnp.clip(jax.random.normal(key_five, shape_all, jnp.float32), -3.0, 3.0)
    level = 1.0
    return jnp.clip(4.0 * (level + 0.6 * smooth + roughness), -4.0, 12.0).astype(jnp.bfloat16)


def levels(key, dims, cuts, low, largest):
    gain = 1.0
    for dim, shards_of in cuts:
        steps = jax.random.uniform(jax.random.fold_in(jax.random.fold_in(key, 6), dim), (shards_of,), jnp.float32, low / len(cuts), largest / len(cuts))
        gain = gain * jnp.repeat(jnp.exp(steps), dims[dim] // shards_of).reshape((-1,) + (1,) * (len(dims) - 1 - dim))
    return gain


def setup_inputs(seed: int = 0) -> dict:
    key_of = jax.random.split(jax.random.key(seed), 10)
    volume0 = draw_volume0(jax.random.fold_in(key_of[9], 71), 0)
    weights = draw_weights(jax.random.fold_in(key_of[9], 71), 0)
    tile_block = draw_tile_block(jax.random.fold_in(key_of[9], 71), 0)
    tile_count = draw_tile_count(jax.random.fold_in(key_of[9], 71), 0)
    owner = draw_owner(jax.random.fold_in(key_of[9], 71), 0)
    sino = draw_sino(jax.random.fold_in(key_of[9], 71), 0)
    weight_z = jnp.clip(jnp.exp(math.log(2.0) - 2.0794415 * jax.random.uniform(key_of[6], (NZ, NY, NX), jnp.float32) ** levels(key_of[6], (NZ, NY, NX), ((0, 16),), -0.2, 0.2)), 0.25, 2.0).astype(jnp.bfloat16)
    weight_y = jnp.clip(jnp.exp(math.log(2.0) - 2.0794415 * jax.random.uniform(key_of[7], (NZ, NY, NX), jnp.float32) ** levels(key_of[7], (NZ, NY, NX), ((0, 16),), -0.2, 0.2)), 0.25, 2.0).astype(jnp.bfloat16)
    weight_x = jnp.clip(jnp.exp(math.log(2.0) - 2.0794415 * jax.random.uniform(key_of[8], (NZ, NY, NX), jnp.float32) ** levels(key_of[8], (NZ, NY, NX), ((0, 16),), -0.2, 0.2)), 0.25, 2.0).astype(jnp.bfloat16)
    return dict(volume0=volume0, weights=weights, tile_block=tile_block, tile_count=tile_count, owner=owner, sino=sino, weight_z=weight_z, weight_y=weight_y, weight_x=weight_x)


SMOOTH_EPS = 0.01
SMOOTH_RATE = 0.15

def limiter(difference):
    return difference / jnp.sqrt(difference * difference + SMOOTH_EPS)

def smoothing(volume, weight_z, weight_y, weight_x):
    change = jnp.zeros_like(volume)
    for axis_num, weight_val in ((0, weight_z), (1, weight_y), (2, weight_x)):
        length = volume.shape[axis_num]
        first_cut = lax.slice_in_dim(volume, 0, 1, axis=axis_num)
        following = jnp.concatenate([lax.slice_in_dim(volume, 1, length, axis=axis_num), jnp.zeros_like(first_cut)], axis=axis_num)
        inside = (lax.broadcasted_iota(jnp.int32, volume.shape, axis_num) < length - 1).astype(jnp.float32)
        face_flux = weight_val.astype(jnp.float32) * limiter(following - volume) * inside
        previous = jnp.concatenate([jnp.zeros_like(first_cut), lax.slice_in_dim(face_flux, 0, length - 1, axis=axis_num)], axis=axis_num)
        change = change + face_flux - previous
    return volume + SMOOTH_RATE * change

def reference(volume0, weights, tile_block, tile_count, owner, sino, weight_z, weight_y, weight_x):
    live_slots = jnp.arange(TPD, dtype=jnp.int32)[None, None, :] < tile_count[:, :, None]
    select = ((owner[None, :, None, :] == tile_block[:, :, :, None]) & live_slots[:, :, :, None]).astype(jnp.float32)
    live_float = live_slots.astype(jnp.float32)

    def totals(slab_index):
        tiles = weights[slab_index].astype(jnp.float32)
        return (lax.optimization_barrier(jnp.sum(tiles, axis=3)), jnp.einsum('at,atrv->v', live_float[slab_index], tiles))
    ray_sums, voxel_sums = lax.map(totals, jnp.arange(N_SLAB))
    ray_scale = 1.0 / jnp.einsum('satj,satr->ajr', select, ray_sums)
    voxel_scale = (1.0 / voxel_sums).reshape(NZ, NY, 1)
    volume = volume0
    residual = jnp.zeros((N_ANGLE, NB, RB, NX), jnp.float32)
    for iteration in range(ITERS):
        slabs = volume.astype(jnp.bfloat16).reshape(N_SLAB, VOXP, NX)

        def forward(carried, slab_index):
            tiles = weights[slab_index].astype(jnp.float32)
            products = jnp.einsum('atrv,vn->atrn', tiles, slabs[slab_index].astype(jnp.float32))
            products = lax.optimization_barrier(products.astype(jnp.bfloat16)).astype(jnp.float32)
            return (carried + jnp.einsum('atj,atrn->ajrn', select[slab_index], products), None)
        projected, unused = lax.scan(forward, jnp.zeros((N_ANGLE, NB, RB, NX), jnp.float32), jnp.arange(N_SLAB))
        residual = (sino.astype(jnp.float32) - projected) * ray_scale[..., None]
        rounded = lax.optimization_barrier(residual.astype(jnp.bfloat16)).astype(jnp.float32)

        def backward(slab_index):
            tiles = weights[slab_index].astype(jnp.float32)
            picked = jnp.einsum('atj,ajrn->atrn', select[slab_index], rounded)
            return jnp.einsum('atrv,atrn->vn', tiles, picked)
        back = lax.map(backward, jnp.arange(N_SLAB)).reshape(NZ, NY, NX)
        volume = volume + voxel_scale * back
        volume = smoothing(volume, weight_z, weight_y, weight_x)
    return (volume, residual)
```

```python
import functools

import jax
import jax.numpy as jnp
from jax import lax
from jax.experimental import pallas as pl
from jax.experimental.pallas import tpu as pltpu
from jax.sharding import PartitionSpec as P

ITERS = 3


SMOOTH_EPS = 0.01
SMOOTH_RATE = 0.15

MESH_ID = pl.DeviceIdType.MESH


def from_behind(value, axis, steps):
    count = lax.axis_size(axis)
    first, last = (max(0, -steps), min(count, count - steps))
    return lax.ppermute(value, axis, [(source, source + steps) for source in range(first, last)])


def limiter(difference):
    return difference / jnp.sqrt(difference * difference + SMOOTH_EPS)


def _where_am_i():
    slab = lax.axis_index("slab")
    here = lax.axis_index("angle")
    chip = here // 2
    core = here % 2
    partner = here + 1 - 2 * core
    return slab, here, chip, core, partner


def _greet(slab, chip, core, partner, n_chip):
    barrier = pltpu.get_barrier_semaphore()
    pl.semaphore_signal(barrier, 1, device_id=(slab, partner), device_id_type=MESH_ID)
    for d in range(1, n_chip):
        peer = ((chip + d) % n_chip) * 2 + core
        pl.semaphore_signal(barrier, 1, device_id=(slab, peer), device_id_type=MESH_ID)
    pl.semaphore_wait(barrier, n_chip)


def _scatter_kernel(n_chip, part_ref, out_ref, got_pair, got_ring, chip_sum,
                    send_a, recv_a, send_b, recv_b):
    slab, here, chip, core, partner = _where_am_i()
    _greet(slab, chip, core, partner, n_chip)
    pair = []
    for k in range(n_chip):
        copy = pltpu.make_async_remote_copy(
            src_ref=part_ref.at[2 * k + 1 - core],
            dst_ref=got_pair.at[k],
            send_sem=send_a.at[k],
            recv_sem=recv_a.at[k],
            device_id=(slab, partner),
            device_id_type=MESH_ID,
        )
        copy.start()
        pair.append(copy)
    for copy in pair:
        copy.wait()
    for k in range(n_chip):
        chip_sum[k] = part_ref[2 * k + core] + got_pair[k]
    ring = []
    for d in range(1, n_chip):
        dest = (chip + d) % n_chip
        copy = pltpu.make_async_remote_copy(
            src_ref=chip_sum.at[dest],
            dst_ref=got_ring.at[d],
            send_sem=send_b.at[d],
            recv_sem=recv_b.at[d],
            device_id=(slab, 2 * dest + core),
            device_id_type=MESH_ID,
        )
        copy.start()
        ring.append(copy)
    for copy in ring:
        copy.wait()
    total = chip_sum[chip]
    for d in range(1, n_chip):
        total = total + got_ring[d]
    out_ref[...] = total


def scatter_angle(part):
    blocks, rows, cols = part.shape
    n_chip = blocks // 2
    return pl.pallas_call(
        functools.partial(_scatter_kernel, n_chip),
        out_shape=jax.ShapeDtypeStruct((rows, cols), jnp.float32),
        in_specs=[pl.BlockSpec(memory_space=pltpu.VMEM)],
        out_specs=pl.BlockSpec(memory_space=pltpu.VMEM),
        scratch_shapes=[
            pltpu.VMEM((n_chip, rows, cols), jnp.float32),
            pltpu.VMEM((n_chip, rows, cols), jnp.float32),
            pltpu.VMEM((n_chip, rows, cols), jnp.float32),
            pltpu.SemaphoreType.DMA((n_chip,)),
            pltpu.SemaphoreType.DMA((n_chip,)),
            pltpu.SemaphoreType.DMA((n_chip,)),
            pltpu.SemaphoreType.DMA((n_chip,)),
        ],
        compiler_params=pltpu.CompilerParams(collective_id=0, has_side_effects=True),
        cost_estimate=pl.CostEstimate(
            flops=2 * blocks * rows * cols, bytes_accessed=4 * 3 * blocks * rows * cols,
            transcendentals=0,
        ),
    )(part)


def _gather_kernel(n_chip, own_ref, out_ref, held, send_a, recv_a, send_b, recv_b, local_sem):
    slab, here, chip, core, partner = _where_am_i()
    _greet(slab, chip, core, partner, n_chip)
    mine = pltpu.make_async_copy(own_ref, held.at[here], local_sem.at[0])
    mine.start()
    ring = []
    for d in range(1, n_chip):
        dest = (chip + d) % n_chip
        copy = pltpu.make_async_remote_copy(
            src_ref=own_ref,
            dst_ref=held.at[here],
            send_sem=send_a.at[d],
            recv_sem=recv_a.at[d],
            device_id=(slab, 2 * dest + core),
            device_id_type=MESH_ID,
        )
        copy.start()
        ring.append(copy)
    mine.wait()
    for copy in ring:
        copy.wait()
    pair = []
    for k in range(n_chip):
        copy = pltpu.make_async_remote_copy(
            src_ref=held.at[2 * k + core],
            dst_ref=held.at[2 * k + core],
            send_sem=send_b.at[k],
            recv_sem=recv_b.at[k],
            device_id=(slab, partner),
            device_id_type=MESH_ID,
        )
        copy.start()
        pair.append(copy)
    for copy in pair:
        copy.wait()
    out_ref[...] = held[...]


def gather_angle(own, groups):
    rows, cols = own.shape
    n_chip = groups // 2
    return pl.pallas_call(
        functools.partial(_gather_kernel, n_chip),
        out_shape=jax.ShapeDtypeStruct((groups, rows, cols), own.dtype),
        in_specs=[pl.BlockSpec(memory_space=pltpu.VMEM)],
        out_specs=pl.BlockSpec(memory_space=pltpu.VMEM),
        scratch_shapes=[
            pltpu.VMEM((groups, rows, cols), own.dtype),
            pltpu.SemaphoreType.DMA((n_chip,)),
            pltpu.SemaphoreType.DMA((n_chip,)),
            pltpu.SemaphoreType.DMA((n_chip,)),
            pltpu.SemaphoreType.DMA((n_chip,)),
            pltpu.SemaphoreType.DMA((1,)),
        ],
        compiler_params=pltpu.CompilerParams(collective_id=1, has_side_effects=True),
        cost_estimate=pl.CostEstimate(
            flops=0, bytes_accessed=2 * 2 * groups * rows * cols, transcendentals=0,
        ),
    )(own)


def smooth_share(
    volume,
    weight_z,
    weight_y,
    weight_x,
    lower_rim,
    left_rim,
    z_first,
    z_total,
    x_first,
    x_total,
):
    upper_halo = from_behind(volume[:, 0], "slab", -1)
    lower_halo = from_behind(volume[:, -1], "slab", 1)
    right_halo = from_behind(volume[0], "angle", -1)
    left_halo = from_behind(volume[-1], "angle", 1)
    upper = jnp.concatenate([volume[:, 1:], upper_halo[:, None]], axis=1)
    inside = (z_first + lax.broadcasted_iota(jnp.int32, volume.shape, 1) + 1 < z_total).astype(
        jnp.float32
    )
    face_flux = weight_z * limiter(upper - volume) * inside
    lower_flux = lower_rim * limiter(volume[:, 0] - lower_halo)
    previous = jnp.concatenate([lower_flux[:, None], face_flux[:, :-1]], axis=1)
    change = face_flux - previous
    following = jnp.concatenate([volume[:, :, 1:], jnp.zeros_like(volume[:, :, :1])], axis=2)
    inside = (lax.broadcasted_iota(jnp.int32, volume.shape, 2) < volume.shape[2] - 1).astype(
        jnp.float32
    )
    face_flux = weight_y * limiter(following - volume) * inside
    previous = jnp.concatenate([jnp.zeros_like(face_flux[:, :, :1]), face_flux[:, :, :-1]], axis=2)
    change = change + face_flux - previous
    following = jnp.concatenate([volume[1:], right_halo[None]], axis=0)
    inside = (x_first + lax.broadcasted_iota(jnp.int32, volume.shape, 0) + 1 < x_total).astype(
        jnp.float32
    )
    face_flux = weight_x * limiter(following - volume) * inside
    lower_flux = left_rim * limiter(volume[0] - left_halo)
    previous = jnp.concatenate([lower_flux[None], face_flux[:-1]], axis=0)
    change = change + face_flux - previous
    return volume + SMOOTH_RATE * change


def shards(volume0, weights, tile_block, tile_count, owner, sino, weight_z, weight_y, weight_x):
    tiles = weights[0, 0]
    slot_count, ray_count, voxels = tiles.shape
    slab_depth, height, column_count = volume0.shape
    blocks = tile_block[0, 0]
    live_count = tile_count[0, 0]
    owner_row = owner[0]
    live_slots = jnp.arange(slot_count, dtype=jnp.int32) < live_count
    select = (owner_row[None, :] == blocks[:, None]) & live_slots[:, None]
    slab_pos = lax.axis_index("slab")
    holder_ids = jnp.arange(owner_row.shape[0], dtype=jnp.int32)
    target = jnp.sum(jnp.where(select, holder_ids[None, :], 0), axis=1)
    distance_ids = jnp.arange(slot_count, dtype=jnp.int32)
    relative = ((target - slab_pos)[:, None] == distance_ids[None, :]) & live_slots[:, None]
    relative_float = relative.astype(jnp.float32)
    relative_half = relative.astype(jnp.bfloat16)
    flat_tiles = tiles.reshape(slot_count * ray_count, voxels)
    ray_local = jnp.dot(
        flat_tiles, jnp.ones((voxels,), jnp.bfloat16), preferred_element_type=jnp.float32
    )
    ray_sends = jnp.einsum("td,tr->dr", relative_float, ray_local.reshape(slot_count, ray_count))
    ray_total = ray_sends[0]
    for distance in range(1, slot_count):
        ray_total = ray_total + from_behind(ray_sends[distance], "slab", distance)
    live_rows = jnp.repeat(live_slots, ray_count).astype(jnp.bfloat16)
    voxel_local = jnp.dot(live_rows, flat_tiles, preferred_element_type=jnp.float32)
    voxel_total = lax.psum(voxel_local, "angle")
    ray_scale = 1.0 / ray_total
    voxel_scale = (1.0 / voxel_total).reshape(1, slab_depth, height)
    lower_all = from_behind(weight_z[slab_depth - 1], "slab", 1)
    z_first = slab_pos * slab_depth
    z_total = slab_depth * lax.axis_size("slab")
    groups = lax.axis_size("angle")
    share_width = column_count // groups
    angle_pos = lax.axis_index("angle")
    share_first = angle_pos * share_width

    def share_of(array):
        part = lax.dynamic_slice_in_dim(array, share_first, share_width, array.ndim - 1)
        return jnp.moveaxis(part, -1, 0).astype(jnp.float32)

    measured = sino[0, 0].astype(jnp.float32)
    volume = share_of(volume0)
    local_z = share_of(weight_z)
    local_y = share_of(weight_y)
    local_x = share_of(weight_x)
    lower_rim = share_of(lower_all)
    left_index = jnp.maximum(share_first - 1, 0)
    left_rim = lax.dynamic_index_in_dim(weight_x, left_index, 2, keepdims=False).astype(
        jnp.float32
    ) * (angle_pos > 0).astype(jnp.float32)
    gathered = None
    residual = jnp.zeros((ray_count, column_count), jnp.float32)
    for iteration in range(ITERS):
        if gathered is None:
            flat_volume = volume0.astype(jnp.bfloat16).reshape(voxels, column_count)
            products = jnp.einsum(
                "trv,vn->trn", tiles, flat_volume, preferred_element_type=jnp.float32
            ).astype(jnp.bfloat16)
        else:
            products = jnp.einsum(
                "trv,nv->trn", tiles, gathered, preferred_element_type=jnp.float32
            ).astype(jnp.bfloat16)
        sends = jnp.einsum(
            "td,trn->drn", relative_half, products, preferred_element_type=jnp.float32
        )
        sends_half = sends.astype(jnp.bfloat16)
        projected = sends[0]
        for distance in range(1, slot_count):
            arrived = from_behind(sends_half[distance], "slab", distance)
            projected = projected + arrived.astype(jnp.float32)
        residual = (measured - projected) * ray_scale[:, None]
        residual_half = residual.astype(jnp.bfloat16)
        nearby = [residual_half] + [
            from_behind(residual_half, "slab", -distance) for distance in range(1, slot_count)
        ]
        picked = jnp.einsum(
            "td,drn->trn", relative_half, jnp.stack(nearby), preferred_element_type=jnp.float32
        ).astype(jnp.bfloat16)
        back_t = jnp.einsum("trn,trv->nv", picked, tiles, preferred_element_type=jnp.float32)
        back_own = scatter_angle(back_t.reshape(groups, share_width, voxels))
        volume = volume + voxel_scale * back_own.reshape(share_width, slab_depth, height)
        volume = smooth_share(
            volume,
            local_z,
            local_y,
            local_x,
            lower_rim,
            left_rim,
            z_first,
            z_total,
            share_first,
            column_count,
        )
        if iteration + 1 < ITERS:
            own_half = volume.astype(jnp.bfloat16).reshape(share_width, voxels)
            gathered = gather_angle(own_half, groups).reshape(column_count, voxels)
    volume_out = jnp.moveaxis(volume, 0, -1)
    return (volume_out, residual[None, None])


def solution(mesh):
    in_specs = (
        P("slab", None, None),
        P("slab", "angle", None, None, None),
        P("slab", "angle", None),
        P("slab", "angle"),
        P("angle", None),
        P("angle", "slab", None, None),
        P("slab", None, None),
        P("slab", None, None),
        P("slab", None, None),
    )
    out_specs = (P("slab", None, "angle"), P("angle", "slab", None, None))
    return jax.shard_map(shards, mesh=mesh, in_specs=in_specs, out_specs=out_specs, check_vma=False)
```

```python
import functools

import jax
import jax.numpy as jnp
from jax import lax
from jax.experimental import pallas as pl
from jax.experimental.pallas import tpu as pltpu
from jax.sharding import PartitionSpec as P

ITERS = 3


SMOOTH_EPS = 0.01
SMOOTH_RATE = 0.15

MESH_ID = pl.DeviceIdType.MESH


def from_behind(value, axis, steps):
    count = lax.axis_size(axis)
    first, last = (max(0, -steps), min(count, count - steps))
    return lax.ppermute(value, axis, [(source, source + steps) for source in range(first, last)])


def limiter(difference):
    return difference / jnp.sqrt(difference * difference + SMOOTH_EPS)


def _where_am_i():
    slab = lax.axis_index("slab")
    here = lax.axis_index("angle")
    chip = here // 2
    core = here % 2
    partner = here + 1 - 2 * core
    return slab, here, chip, core, partner


def _greet(slab, chip, core, partner, n_chip):
    barrier = pltpu.get_barrier_semaphore()
    pl.semaphore_signal(barrier, 1, device_id=(slab, partner), device_id_type=MESH_ID)
    for d in range(1, n_chip):
        peer = ((chip + d) % n_chip) * 2 + core
        pl.semaphore_signal(barrier, 1, device_id=(slab, peer), device_id_type=MESH_ID)
    pl.semaphore_wait(barrier, n_chip)


def _scatter_kernel(n_chip, part_ref, half_ref, out_ref, got_pair, got_ring, chip_sum,
                    send_a, recv_a, send_b, recv_b):
    slab, here, chip, core, partner = _where_am_i()
    _greet(slab, chip, core, partner, n_chip)
    pair = []
    for k in range(n_chip):
        copy = pltpu.make_async_remote_copy(
            src_ref=half_ref.at[2 * k + 1 - core],
            dst_ref=got_pair.at[k],
            send_sem=send_a.at[k],
            recv_sem=recv_a.at[k],
            device_id=(slab, partner),
            device_id_type=MESH_ID,
        )
        copy.start()
        pair.append(copy)
    for copy in pair:
        copy.wait()
    for d in range(1, n_chip):
        dest = (chip + d) % n_chip
        chip_sum[dest] = (
            part_ref[2 * dest + core] + got_pair[dest].astype(jnp.float32)
        ).astype(chip_sum.dtype)
    ring = []
    for d in range(1, n_chip):
        dest = (chip + d) % n_chip
        copy = pltpu.make_async_remote_copy(
            src_ref=chip_sum.at[dest],
            dst_ref=got_ring.at[d],
            send_sem=send_b.at[d],
            recv_sem=recv_b.at[d],
            device_id=(slab, 2 * dest + core),
            device_id_type=MESH_ID,
        )
        copy.start()
        ring.append(copy)
    total = part_ref[here] + got_pair[chip].astype(jnp.float32)
    for copy in ring:
        copy.wait()
    for d in range(1, n_chip):
        total = total + got_ring[d].astype(jnp.float32)
    out_ref[...] = total


def scatter_angle(part):
    blocks, rows, cols = part.shape
    n_chip = blocks // 2
    link = part.dtype
    return pl.pallas_call(
        functools.partial(_scatter_kernel, n_chip),
        out_shape=jax.ShapeDtypeStruct((rows, cols), jnp.float32),
        in_specs=[pl.BlockSpec(memory_space=pltpu.VMEM)] * 2,
        out_specs=pl.BlockSpec(memory_space=pltpu.VMEM),
        scratch_shapes=[
            pltpu.VMEM((n_chip, rows, cols), link),
            pltpu.VMEM((n_chip, rows, cols), link),
            pltpu.VMEM((n_chip, rows, cols), link),
            pltpu.SemaphoreType.DMA((n_chip,)),
            pltpu.SemaphoreType.DMA((n_chip,)),
            pltpu.SemaphoreType.DMA((n_chip,)),
            pltpu.SemaphoreType.DMA((n_chip,)),
        ],
        compiler_params=pltpu.CompilerParams(collective_id=0, has_side_effects=True),
        cost_estimate=pl.CostEstimate(
            flops=2 * blocks * rows * cols, bytes_accessed=4 * 3 * blocks * rows * cols,
            transcendentals=0,
        ),
    )(part, part.astype(link))


def _sum_kernel(groups, part_ref, out_ref, got, send_sem, recv_sem):
    slab = lax.axis_index("slab")
    here = lax.axis_index("angle")
    barrier = pltpu.get_barrier_semaphore()
    for d in range(1, groups):
        peer = (here + d) % groups
        pl.semaphore_signal(barrier, 1, device_id=(slab, peer), device_id_type=MESH_ID)
    pl.semaphore_wait(barrier, groups - 1)
    copies = []
    for d in range(1, groups):
        copy = pltpu.make_async_remote_copy(
            src_ref=part_ref,
            dst_ref=got.at[d],
            send_sem=send_sem.at[d],
            recv_sem=recv_sem.at[d],
            device_id=(slab, (here + d) % groups),
            device_id_type=MESH_ID,
        )
        copy.start()
        copies.append(copy)
    total = part_ref[...]
    for copy in copies:
        copy.wait()
    for d in range(1, groups):
        total = total + got[d]
    out_ref[...] = total


def sum_angle(part, groups):
    return pl.pallas_call(
        functools.partial(_sum_kernel, groups),
        out_shape=jax.ShapeDtypeStruct(part.shape, part.dtype),
        in_specs=[pl.BlockSpec(memory_space=pltpu.VMEM)],
        out_specs=pl.BlockSpec(memory_space=pltpu.VMEM),
        scratch_shapes=[
            pltpu.VMEM((groups,) + part.shape, part.dtype),
            pltpu.SemaphoreType.DMA((groups,)),
            pltpu.SemaphoreType.DMA((groups,)),
        ],
        compiler_params=pltpu.CompilerParams(collective_id=2, has_side_effects=True),
        cost_estimate=pl.CostEstimate(
            flops=groups * part.size, bytes_accessed=4 * 2 * groups * part.size,
            transcendentals=0,
        ),
    )(part)


def _gather_kernel(n_chip, own_ref, out_ref, held, send_a, recv_a, send_b, recv_b, local_sem):
    slab, here, chip, core, partner = _where_am_i()
    _greet(slab, chip, core, partner, n_chip)
    mine = pltpu.make_async_copy(own_ref, held.at[here], local_sem.at[0])
    mine.start()
    ring = []
    for d in range(1, n_chip):
        dest = (chip + d) % n_chip
        copy = pltpu.make_async_remote_copy(
            src_ref=own_ref,
            dst_ref=held.at[here],
            send_sem=send_a.at[d],
            recv_sem=recv_a.at[d],
            device_id=(slab, 2 * dest + core),
            device_id_type=MESH_ID,
        )
        copy.start()
        ring.append(copy)
    mine.wait()
    for copy in ring:
        copy.wait()
    pair = []
    for k in range(n_chip):
        copy = pltpu.make_async_remote_copy(
            src_ref=held.at[2 * k + core],
            dst_ref=held.at[2 * k + core],
            send_sem=send_b.at[k],
            recv_sem=recv_b.at[k],
            device_id=(slab, partner),
            device_id_type=MESH_ID,
        )
        copy.start()
        pair.append(copy)
    for copy in pair:
        copy.wait()
    out_ref[...] = held[...]


def gather_angle(own, groups):
    rows, cols = own.shape
    n_chip = groups // 2
    return pl.pallas_call(
        functools.partial(_gather_kernel, n_chip),
        out_shape=jax.ShapeDtypeStruct((groups, rows, cols), own.dtype),
        in_specs=[pl.BlockSpec(memory_space=pltpu.VMEM)],
        out_specs=pl.BlockSpec(memory_space=pltpu.VMEM),
        scratch_shapes=[
            pltpu.VMEM((groups, rows, cols), own.dtype),
            pltpu.SemaphoreType.DMA((n_chip,)),
            pltpu.SemaphoreType.DMA((n_chip,)),
            pltpu.SemaphoreType.DMA((n_chip,)),
            pltpu.SemaphoreType.DMA((n_chip,)),
            pltpu.SemaphoreType.DMA((1,)),
        ],
        compiler_params=pltpu.CompilerParams(collective_id=1, has_side_effects=True),
        cost_estimate=pl.CostEstimate(
            flops=0, bytes_accessed=2 * 2 * groups * rows * cols, transcendentals=0,
        ),
    )(own)


def smooth_share(
    volume,
    weight_z,
    weight_y,
    weight_x,
    lower_rim,
    left_rim,
    z_first,
    z_total,
    x_first,
    x_total,
):
    upper_halo = from_behind(volume[:, 0], "slab", -1)
    lower_halo = from_behind(volume[:, -1], "slab", 1)
    right_halo = from_behind(volume[0], "angle", -1)
    left_halo = from_behind(volume[-1], "angle", 1)
    upper = jnp.concatenate([volume[:, 1:], upper_halo[:, None]], axis=1)
    inside = (z_first + lax.broadcasted_iota(jnp.int32, volume.shape, 1) + 1 < z_total).astype(
        jnp.float32
    )
    face_flux = weight_z * limiter(upper - volume) * inside
    lower_flux = lower_rim * limiter(volume[:, 0] - lower_halo)
    previous = jnp.concatenate([lower_flux[:, None], face_flux[:, :-1]], axis=1)
    change = face_flux - previous
    following = jnp.concatenate([volume[:, :, 1:], jnp.zeros_like(volume[:, :, :1])], axis=2)
    inside = (lax.broadcasted_iota(jnp.int32, volume.shape, 2) < volume.shape[2] - 1).astype(
        jnp.float32
    )
    face_flux = weight_y * limiter(following - volume) * inside
    previous = jnp.concatenate([jnp.zeros_like(face_flux[:, :, :1]), face_flux[:, :, :-1]], axis=2)
    change = change + face_flux - previous
    following = jnp.concatenate([volume[1:], right_halo[None]], axis=0)
    inside = (x_first + lax.broadcasted_iota(jnp.int32, volume.shape, 0) + 1 < x_total).astype(
        jnp.float32
    )
    face_flux = weight_x * limiter(following - volume) * inside
    lower_flux = left_rim * limiter(volume[0] - left_halo)
    previous = jnp.concatenate([lower_flux[None], face_flux[:-1]], axis=0)
    change = change + face_flux - previous
    return volume + SMOOTH_RATE * change


def shards(volume0, weights, tile_block, tile_count, owner, sino, weight_z, weight_y, weight_x):
    tiles = weights[0, 0]
    slot_count, ray_count, voxels = tiles.shape
    slab_depth, height, column_count = volume0.shape
    blocks = tile_block[0, 0]
    live_count = tile_count[0, 0]
    owner_row = owner[0]
    live_slots = jnp.arange(slot_count, dtype=jnp.int32) < live_count
    select = (owner_row[None, :] == blocks[:, None]) & live_slots[:, None]
    slab_pos = lax.axis_index("slab")
    holder_ids = jnp.arange(owner_row.shape[0], dtype=jnp.int32)
    target = jnp.sum(jnp.where(select, holder_ids[None, :], 0), axis=1)
    distance_ids = jnp.arange(slot_count, dtype=jnp.int32)
    relative = ((target - slab_pos)[:, None] == distance_ids[None, :]) & live_slots[:, None]
    relative_float = relative.astype(jnp.float32)
    relative_half = relative.astype(jnp.bfloat16)
    flat_tiles = tiles.reshape(slot_count * ray_count, voxels)
    ray_local = jnp.dot(
        flat_tiles, jnp.ones((voxels,), jnp.bfloat16), preferred_element_type=jnp.float32
    )
    ray_sends = jnp.einsum("td,tr->dr", relative_float, ray_local.reshape(slot_count, ray_count))
    ray_total = ray_sends[0]
    for distance in range(1, slot_count):
        ray_total = ray_total + from_behind(ray_sends[distance], "slab", distance)
    live_rows = jnp.repeat(live_slots, ray_count).astype(jnp.bfloat16)
    voxel_local = jnp.dot(live_rows, flat_tiles, preferred_element_type=jnp.float32)
    voxel_total = sum_angle(voxel_local.reshape(slab_depth, height), lax.axis_size("angle"))
    ray_scale = 1.0 / ray_total
    voxel_scale = (1.0 / voxel_total).reshape(1, slab_depth, height)
    lower_all = from_behind(weight_z[slab_depth - 1], "slab", 1)
    z_first = slab_pos * slab_depth
    z_total = slab_depth * lax.axis_size("slab")
    groups = lax.axis_size("angle")
    share_width = column_count // groups
    angle_pos = lax.axis_index("angle")
    share_first = angle_pos * share_width

    def share_of(array):
        part = lax.dynamic_slice_in_dim(array, share_first, share_width, array.ndim - 1)
        return jnp.moveaxis(part, -1, 0).astype(jnp.float32)

    measured = sino[0, 0].astype(jnp.float32)
    volume = share_of(volume0)
    local_z = share_of(weight_z)
    local_y = share_of(weight_y)
    local_x = share_of(weight_x)
    lower_rim = share_of(lower_all)
    left_index = jnp.maximum(share_first - 1, 0)
    left_rim = lax.dynamic_index_in_dim(weight_x, left_index, 2, keepdims=False).astype(
        jnp.float32
    ) * (angle_pos > 0).astype(jnp.float32)
    gathered = None
    residual = jnp.zeros((ray_count, column_count), jnp.float32)
    for iteration in range(ITERS):
        if gathered is None:
            flat_volume = volume0.astype(jnp.bfloat16).reshape(voxels, column_count)
            products = jnp.einsum(
                "trv,vn->trn", tiles, flat_volume, preferred_element_type=jnp.float32
            ).astype(jnp.bfloat16)
        else:
            products = jnp.einsum(
                "trv,nv->trn", tiles, gathered, preferred_element_type=jnp.float32
            ).astype(jnp.bfloat16)
        sends = jnp.einsum(
            "td,trn->drn", relative_half, products, preferred_element_type=jnp.float32
        )
        sends_half = sends.astype(jnp.bfloat16)
        projected = sends[0]
        for distance in range(1, slot_count):
            arrived = from_behind(sends_half[distance], "slab", distance)
            projected = projected + arrived.astype(jnp.float32)
        residual = (measured - projected) * ray_scale[:, None]
        residual_half = residual.astype(jnp.bfloat16)
        nearby = [residual_half] + [
            from_behind(residual_half, "slab", -distance) for distance in range(1, slot_count)
        ]
        picked = jnp.einsum(
            "td,drn->trn", relative_half, jnp.stack(nearby), preferred_element_type=jnp.float32
        ).astype(jnp.bfloat16)
        back_t = jnp.einsum("trn,trv->nv", picked, tiles, preferred_element_type=jnp.float32)
        back_own = scatter_angle(back_t.reshape(groups, share_width, voxels))
        volume = volume + voxel_scale * back_own.reshape(share_width, slab_depth, height)
        volume = smooth_share(
            volume,
            local_z,
            local_y,
            local_x,
            lower_rim,
            left_rim,
            z_first,
            z_total,
            share_first,
            column_count,
        )
        if iteration + 1 < ITERS:
            own_half = volume.astype(jnp.bfloat16).reshape(share_width, voxels)
            gathered = gather_angle(own_half, groups).reshape(column_count, voxels)
    volume_out = jnp.moveaxis(volume, 0, -1)
    return (volume_out, residual[None, None])


def solution(mesh):
    in_specs = (
        P("slab", None, None),
        P("slab", "angle", None, None, None),
        P("slab", "angle", None),
        P("slab", "angle"),
        P("angle", None),
        P("angle", "slab", None, None),
        P("slab", None, None),
        P("slab", None, None),
        P("slab", None, None),
    )
    out_specs = (P("slab", None, "angle"), P("angle", "slab", None, None))
    return jax.shard_map(shards, mesh=mesh, in_specs=in_specs, out_specs=out_specs, check_vma=False)
```

```python
import functools

import jax
import jax.numpy as jnp
from jax import lax
from jax.experimental import pallas as pl
from jax.experimental.pallas import tpu as pltpu
from jax.sharding import PartitionSpec as P

ITERS = 3


SMOOTH_EPS = 0.01
SMOOTH_RATE = 0.15

MESH_ID = pl.DeviceIdType.MESH


def from_behind(value, axis, steps):
    count = lax.axis_size(axis)
    first, last = (max(0, -steps), min(count, count - steps))
    return lax.ppermute(value, axis, [(source, source + steps) for source in range(first, last)])


def limiter(difference):
    return difference / jnp.sqrt(difference * difference + SMOOTH_EPS)


def _where_am_i():
    slab = lax.axis_index("slab")
    here = lax.axis_index("angle")
    chip = here // 2
    core = here % 2
    partner = here + 1 - 2 * core
    return slab, here, chip, core, partner


def _greet(slab, chip, core, partner, n_chip):
    barrier = pltpu.get_barrier_semaphore()
    pl.semaphore_signal(barrier, 1, device_id=(slab, partner), device_id_type=MESH_ID)
    for d in range(1, n_chip):
        peer = ((chip + d) % n_chip) * 2 + core
        pl.semaphore_signal(barrier, 1, device_id=(slab, peer), device_id_type=MESH_ID)
    pl.semaphore_wait(barrier, n_chip)


def _scatter_kernel(n_chip, part_ref, half_ref, out_ref, got_pair, got_ring, chip_sum,
                    send_a, recv_a, send_b, recv_b):
    slab, here, chip, core, partner = _where_am_i()
    _greet(slab, chip, core, partner, n_chip)
    pair = []
    for k in range(n_chip):
        copy = pltpu.make_async_remote_copy(
            src_ref=half_ref.at[2 * k + 1 - core],
            dst_ref=got_pair.at[k],
            send_sem=send_a.at[k],
            recv_sem=recv_a.at[k],
            device_id=(slab, partner),
            device_id_type=MESH_ID,
        )
        copy.start()
        pair.append(copy)
    for copy in pair:
        copy.wait()
    for d in range(1, n_chip):
        dest = (chip + d) % n_chip
        chip_sum[dest] = (
            part_ref[2 * dest + core] + got_pair[dest].astype(jnp.float32)
        ).astype(chip_sum.dtype)
    ring = []
    for d in range(1, n_chip):
        dest = (chip + d) % n_chip
        copy = pltpu.make_async_remote_copy(
            src_ref=chip_sum.at[dest],
            dst_ref=got_ring.at[d],
            send_sem=send_b.at[d],
            recv_sem=recv_b.at[d],
            device_id=(slab, 2 * dest + core),
            device_id_type=MESH_ID,
        )
        copy.start()
        ring.append(copy)
    total = part_ref[here] + got_pair[chip].astype(jnp.float32)
    for copy in ring:
        copy.wait()
    for d in range(1, n_chip):
        total = total + got_ring[d].astype(jnp.float32)
    out_ref[...] = total


def scatter_angle(part):
    blocks, rows, cols = part.shape
    n_chip = blocks // 2
    link = part.dtype
    return pl.pallas_call(
        functools.partial(_scatter_kernel, n_chip),
        out_shape=jax.ShapeDtypeStruct((rows, cols), jnp.float32),
        in_specs=[pl.BlockSpec(memory_space=pltpu.VMEM)] * 2,
        out_specs=pl.BlockSpec(memory_space=pltpu.VMEM),
        scratch_shapes=[
            pltpu.VMEM((n_chip, rows, cols), link),
            pltpu.VMEM((n_chip, rows, cols), link),
            pltpu.VMEM((n_chip, rows, cols), link),
            pltpu.SemaphoreType.DMA((n_chip,)),
            pltpu.SemaphoreType.DMA((n_chip,)),
            pltpu.SemaphoreType.DMA((n_chip,)),
            pltpu.SemaphoreType.DMA((n_chip,)),
        ],
        compiler_params=pltpu.CompilerParams(collective_id=0, has_side_effects=True),
        cost_estimate=pl.CostEstimate(
            flops=2 * blocks * rows * cols, bytes_accessed=4 * 3 * blocks * rows * cols,
            transcendentals=0,
        ),
    )(part, part.astype(link))


def _sum_kernel(groups, part_ref, out_ref, got, send_sem, recv_sem):
    slab = lax.axis_index("slab")
    here = lax.axis_index("angle")
    barrier = pltpu.get_barrier_semaphore()
    for d in range(1, groups):
        peer = (here + d) % groups
        pl.semaphore_signal(barrier, 1, device_id=(slab, peer), device_id_type=MESH_ID)
    pl.semaphore_wait(barrier, groups - 1)
    copies = []
    for d in range(1, groups):
        copy = pltpu.make_async_remote_copy(
            src_ref=part_ref,
            dst_ref=got.at[d],
            send_sem=send_sem.at[d],
            recv_sem=recv_sem.at[d],
            device_id=(slab, (here + d) % groups),
            device_id_type=MESH_ID,
        )
        copy.start()
        copies.append(copy)
    total = part_ref[...]
    for copy in copies:
        copy.wait()
    for d in range(1, groups):
        total = total + got[d]
    out_ref[...] = total


def sum_angle(part, groups):
    return pl.pallas_call(
        functools.partial(_sum_kernel, groups),
        out_shape=jax.ShapeDtypeStruct(part.shape, part.dtype),
        in_specs=[pl.BlockSpec(memory_space=pltpu.VMEM)],
        out_specs=pl.BlockSpec(memory_space=pltpu.VMEM),
        scratch_shapes=[
            pltpu.VMEM((groups,) + part.shape, part.dtype),
            pltpu.SemaphoreType.DMA((groups,)),
            pltpu.SemaphoreType.DMA((groups,)),
        ],
        compiler_params=pltpu.CompilerParams(collective_id=2, has_side_effects=True),
        cost_estimate=pl.CostEstimate(
            flops=groups * part.size, bytes_accessed=4 * 2 * groups * part.size,
            transcendentals=0,
        ),
    )(part)


def _slab_kernel(shifts, send_ref, out_ref, got, send_sem, recv_sem):
    slab = lax.axis_index("slab")
    here = lax.axis_index("angle")
    count = lax.axis_size("slab")
    barrier = pltpu.get_barrier_semaphore()
    for shift in shifts:
        sender = (slab - shift + count) % count
        pl.semaphore_signal(barrier, 1, device_id=(sender, here), device_id_type=MESH_ID)
    pl.semaphore_wait(barrier, len(shifts))
    copies = []
    for i, shift in enumerate(shifts):
        copy = pltpu.make_async_remote_copy(
            src_ref=send_ref.at[i if send_ref.shape[0] > 1 else 0],
            dst_ref=got.at[i],
            send_sem=send_sem.at[i],
            recv_sem=recv_sem.at[i],
            device_id=((slab + shift + count) % count, here),
            device_id_type=MESH_ID,
        )
        copy.start()
        copies.append(copy)
    for copy in copies:
        copy.wait()
    out_ref[...] = got[...]


def exchange_slab(send, shifts, collective_id):
    rows, cols = send.shape[1:]
    moves = len(shifts)
    return pl.pallas_call(
        functools.partial(_slab_kernel, shifts),
        out_shape=jax.ShapeDtypeStruct((moves, rows, cols), send.dtype),
        in_specs=[pl.BlockSpec(memory_space=pltpu.VMEM)],
        out_specs=pl.BlockSpec(memory_space=pltpu.VMEM),
        scratch_shapes=[
            pltpu.VMEM((moves, rows, cols), send.dtype),
            pltpu.SemaphoreType.DMA((moves,)),
            pltpu.SemaphoreType.DMA((moves,)),
        ],
        compiler_params=pltpu.CompilerParams(collective_id=collective_id, has_side_effects=True),
        cost_estimate=pl.CostEstimate(
            flops=0, bytes_accessed=4 * moves * rows * cols * send.dtype.itemsize,
            transcendentals=0,
        ),
    )(send)


def _gather_kernel(n_chip, own_ref, out_ref, held, send_a, recv_a, send_b, recv_b, local_sem):
    slab, here, chip, core, partner = _where_am_i()
    _greet(slab, chip, core, partner, n_chip)
    mine = pltpu.make_async_copy(own_ref, held.at[here], local_sem.at[0])
    mine.start()
    ring = []
    for d in range(1, n_chip):
        dest = (chip + d) % n_chip
        copy = pltpu.make_async_remote_copy(
            src_ref=own_ref,
            dst_ref=held.at[here],
            send_sem=send_a.at[d],
            recv_sem=recv_a.at[d],
            device_id=(slab, 2 * dest + core),
            device_id_type=MESH_ID,
        )
        copy.start()
        ring.append(copy)
    mine.wait()
    for copy in ring:
        copy.wait()
    pair = []
    for k in range(n_chip):
        copy = pltpu.make_async_remote_copy(
            src_ref=held.at[2 * k + core],
            dst_ref=held.at[2 * k + core],
            send_sem=send_b.at[k],
            recv_sem=recv_b.at[k],
            device_id=(slab, partner),
            device_id_type=MESH_ID,
        )
        copy.start()
        pair.append(copy)
    for copy in pair:
        copy.wait()
    out_ref[...] = held[...]


def gather_angle(own, groups):
    rows, cols = own.shape
    n_chip = groups // 2
    return pl.pallas_call(
        functools.partial(_gather_kernel, n_chip),
        out_shape=jax.ShapeDtypeStruct((groups, rows, cols), own.dtype),
        in_specs=[pl.BlockSpec(memory_space=pltpu.VMEM)],
        out_specs=pl.BlockSpec(memory_space=pltpu.VMEM),
        scratch_shapes=[
            pltpu.VMEM((groups, rows, cols), own.dtype),
            pltpu.SemaphoreType.DMA((n_chip,)),
            pltpu.SemaphoreType.DMA((n_chip,)),
            pltpu.SemaphoreType.DMA((n_chip,)),
            pltpu.SemaphoreType.DMA((n_chip,)),
            pltpu.SemaphoreType.DMA((1,)),
        ],
        compiler_params=pltpu.CompilerParams(collective_id=1, has_side_effects=True),
        cost_estimate=pl.CostEstimate(
            flops=0, bytes_accessed=2 * 2 * groups * rows * cols, transcendentals=0,
        ),
    )(own)


def smooth_share(
    volume,
    weight_z,
    weight_y,
    weight_x,
    lower_rim,
    left_rim,
    z_first,
    z_total,
    x_first,
    x_total,
):
    upper_halo = from_behind(volume[:, 0], "slab", -1)
    lower_halo = from_behind(volume[:, -1], "slab", 1)
    right_halo = from_behind(volume[0], "angle", -1)
    left_halo = from_behind(volume[-1], "angle", 1)
    upper = jnp.concatenate([volume[:, 1:], upper_halo[:, None]], axis=1)
    inside = (z_first + lax.broadcasted_iota(jnp.int32, volume.shape, 1) + 1 < z_total).astype(
        jnp.float32
    )
    face_flux = weight_z * limiter(upper - volume) * inside
    lower_flux = lower_rim * limiter(volume[:, 0] - lower_halo)
    previous = jnp.concatenate([lower_flux[:, None], face_flux[:, :-1]], axis=1)
    change = face_flux - previous
    following = jnp.concatenate([volume[:, :, 1:], jnp.zeros_like(volume[:, :, :1])], axis=2)
    inside = (lax.broadcasted_iota(jnp.int32, volume.shape, 2) < volume.shape[2] - 1).astype(
        jnp.float32
    )
    face_flux = weight_y * limiter(following - volume) * inside
    previous = jnp.concatenate([jnp.zeros_like(face_flux[:, :, :1]), face_flux[:, :, :-1]], axis=2)
    change = change + face_flux - previous
    following = jnp.concatenate([volume[1:], right_halo[None]], axis=0)
    inside = (x_first + lax.broadcasted_iota(jnp.int32, volume.shape, 0) + 1 < x_total).astype(
        jnp.float32
    )
    face_flux = weight_x * limiter(following - volume) * inside
    lower_flux = left_rim * limiter(volume[0] - left_halo)
    previous = jnp.concatenate([lower_flux[None], face_flux[:-1]], axis=0)
    change = change + face_flux - previous
    return volume + SMOOTH_RATE * change


def shards(volume0, weights, tile_block, tile_count, owner, sino, weight_z, weight_y, weight_x):
    tiles = weights[0, 0]
    slot_count, ray_count, voxels = tiles.shape
    slab_depth, height, column_count = volume0.shape
    blocks = tile_block[0, 0]
    live_count = tile_count[0, 0]
    owner_row = owner[0]
    live_slots = jnp.arange(slot_count, dtype=jnp.int32) < live_count
    select = (owner_row[None, :] == blocks[:, None]) & live_slots[:, None]
    slab_pos = lax.axis_index("slab")
    holder_ids = jnp.arange(owner_row.shape[0], dtype=jnp.int32)
    target = jnp.sum(jnp.where(select, holder_ids[None, :], 0), axis=1)
    distance_ids = jnp.arange(slot_count, dtype=jnp.int32)
    relative = ((target - slab_pos)[:, None] == distance_ids[None, :]) & live_slots[:, None]
    relative_float = relative.astype(jnp.float32)
    relative_half = relative.astype(jnp.bfloat16)
    flat_tiles = tiles.reshape(slot_count * ray_count, voxels)
    ray_local = jnp.dot(
        flat_tiles, jnp.ones((voxels,), jnp.bfloat16), preferred_element_type=jnp.float32
    )
    ray_sends = jnp.einsum("td,tr->dr", relative_float, ray_local.reshape(slot_count, ray_count))
    ray_total = ray_sends[0]
    for distance in range(1, slot_count):
        ray_total = ray_total + from_behind(ray_sends[distance], "slab", distance)
    live_rows = jnp.repeat(live_slots, ray_count).astype(jnp.bfloat16)
    voxel_local = jnp.dot(live_rows, flat_tiles, preferred_element_type=jnp.float32)
    voxel_total = sum_angle(voxel_local.reshape(slab_depth, height), lax.axis_size("angle"))
    ray_scale = 1.0 / ray_total
    voxel_scale = (1.0 / voxel_total).reshape(1, slab_depth, height)
    lower_all = from_behind(weight_z[slab_depth - 1], "slab", 1)
    z_first = slab_pos * slab_depth
    z_total = slab_depth * lax.axis_size("slab")
    groups = lax.axis_size("angle")
    share_width = column_count // groups
    angle_pos = lax.axis_index("angle")
    share_first = angle_pos * share_width

    def share_of(array):
        part = lax.dynamic_slice_in_dim(array, share_first, share_width, array.ndim - 1)
        return jnp.moveaxis(part, -1, 0).astype(jnp.float32)

    measured = sino[0, 0].astype(jnp.float32)
    volume = share_of(volume0)
    local_z = share_of(weight_z)
    local_y = share_of(weight_y)
    local_x = share_of(weight_x)
    lower_rim = share_of(lower_all)
    left_index = jnp.maximum(share_first - 1, 0)
    left_rim = lax.dynamic_index_in_dim(weight_x, left_index, 2, keepdims=False).astype(
        jnp.float32
    ) * (angle_pos > 0).astype(jnp.float32)
    gathered = None
    residual = jnp.zeros((ray_count, column_count), jnp.float32)
    for iteration in range(ITERS):
        if gathered is None:
            flat_volume = volume0.astype(jnp.bfloat16).reshape(voxels, column_count)
            products = jnp.einsum(
                "trv,vn->trn", tiles, flat_volume, preferred_element_type=jnp.float32
            ).astype(jnp.bfloat16)
        else:
            products = jnp.einsum(
                "trv,nv->trn", tiles, gathered, preferred_element_type=jnp.float32
            ).astype(jnp.bfloat16)
        sends = jnp.einsum(
            "td,trn->drn", relative_half, products, preferred_element_type=jnp.float32
        )
        sends_half = sends.astype(jnp.bfloat16)
        shifts = tuple(range(1, slot_count))
        arrived = exchange_slab(sends_half[1:], shifts, 3)
        projected = sends[0]
        for distance in range(1, slot_count):
            projected = projected + arrived[distance - 1].astype(jnp.float32)
        residual = (measured - projected) * ray_scale[:, None]
        residual_half = residual.astype(jnp.bfloat16)
        returned = exchange_slab(residual_half[None], tuple(-s for s in shifts), 4)
        nearby = jnp.concatenate([residual_half[None], returned], axis=0)
        picked = jnp.einsum(
            "td,drn->trn", relative_half, nearby, preferred_element_type=jnp.float32
        ).astype(jnp.bfloat16)
        back_t = jnp.einsum("trn,trv->nv", picked, tiles, preferred_element_type=jnp.float32)
        back_own = scatter_angle(back_t.reshape(groups, share_width, voxels))
        volume = volume + voxel_scale * back_own.reshape(share_width, slab_depth, height)
        volume = smooth_share(
            volume,
            local_z,
            local_y,
            local_x,
            lower_rim,
            left_rim,
            z_first,
            z_total,
            share_first,
            column_count,
        )
        if iteration + 1 < ITERS:
            own_half = volume.astype(jnp.bfloat16).reshape(share_width, voxels)
            gathered = gather_angle(own_half, groups).reshape(column_count, voxels)
    volume_out = jnp.moveaxis(volume, 0, -1)
    return (volume_out, residual[None, None])


def solution(mesh):
    in_specs = (
        P("slab", None, None),
        P("slab", "angle", None, None, None),
        P("slab", "angle", None),
        P("slab", "angle"),
        P("angle", None),
        P("angle", "slab", None, None),
        P("slab", None, None),
        P("slab", None, None),
        P("slab", None, None),
    )
    out_specs = (P("slab", None, "angle"), P("angle", "slab", None, None))
    return jax.shard_map(shards, mesh=mesh, in_specs=in_specs, out_specs=out_specs, check_vma=False)
```

```python
import functools

import jax
import jax.numpy as jnp
from jax import lax
from jax.experimental import pallas as pl
from jax.experimental.pallas import tpu as pltpu
from jax.sharding import PartitionSpec as P

ITERS = 3


SMOOTH_EPS = 0.01
SMOOTH_RATE = 0.15

MESH_ID = pl.DeviceIdType.MESH


def from_behind(value, axis, steps):
    count = lax.axis_size(axis)
    first, last = (max(0, -steps), min(count, count - steps))
    return lax.ppermute(value, axis, [(source, source + steps) for source in range(first, last)])


def limiter(difference):
    return difference / jnp.sqrt(difference * difference + SMOOTH_EPS)


def _where_am_i():
    slab = lax.axis_index("slab")
    here = lax.axis_index("angle")
    chip = here // 2
    core = here % 2
    partner = here + 1 - 2 * core
    return slab, here, chip, core, partner


def _greet(slab, chip, core, partner, n_chip):
    barrier = pltpu.get_barrier_semaphore()
    pl.semaphore_signal(barrier, 1, device_id=(slab, partner), device_id_type=MESH_ID)
    for d in range(1, n_chip):
        peer = ((chip + d) % n_chip) * 2 + core
        pl.semaphore_signal(barrier, 1, device_id=(slab, peer), device_id_type=MESH_ID)
    pl.semaphore_wait(barrier, n_chip)


def _scatter_kernel(n_chip, part_ref, half_ref, out_ref, got_pair, got_ring, chip_sum,
                    send_a, recv_a, send_b, recv_b):
    slab, here, chip, core, partner = _where_am_i()
    _greet(slab, chip, core, partner, n_chip)
    pair = []
    for k in range(n_chip):
        copy = pltpu.make_async_remote_copy(
            src_ref=half_ref.at[2 * k + 1 - core],
            dst_ref=got_pair.at[k],
            send_sem=send_a.at[k],
            recv_sem=recv_a.at[k],
            device_id=(slab, partner),
            device_id_type=MESH_ID,
        )
        copy.start()
        pair.append(copy)
    for copy in pair:
        copy.wait()
    for d in range(1, n_chip):
        dest = (chip + d) % n_chip
        chip_sum[dest] = (
            part_ref[2 * dest + core] + got_pair[dest].astype(jnp.float32)
        ).astype(chip_sum.dtype)
    ring = []
    for d in range(1, n_chip):
        dest = (chip + d) % n_chip
        copy = pltpu.make_async_remote_copy(
            src_ref=chip_sum.at[dest],
            dst_ref=got_ring.at[d],
            send_sem=send_b.at[d],
            recv_sem=recv_b.at[d],
            device_id=(slab, 2 * dest + core),
            device_id_type=MESH_ID,
        )
        copy.start()
        ring.append(copy)
    total = part_ref[here] + got_pair[chip].astype(jnp.float32)
    for copy in ring:
        copy.wait()
    for d in range(1, n_chip):
        total = total + got_ring[d].astype(jnp.float32)
    out_ref[...] = total


def scatter_angle(part):
    blocks, rows, cols = part.shape
    n_chip = blocks // 2
    link = part.dtype
    return pl.pallas_call(
        functools.partial(_scatter_kernel, n_chip),
        out_shape=jax.ShapeDtypeStruct((rows, cols), jnp.float32),
        in_specs=[pl.BlockSpec(memory_space=pltpu.VMEM)] * 2,
        out_specs=pl.BlockSpec(memory_space=pltpu.VMEM),
        scratch_shapes=[
            pltpu.VMEM((n_chip, rows, cols), link),
            pltpu.VMEM((n_chip, rows, cols), link),
            pltpu.VMEM((n_chip, rows, cols), link),
            pltpu.SemaphoreType.DMA((n_chip,)),
            pltpu.SemaphoreType.DMA((n_chip,)),
            pltpu.SemaphoreType.DMA((n_chip,)),
            pltpu.SemaphoreType.DMA((n_chip,)),
        ],
        compiler_params=pltpu.CompilerParams(collective_id=0, has_side_effects=True),
        cost_estimate=pl.CostEstimate(
            flops=2 * blocks * rows * cols, bytes_accessed=4 * 3 * blocks * rows * cols,
            transcendentals=0,
        ),
    )(part, part.astype(link))


def _sum_kernel(groups, part_ref, out_ref, got, send_sem, recv_sem):
    slab = lax.axis_index("slab")
    here = lax.axis_index("angle")
    barrier = pltpu.get_barrier_semaphore()
    for d in range(1, groups):
        peer = (here + d) % groups
        pl.semaphore_signal(barrier, 1, device_id=(slab, peer), device_id_type=MESH_ID)
    pl.semaphore_wait(barrier, groups - 1)
    copies = []
    for d in range(1, groups):
        copy = pltpu.make_async_remote_copy(
            src_ref=part_ref,
            dst_ref=got.at[d],
            send_sem=send_sem.at[d],
            recv_sem=recv_sem.at[d],
            device_id=(slab, (here + d) % groups),
            device_id_type=MESH_ID,
        )
        copy.start()
        copies.append(copy)
    total = part_ref[...]
    for copy in copies:
        copy.wait()
    for d in range(1, groups):
        total = total + got[d]
    out_ref[...] = total


def sum_angle(part, groups):
    return pl.pallas_call(
        functools.partial(_sum_kernel, groups),
        out_shape=jax.ShapeDtypeStruct(part.shape, part.dtype),
        in_specs=[pl.BlockSpec(memory_space=pltpu.VMEM)],
        out_specs=pl.BlockSpec(memory_space=pltpu.VMEM),
        scratch_shapes=[
            pltpu.VMEM((groups,) + part.shape, part.dtype),
            pltpu.SemaphoreType.DMA((groups,)),
            pltpu.SemaphoreType.DMA((groups,)),
        ],
        compiler_params=pltpu.CompilerParams(collective_id=2, has_side_effects=True),
        cost_estimate=pl.CostEstimate(
            flops=groups * part.size, bytes_accessed=4 * 2 * groups * part.size,
            transcendentals=0,
        ),
    )(part)


def _gather_kernel(n_chip, own_ref, out_ref, held, send_a, recv_a, send_b, recv_b, local_sem):
    slab, here, chip, core, partner = _where_am_i()
    _greet(slab, chip, core, partner, n_chip)
    mine = pltpu.make_async_copy(own_ref, held.at[here], local_sem.at[0])
    mine.start()
    ring = []
    for d in range(1, n_chip):
        dest = (chip + d) % n_chip
        copy = pltpu.make_async_remote_copy(
            src_ref=own_ref,
            dst_ref=held.at[here],
            send_sem=send_a.at[d],
            recv_sem=recv_a.at[d],
            device_id=(slab, 2 * dest + core),
            device_id_type=MESH_ID,
        )
        copy.start()
        ring.append(copy)
    mine.wait()
    for copy in ring:
        copy.wait()
    pair = []
    for k in range(n_chip):
        copy = pltpu.make_async_remote_copy(
            src_ref=held.at[2 * k + core],
            dst_ref=held.at[2 * k + core],
            send_sem=send_b.at[k],
            recv_sem=recv_b.at[k],
            device_id=(slab, partner),
            device_id_type=MESH_ID,
        )
        copy.start()
        pair.append(copy)
    for copy in pair:
        copy.wait()
    out_ref[...] = held[...]


def gather_angle(own, groups):
    rows, cols = own.shape
    n_chip = groups // 2
    return pl.pallas_call(
        functools.partial(_gather_kernel, n_chip),
        out_shape=jax.ShapeDtypeStruct((groups, rows, cols), own.dtype),
        in_specs=[pl.BlockSpec(memory_space=pltpu.VMEM)],
        out_specs=pl.BlockSpec(memory_space=pltpu.VMEM),
        scratch_shapes=[
            pltpu.VMEM((groups, rows, cols), own.dtype),
            pltpu.SemaphoreType.DMA((n_chip,)),
            pltpu.SemaphoreType.DMA((n_chip,)),
            pltpu.SemaphoreType.DMA((n_chip,)),
            pltpu.SemaphoreType.DMA((n_chip,)),
            pltpu.SemaphoreType.DMA((1,)),
        ],
        compiler_params=pltpu.CompilerParams(collective_id=1, has_side_effects=True),
        cost_estimate=pl.CostEstimate(
            flops=0, bytes_accessed=2 * 2 * groups * rows * cols, transcendentals=0,
        ),
    )(own)


def smooth_share(
    volume,
    weight_z,
    weight_y,
    weight_x,
    lower_rim,
    left_rim,
    z_first,
    z_total,
    x_first,
    x_total,
):
    upper_halo = from_behind(volume[:, 0], "slab", -1)
    lower_halo = from_behind(volume[:, -1], "slab", 1)
    right_halo = from_behind(volume[0], "angle", -1)
    left_halo = from_behind(volume[-1], "angle", 1)
    upper = jnp.concatenate([volume[:, 1:], upper_halo[:, None]], axis=1)
    inside = (z_first + lax.broadcasted_iota(jnp.int32, volume.shape, 1) + 1 < z_total).astype(
        jnp.float32
    )
    face_flux = weight_z * limiter(upper - volume) * inside
    lower_flux = lower_rim * limiter(volume[:, 0] - lower_halo)
    previous = jnp.concatenate([lower_flux[:, None], face_flux[:, :-1]], axis=1)
    change = face_flux - previous
    following = jnp.concatenate([volume[:, :, 1:], jnp.zeros_like(volume[:, :, :1])], axis=2)
    inside = (lax.broadcasted_iota(jnp.int32, volume.shape, 2) < volume.shape[2] - 1).astype(
        jnp.float32
    )
    face_flux = weight_y * limiter(following - volume) * inside
    previous = jnp.concatenate([jnp.zeros_like(face_flux[:, :, :1]), face_flux[:, :, :-1]], axis=2)
    change = change + face_flux - previous
    following = jnp.concatenate([volume[1:], right_halo[None]], axis=0)
    inside = (x_first + lax.broadcasted_iota(jnp.int32, volume.shape, 0) + 1 < x_total).astype(
        jnp.float32
    )
    face_flux = weight_x * limiter(following - volume) * inside
    lower_flux = left_rim * limiter(volume[0] - left_halo)
    previous = jnp.concatenate([lower_flux[None], face_flux[:-1]], axis=0)
    change = change + face_flux - previous
    return volume + SMOOTH_RATE * change


def shards(volume0, weights, tile_block, tile_count, owner, sino, weight_z, weight_y, weight_x):
    tiles = weights[0, 0]
    slot_count, ray_count, voxels = tiles.shape
    slab_depth, height, column_count = volume0.shape
    blocks = tile_block[0, 0]
    live_count = tile_count[0, 0]
    owner_row = owner[0]
    live_slots = jnp.arange(slot_count, dtype=jnp.int32) < live_count
    select = (owner_row[None, :] == blocks[:, None]) & live_slots[:, None]
    slab_pos = lax.axis_index("slab")
    holder_ids = jnp.arange(owner_row.shape[0], dtype=jnp.int32)
    target = jnp.sum(jnp.where(select, holder_ids[None, :], 0), axis=1)
    distance_ids = jnp.arange(slot_count, dtype=jnp.int32)
    relative = ((target - slab_pos)[:, None] == distance_ids[None, :]) & live_slots[:, None]
    relative_float = relative.astype(jnp.float32)
    relative_half = relative.astype(jnp.bfloat16)
    first_volume = jnp.concatenate(
        [
            volume0.astype(jnp.bfloat16).reshape(voxels, column_count),
            jnp.ones((voxels, 1), jnp.bfloat16),
        ],
        axis=1,
    )
    first_products = jnp.einsum(
        "trv,vn->trn", tiles, first_volume, preferred_element_type=jnp.float32
    )
    ray_local = first_products[:, :, column_count]
    ray_sends = jnp.einsum("td,tr->dr", relative_float, ray_local)
    ray_total = ray_sends[0]
    for distance in range(1, slot_count):
        ray_total = ray_total + from_behind(ray_sends[distance], "slab", distance)
    ray_scale = 1.0 / ray_total
    live_column = jnp.broadcast_to(
        live_slots.astype(jnp.bfloat16)[:, None, None], (slot_count, ray_count, 1)
    )
    lower_all = from_behind(weight_z[slab_depth - 1], "slab", 1)
    z_first = slab_pos * slab_depth
    z_total = slab_depth * lax.axis_size("slab")
    groups = lax.axis_size("angle")
    share_width = column_count // groups
    angle_pos = lax.axis_index("angle")
    share_first = angle_pos * share_width

    def share_of(array):
        part = lax.dynamic_slice_in_dim(array, share_first, share_width, array.ndim - 1)
        return jnp.moveaxis(part, -1, 0).astype(jnp.float32)

    measured = sino[0, 0].astype(jnp.float32)
    volume = share_of(volume0)
    local_z = share_of(weight_z)
    local_y = share_of(weight_y)
    local_x = share_of(weight_x)
    lower_rim = share_of(lower_all)
    left_index = jnp.maximum(share_first - 1, 0)
    left_rim = lax.dynamic_index_in_dim(weight_x, left_index, 2, keepdims=False).astype(
        jnp.float32
    ) * (angle_pos > 0).astype(jnp.float32)
    gathered = None
    residual = jnp.zeros((ray_count, column_count), jnp.float32)
    for iteration in range(ITERS):
        if gathered is None:
            products = first_products[:, :, :column_count].astype(jnp.bfloat16)
        else:
            products = jnp.einsum(
                "trv,nv->trn", tiles, gathered, preferred_element_type=jnp.float32
            ).astype(jnp.bfloat16)
        sends = jnp.einsum(
            "td,trn->drn", relative_half, products, preferred_element_type=jnp.float32
        )
        sends_half = sends.astype(jnp.bfloat16)
        projected = sends[0]
        for distance in range(1, slot_count):
            arrived = from_behind(sends_half[distance], "slab", distance)
            projected = projected + arrived.astype(jnp.float32)
        residual = (measured - projected) * ray_scale[:, None]
        residual_half = residual.astype(jnp.bfloat16)
        nearby = [residual_half] + [
            from_behind(residual_half, "slab", -distance) for distance in range(1, slot_count)
        ]
        picked = jnp.einsum(
            "td,drn->trn", relative_half, jnp.stack(nearby), preferred_element_type=jnp.float32
        ).astype(jnp.bfloat16)
        if iteration == 0:
            picked_ext = jnp.concatenate([picked, live_column], axis=2)
            back_ext = jnp.einsum(
                "trn,trv->nv", picked_ext, tiles, preferred_element_type=jnp.float32
            )
            back_t = back_ext[:column_count]
            voxel_local = back_ext[column_count]
            voxel_total = sum_angle(voxel_local.reshape(slab_depth, height), groups)
            voxel_scale = (1.0 / voxel_total).reshape(1, slab_depth, height)
        else:
            back_t = jnp.einsum(
                "trn,trv->nv", picked, tiles, preferred_element_type=jnp.float32
            )
        back_own = scatter_angle(back_t.reshape(groups, share_width, voxels))
        volume = volume + voxel_scale * back_own.reshape(share_width, slab_depth, height)
        volume = smooth_share(
            volume,
            local_z,
            local_y,
            local_x,
            lower_rim,
            left_rim,
            z_first,
            z_total,
            share_first,
            column_count,
        )
        if iteration + 1 < ITERS:
            own_half = volume.astype(jnp.bfloat16).reshape(share_width, voxels)
            gathered = gather_angle(own_half, groups).reshape(column_count, voxels)
    volume_out = jnp.moveaxis(volume, 0, -1)
    return (volume_out, residual[None, None])


def solution(mesh):
    in_specs = (
        P("slab", None, None),
        P("slab", "angle", None, None, None),
        P("slab", "angle", None),
        P("slab", "angle"),
        P("angle", None),
        P("angle", "slab", None, None),
        P("slab", None, None),
        P("slab", None, None),
        P("slab", None, None),
    )
    out_specs = (P("slab", None, "angle"), P("angle", "slab", None, None))
    return jax.shard_map(shards, mesh=mesh, in_specs=in_specs, out_specs=out_specs, check_vma=False)
```

```python
import functools

import jax
import jax.numpy as jnp
from jax import lax
from jax.experimental import pallas as pl
from jax.experimental.pallas import tpu as pltpu
from jax.sharding import PartitionSpec as P

ITERS = 3


SMOOTH_EPS = 0.01
SMOOTH_RATE = 0.15

MESH_ID = pl.DeviceIdType.MESH


def from_behind(value, axis, steps):
    count = lax.axis_size(axis)
    first, last = (max(0, -steps), min(count, count - steps))
    return lax.ppermute(value, axis, [(source, source + steps) for source in range(first, last)])


def limiter(difference):
    return difference / jnp.sqrt(difference * difference + SMOOTH_EPS)


def _where_am_i():
    slab = lax.axis_index("slab")
    here = lax.axis_index("angle")
    chip = here // 2
    core = here % 2
    partner = here + 1 - 2 * core
    return slab, here, chip, core, partner


def _greet(slab, chip, core, partner, n_chip):
    barrier = pltpu.get_barrier_semaphore()
    pl.semaphore_signal(barrier, 1, device_id=(slab, partner), device_id_type=MESH_ID)
    for d in range(1, n_chip):
        peer = ((chip + d) % n_chip) * 2 + core
        pl.semaphore_signal(barrier, 1, device_id=(slab, peer), device_id_type=MESH_ID)
    pl.semaphore_wait(barrier, n_chip)


def _scatter_kernel(n_chip, part_ref, half_ref, out_ref, got_pair, got_ring, chip_sum,
                    send_a, recv_a, send_b, recv_b):
    slab, here, chip, core, partner = _where_am_i()
    _greet(slab, chip, core, partner, n_chip)
    order = list(range(1, n_chip)) + [0]
    pair = []
    for i, d in enumerate(order):
        dest = (chip + d) % n_chip
        copy = pltpu.make_async_remote_copy(
            src_ref=half_ref.at[2 * dest + 1 - core],
            dst_ref=got_pair.at[i],
            send_sem=send_a.at[i],
            recv_sem=recv_a.at[i],
            device_id=(slab, partner),
            device_id_type=MESH_ID,
        )
        copy.start()
        pair.append(copy)
    ring = []
    for i, d in enumerate(order[:-1]):
        dest = (chip + d) % n_chip
        pair[i].wait_recv()
        chip_sum[i] = (
            part_ref[2 * dest + core] + got_pair[i].astype(jnp.float32)
        ).astype(chip_sum.dtype)
        copy = pltpu.make_async_remote_copy(
            src_ref=chip_sum.at[i],
            dst_ref=got_ring.at[d],
            send_sem=send_b.at[d],
            recv_sem=recv_b.at[d],
            device_id=(slab, 2 * dest + core),
            device_id_type=MESH_ID,
        )
        copy.start()
        ring.append(copy)
    pair[-1].wait_recv()
    total = part_ref[here] + got_pair[n_chip - 1].astype(jnp.float32)
    for copy in pair:
        copy.wait_send()
    for copy in ring:
        copy.wait()
    for d in range(1, n_chip):
        total = total + got_ring[d].astype(jnp.float32)
    out_ref[...] = total


def scatter_angle(part):
    blocks, rows, cols = part.shape
    n_chip = blocks // 2
    link = part.dtype
    return pl.pallas_call(
        functools.partial(_scatter_kernel, n_chip),
        out_shape=jax.ShapeDtypeStruct((rows, cols), jnp.float32),
        in_specs=[pl.BlockSpec(memory_space=pltpu.VMEM)] * 2,
        out_specs=pl.BlockSpec(memory_space=pltpu.VMEM),
        scratch_shapes=[
            pltpu.VMEM((n_chip, rows, cols), link),
            pltpu.VMEM((n_chip, rows, cols), link),
            pltpu.VMEM((n_chip, rows, cols), link),
            pltpu.SemaphoreType.DMA((n_chip,)),
            pltpu.SemaphoreType.DMA((n_chip,)),
            pltpu.SemaphoreType.DMA((n_chip,)),
            pltpu.SemaphoreType.DMA((n_chip,)),
        ],
        compiler_params=pltpu.CompilerParams(collective_id=0, has_side_effects=True),
        cost_estimate=pl.CostEstimate(
            flops=2 * blocks * rows * cols, bytes_accessed=4 * 3 * blocks * rows * cols,
            transcendentals=0,
        ),
    )(part, part.astype(link))


def _sum_kernel(groups, part_ref, out_ref, got, send_sem, recv_sem):
    slab = lax.axis_index("slab")
    here = lax.axis_index("angle")
    barrier = pltpu.get_barrier_semaphore()
    for d in range(1, groups):
        peer = (here + d) % groups
        pl.semaphore_signal(barrier, 1, device_id=(slab, peer), device_id_type=MESH_ID)
    pl.semaphore_wait(barrier, groups - 1)
    copies = []
    for d in range(1, groups):
        copy = pltpu.make_async_remote_copy(
            src_ref=part_ref,
            dst_ref=got.at[d],
            send_sem=send_sem.at[d],
            recv_sem=recv_sem.at[d],
            device_id=(slab, (here + d) % groups),
            device_id_type=MESH_ID,
        )
        copy.start()
        copies.append(copy)
    total = part_ref[...]
    for copy in copies:
        copy.wait()
    for d in range(1, groups):
        total = total + got[d]
    out_ref[...] = total


def sum_angle(part, groups):
    return pl.pallas_call(
        functools.partial(_sum_kernel, groups),
        out_shape=jax.ShapeDtypeStruct(part.shape, part.dtype),
        in_specs=[pl.BlockSpec(memory_space=pltpu.VMEM)],
        out_specs=pl.BlockSpec(memory_space=pltpu.VMEM),
        scratch_shapes=[
            pltpu.VMEM((groups,) + part.shape, part.dtype),
            pltpu.SemaphoreType.DMA((groups,)),
            pltpu.SemaphoreType.DMA((groups,)),
        ],
        compiler_params=pltpu.CompilerParams(collective_id=2, has_side_effects=True),
        cost_estimate=pl.CostEstimate(
            flops=groups * part.size, bytes_accessed=4 * 2 * groups * part.size,
            transcendentals=0,
        ),
    )(part)


def _gather_kernel(n_chip, own_ref, out_ref, held, send_a, recv_a, send_b, recv_b, local_sem):
    slab, here, chip, core, partner = _where_am_i()
    _greet(slab, chip, core, partner, n_chip)
    mine = pltpu.make_async_copy(own_ref, held.at[here], local_sem.at[0])
    mine.start()
    pair = [
        pltpu.make_async_remote_copy(
            src_ref=own_ref,
            dst_ref=held.at[here],
            send_sem=send_b.at[0],
            recv_sem=recv_b.at[0],
            device_id=(slab, partner),
            device_id_type=MESH_ID,
        )
    ]
    pair[0].start()
    ring = [None]
    for d in range(1, n_chip):
        dest = (chip + d) % n_chip
        copy = pltpu.make_async_remote_copy(
            src_ref=own_ref,
            dst_ref=held.at[here],
            send_sem=send_a.at[d],
            recv_sem=recv_a.at[d],
            device_id=(slab, 2 * dest + core),
            device_id_type=MESH_ID,
        )
        copy.start()
        ring.append(copy)
    for d in range(1, n_chip):
        ring[d].wait_recv()
        block = 2 * ((chip - d + n_chip) % n_chip) + core
        copy = pltpu.make_async_remote_copy(
            src_ref=held.at[block],
            dst_ref=held.at[block],
            send_sem=send_b.at[d],
            recv_sem=recv_b.at[d],
            device_id=(slab, partner),
            device_id_type=MESH_ID,
        )
        copy.start()
        pair.append(copy)
    mine.wait()
    for d in range(1, n_chip):
        ring[d].wait_send()
    for copy in pair:
        copy.wait()
    out_ref[...] = held[...]


def gather_angle(own, groups):
    rows, cols = own.shape
    n_chip = groups // 2
    return pl.pallas_call(
        functools.partial(_gather_kernel, n_chip),
        out_shape=jax.ShapeDtypeStruct((groups, rows, cols), own.dtype),
        in_specs=[pl.BlockSpec(memory_space=pltpu.VMEM)],
        out_specs=pl.BlockSpec(memory_space=pltpu.VMEM),
        scratch_shapes=[
            pltpu.VMEM((groups, rows, cols), own.dtype),
            pltpu.SemaphoreType.DMA((n_chip,)),
            pltpu.SemaphoreType.DMA((n_chip,)),
            pltpu.SemaphoreType.DMA((n_chip,)),
            pltpu.SemaphoreType.DMA((n_chip,)),
            pltpu.SemaphoreType.DMA((1,)),
        ],
        compiler_params=pltpu.CompilerParams(collective_id=1, has_side_effects=True),
        cost_estimate=pl.CostEstimate(
            flops=0, bytes_accessed=2 * 2 * groups * rows * cols, transcendentals=0,
        ),
    )(own)


def smooth_share(
    volume,
    weight_z,
    weight_y,
    weight_x,
    lower_rim,
    left_rim,
    z_first,
    z_total,
    x_first,
    x_total,
):
    upper_halo = from_behind(volume[:, 0], "slab", -1)
    lower_halo = from_behind(volume[:, -1], "slab", 1)
    right_halo = from_behind(volume[0], "angle", -1)
    left_halo = from_behind(volume[-1], "angle", 1)
    upper = jnp.concatenate([volume[:, 1:], upper_halo[:, None]], axis=1)
    inside = (z_first + lax.broadcasted_iota(jnp.int32, volume.shape, 1) + 1 < z_total).astype(
        jnp.float32
    )
    face_flux = weight_z * limiter(upper - volume) * inside
    lower_flux = lower_rim * limiter(volume[:, 0] - lower_halo)
    previous = jnp.concatenate([lower_flux[:, None], face_flux[:, :-1]], axis=1)
    change = face_flux - previous
    following = jnp.concatenate([volume[:, :, 1:], jnp.zeros_like(volume[:, :, :1])], axis=2)
    inside = (lax.broadcasted_iota(jnp.int32, volume.shape, 2) < volume.shape[2] - 1).astype(
        jnp.float32
    )
    face_flux = weight_y * limiter(following - volume) * inside
    previous = jnp.concatenate([jnp.zeros_like(face_flux[:, :, :1]), face_flux[:, :, :-1]], axis=2)
    change = change + face_flux - previous
    following = jnp.concatenate([volume[1:], right_halo[None]], axis=0)
    inside = (x_first + lax.broadcasted_iota(jnp.int32, volume.shape, 0) + 1 < x_total).astype(
        jnp.float32
    )
    face_flux = weight_x * limiter(following - volume) * inside
    lower_flux = left_rim * limiter(volume[0] - left_halo)
    previous = jnp.concatenate([lower_flux[None], face_flux[:-1]], axis=0)
    change = change + face_flux - previous
    return volume + SMOOTH_RATE * change


def shards(volume0, weights, tile_block, tile_count, owner, sino, weight_z, weight_y, weight_x):
    tiles = weights[0, 0]
    slot_count, ray_count, voxels = tiles.shape
    slab_depth, height, column_count = volume0.shape
    blocks = tile_block[0, 0]
    live_count = tile_count[0, 0]
    owner_row = owner[0]
    live_slots = jnp.arange(slot_count, dtype=jnp.int32) < live_count
    select = (owner_row[None, :] == blocks[:, None]) & live_slots[:, None]
    slab_pos = lax.axis_index("slab")
    holder_ids = jnp.arange(owner_row.shape[0], dtype=jnp.int32)
    target = jnp.sum(jnp.where(select, holder_ids[None, :], 0), axis=1)
    distance_ids = jnp.arange(slot_count, dtype=jnp.int32)
    relative = ((target - slab_pos)[:, None] == distance_ids[None, :]) & live_slots[:, None]
    relative_float = relative.astype(jnp.float32)
    relative_half = relative.astype(jnp.bfloat16)
    flat_tiles = tiles.reshape(slot_count * ray_count, voxels)
    ray_local = jnp.dot(
        flat_tiles, jnp.ones((voxels,), jnp.bfloat16), preferred_element_type=jnp.float32
    )
    ray_sends = jnp.einsum("td,tr->dr", relative_float, ray_local.reshape(slot_count, ray_count))
    ray_total = ray_sends[0]
    for distance in range(1, slot_count):
        ray_total = ray_total + from_behind(ray_sends[distance], "slab", distance)
    live_rows = jnp.repeat(live_slots, ray_count).astype(jnp.bfloat16)
    voxel_local = jnp.dot(live_rows, flat_tiles, preferred_element_type=jnp.float32)
    voxel_total = sum_angle(voxel_local.reshape(slab_depth, height), lax.axis_size("angle"))
    ray_scale = 1.0 / ray_total
    voxel_scale = (1.0 / voxel_total).reshape(1, slab_depth, height)
    lower_all = from_behind(weight_z[slab_depth - 1], "slab", 1)
    z_first = slab_pos * slab_depth
    z_total = slab_depth * lax.axis_size("slab")
    groups = lax.axis_size("angle")
    share_width = column_count // groups
    angle_pos = lax.axis_index("angle")
    share_first = angle_pos * share_width

    def share_of(array):
        part = lax.dynamic_slice_in_dim(array, share_first, share_width, array.ndim - 1)
        return jnp.moveaxis(part, -1, 0).astype(jnp.float32)

    measured = sino[0, 0].astype(jnp.float32)
    volume = share_of(volume0)
    local_z = share_of(weight_z)
    local_y = share_of(weight_y)
    local_x = share_of(weight_x)
    lower_rim = share_of(lower_all)
    left_index = jnp.maximum(share_first - 1, 0)
    left_rim = lax.dynamic_index_in_dim(weight_x, left_index, 2, keepdims=False).astype(
        jnp.float32
    ) * (angle_pos > 0).astype(jnp.float32)
    gathered = None
    residual = jnp.zeros((ray_count, column_count), jnp.float32)
    for iteration in range(ITERS):
        if gathered is None:
            flat_volume = volume0.astype(jnp.bfloat16).reshape(voxels, column_count)
            products = jnp.einsum(
                "trv,vn->trn", tiles, flat_volume, preferred_element_type=jnp.float32
            ).astype(jnp.bfloat16)
        else:
            products = jnp.einsum(
                "trv,nv->trn", tiles, gathered, preferred_element_type=jnp.float32
            ).astype(jnp.bfloat16)
        sends = jnp.einsum(
            "td,trn->drn", relative_half, products, preferred_element_type=jnp.float32
        )
        sends_half = sends.astype(jnp.bfloat16)
        projected = sends[0]
        for distance in range(1, slot_count):
            arrived = from_behind(sends_half[distance], "slab", distance)
            projected = projected + arrived.astype(jnp.float32)
        residual = (measured - projected) * ray_scale[:, None]
        residual_half = residual.astype(jnp.bfloat16)
        nearby = [residual_half] + [
            from_behind(residual_half, "slab", -distance) for distance in range(1, slot_count)
        ]
        picked = jnp.einsum(
            "td,drn->trn", relative_half, jnp.stack(nearby), preferred_element_type=jnp.float32
        ).astype(jnp.bfloat16)
        back_t = jnp.einsum("trn,trv->nv", picked, tiles, preferred_element_type=jnp.float32)
        back_own = scatter_angle(back_t.reshape(groups, share_width, voxels))
        volume = volume + voxel_scale * back_own.reshape(share_width, slab_depth, height)
        volume = smooth_share(
            volume,
            local_z,
            local_y,
            local_x,
            lower_rim,
            left_rim,
            z_first,
            z_total,
            share_first,
            column_count,
        )
        if iteration + 1 < ITERS:
            own_half = volume.astype(jnp.bfloat16).reshape(share_width, voxels)
            gathered = gather_angle(own_half, groups).reshape(column_count, voxels)
    volume_out = jnp.moveaxis(volume, 0, -1)
    return (volume_out, residual[None, None])


def solution(mesh):
    in_specs = (
        P("slab", None, None),
        P("slab", "angle", None, None, None),
        P("slab", "angle", None),
        P("slab", "angle"),
        P("angle", None),
        P("angle", "slab", None, None),
        P("slab", None, None),
        P("slab", None, None),
        P("slab", None, None),
    )
    out_specs = (P("slab", None, "angle"), P("angle", "slab", None, None))
    return jax.shard_map(shards, mesh=mesh, in_specs=in_specs, out_specs=out_specs, check_vma=False)
```

```python
import functools

import jax
import jax.numpy as jnp
from jax import lax
from jax.experimental import pallas as pl
from jax.experimental.pallas import tpu as pltpu
from jax.sharding import PartitionSpec as P

ITERS = 3


SMOOTH_EPS = 0.01
SMOOTH_RATE = 0.15

MESH_ID = pl.DeviceIdType.MESH


def from_behind(value, axis, steps):
    count = lax.axis_size(axis)
    first, last = (max(0, -steps), min(count, count - steps))
    return lax.ppermute(value, axis, [(source, source + steps) for source in range(first, last)])


def limiter(difference):
    return difference / jnp.sqrt(difference * difference + SMOOTH_EPS)


def _where_am_i():
    slab = lax.axis_index("slab")
    here = lax.axis_index("angle")
    chip = here // 2
    core = here % 2
    partner = here + 1 - 2 * core
    return slab, here, chip, core, partner


def _greet(slab, chip, core, partner, n_chip):
    barrier = pltpu.get_barrier_semaphore()
    pl.semaphore_signal(barrier, 1, device_id=(slab, partner), device_id_type=MESH_ID)
    for d in range(1, n_chip):
        peer = ((chip + d) % n_chip) * 2 + core
        pl.semaphore_signal(barrier, 1, device_id=(slab, peer), device_id_type=MESH_ID)
    pl.semaphore_wait(barrier, n_chip)


def _scatter_kernel(n_chip, part_ref, half_ref, out_ref, got_pair, got_ring, chip_sum,
                    send_a, recv_a, send_b, recv_b):
    slab, here, chip, core, partner = _where_am_i()
    _greet(slab, chip, core, partner, n_chip)
    order = list(range(1, n_chip)) + [0]
    pair = []
    for i, d in enumerate(order):
        dest = (chip + d) % n_chip
        copy = pltpu.make_async_remote_copy(
            src_ref=half_ref.at[2 * dest + 1 - core],
            dst_ref=got_pair.at[i],
            send_sem=send_a.at[i],
            recv_sem=recv_a.at[i],
            device_id=(slab, partner),
            device_id_type=MESH_ID,
        )
        copy.start()
        pair.append(copy)
    ring = []
    for i, d in enumerate(order[:-1]):
        dest = (chip + d) % n_chip
        pair[i].wait_recv()
        chip_sum[i] = (
            part_ref[2 * dest + core] + got_pair[i].astype(jnp.float32)
        ).astype(chip_sum.dtype)
        copy = pltpu.make_async_remote_copy(
            src_ref=chip_sum.at[i],
            dst_ref=got_ring.at[d],
            send_sem=send_b.at[d],
            recv_sem=recv_b.at[d],
            device_id=(slab, 2 * dest + core),
            device_id_type=MESH_ID,
        )
        copy.start()
        ring.append(copy)
    pair[-1].wait_recv()
    total = part_ref[here] + got_pair[n_chip - 1].astype(jnp.float32)
    for copy in pair:
        copy.wait_send()
    for copy in ring:
        copy.wait()
    for d in range(1, n_chip):
        total = total + got_ring[d].astype(jnp.float32)
    out_ref[...] = total


def scatter_angle(part):
    blocks, rows, cols = part.shape
    n_chip = blocks // 2
    link = part.dtype
    return pl.pallas_call(
        functools.partial(_scatter_kernel, n_chip),
        out_shape=jax.ShapeDtypeStruct((rows, cols), jnp.float32),
        in_specs=[pl.BlockSpec(memory_space=pltpu.VMEM)] * 2,
        out_specs=pl.BlockSpec(memory_space=pltpu.VMEM),
        scratch_shapes=[
            pltpu.VMEM((n_chip, rows, cols), link),
            pltpu.VMEM((n_chip, rows, cols), link),
            pltpu.VMEM((n_chip, rows, cols), link),
            pltpu.SemaphoreType.DMA((n_chip,)),
            pltpu.SemaphoreType.DMA((n_chip,)),
            pltpu.SemaphoreType.DMA((n_chip,)),
            pltpu.SemaphoreType.DMA((n_chip,)),
        ],
        compiler_params=pltpu.CompilerParams(collective_id=0, has_side_effects=True),
        cost_estimate=pl.CostEstimate(
            flops=2 * blocks * rows * cols, bytes_accessed=4 * 3 * blocks * rows * cols,
            transcendentals=0,
        ),
    )(part, part.astype(link))


def _sum_kernel(groups, part_ref, out_ref, got, send_sem, recv_sem):
    slab = lax.axis_index("slab")
    here = lax.axis_index("angle")
    barrier = pltpu.get_barrier_semaphore()
    for d in range(1, groups):
        peer = (here + d) % groups
        pl.semaphore_signal(barrier, 1, device_id=(slab, peer), device_id_type=MESH_ID)
    pl.semaphore_wait(barrier, groups - 1)
    copies = []
    for d in range(1, groups):
        copy = pltpu.make_async_remote_copy(
            src_ref=part_ref,
            dst_ref=got.at[d],
            send_sem=send_sem.at[d],
            recv_sem=recv_sem.at[d],
            device_id=(slab, (here + d) % groups),
            device_id_type=MESH_ID,
        )
        copy.start()
        copies.append(copy)
    total = part_ref[...]
    for copy in copies:
        copy.wait()
    for d in range(1, groups):
        total = total + got[d]
    out_ref[...] = total


def sum_angle(part, groups):
    return pl.pallas_call(
        functools.partial(_sum_kernel, groups),
        out_shape=jax.ShapeDtypeStruct(part.shape, part.dtype),
        in_specs=[pl.BlockSpec(memory_space=pltpu.VMEM)],
        out_specs=pl.BlockSpec(memory_space=pltpu.VMEM),
        scratch_shapes=[
            pltpu.VMEM((groups,) + part.shape, part.dtype),
            pltpu.SemaphoreType.DMA((groups,)),
            pltpu.SemaphoreType.DMA((groups,)),
        ],
        compiler_params=pltpu.CompilerParams(collective_id=2, has_side_effects=True),
        cost_estimate=pl.CostEstimate(
            flops=groups * part.size, bytes_accessed=4 * 2 * groups * part.size,
            transcendentals=0,
        ),
    )(part)


def _gather_kernel(n_chip, own_ref, out_ref, held, send_a, recv_a, send_b, recv_b, local_sem):
    slab, here, chip, core, partner = _where_am_i()
    _greet(slab, chip, core, partner, n_chip)
    mine = pltpu.make_async_copy(own_ref, held.at[here], local_sem.at[0])
    mine.start()
    pair = [
        pltpu.make_async_remote_copy(
            src_ref=own_ref,
            dst_ref=held.at[here],
            send_sem=send_b.at[0],
            recv_sem=recv_b.at[0],
            device_id=(slab, partner),
            device_id_type=MESH_ID,
        )
    ]
    pair[0].start()
    ring = [None]
    for d in range(1, n_chip):
        dest = (chip + d) % n_chip
        copy = pltpu.make_async_remote_copy(
            src_ref=own_ref,
            dst_ref=held.at[here],
            send_sem=send_a.at[d],
            recv_sem=recv_a.at[d],
            device_id=(slab, 2 * dest + core),
            device_id_type=MESH_ID,
        )
        copy.start()
        ring.append(copy)
    for d in range(1, n_chip):
        ring[d].wait_recv()
        block = 2 * ((chip - d + n_chip) % n_chip) + core
        copy = pltpu.make_async_remote_copy(
            src_ref=held.at[block],
            dst_ref=held.at[block],
            send_sem=send_b.at[d],
            recv_sem=recv_b.at[d],
            device_id=(slab, partner),
            device_id_type=MESH_ID,
        )
        copy.start()
        pair.append(copy)
    mine.wait()
    for d in range(1, n_chip):
        ring[d].wait_send()
    for copy in pair:
        copy.wait()
    out_ref[...] = held[...]


def gather_angle(own, groups):
    rows, cols = own.shape
    n_chip = groups // 2
    return pl.pallas_call(
        functools.partial(_gather_kernel, n_chip),
        out_shape=jax.ShapeDtypeStruct((groups, rows, cols), own.dtype),
        in_specs=[pl.BlockSpec(memory_space=pltpu.VMEM)],
        out_specs=pl.BlockSpec(memory_space=pltpu.VMEM),
        scratch_shapes=[
            pltpu.VMEM((groups, rows, cols), own.dtype),
            pltpu.SemaphoreType.DMA((n_chip,)),
            pltpu.SemaphoreType.DMA((n_chip,)),
            pltpu.SemaphoreType.DMA((n_chip,)),
            pltpu.SemaphoreType.DMA((n_chip,)),
            pltpu.SemaphoreType.DMA((1,)),
        ],
        compiler_params=pltpu.CompilerParams(collective_id=1, has_side_effects=True),
        cost_estimate=pl.CostEstimate(
            flops=0, bytes_accessed=2 * 2 * groups * rows * cols, transcendentals=0,
        ),
    )(own)


def smooth_share(
    volume,
    weight_z,
    weight_y,
    weight_x,
    lower_rim,
    left_rim,
    z_first,
    z_total,
    x_first,
    x_total,
):
    upper_halo = from_behind(volume[:, 0], "slab", -1)
    lower_halo = from_behind(volume[:, -1], "slab", 1)
    right_halo = from_behind(volume[0], "angle", -1)
    left_halo = from_behind(volume[-1], "angle", 1)
    upper = jnp.concatenate([volume[:, 1:], upper_halo[:, None]], axis=1)
    inside = (z_first + lax.broadcasted_iota(jnp.int32, volume.shape, 1) + 1 < z_total).astype(
        jnp.float32
    )
    face_flux = weight_z * limiter(upper - volume) * inside
    lower_flux = lower_rim * limiter(volume[:, 0] - lower_halo)
    previous = jnp.concatenate([lower_flux[:, None], face_flux[:, :-1]], axis=1)
    change = face_flux - previous
    following = jnp.concatenate([volume[:, :, 1:], jnp.zeros_like(volume[:, :, :1])], axis=2)
    inside = (lax.broadcasted_iota(jnp.int32, volume.shape, 2) < volume.shape[2] - 1).astype(
        jnp.float32
    )
    face_flux = weight_y * limiter(following - volume) * inside
    previous = jnp.concatenate([jnp.zeros_like(face_flux[:, :, :1]), face_flux[:, :, :-1]], axis=2)
    change = change + face_flux - previous
    following = jnp.concatenate([volume[1:], right_halo[None]], axis=0)
    inside = (x_first + lax.broadcasted_iota(jnp.int32, volume.shape, 0) + 1 < x_total).astype(
        jnp.float32
    )
    face_flux = weight_x * limiter(following - volume) * inside
    lower_flux = left_rim * limiter(volume[0] - left_halo)
    previous = jnp.concatenate([lower_flux[None], face_flux[:-1]], axis=0)
    change = change + face_flux - previous
    return volume + SMOOTH_RATE * change


def shards(volume0, weights, tile_block, tile_count, owner, sino, weight_z, weight_y, weight_x):
    tiles = weights[0, 0]
    slot_count, ray_count, voxels = tiles.shape
    slab_depth, height, column_count = volume0.shape
    blocks = tile_block[0, 0]
    live_count = tile_count[0, 0]
    owner_row = owner[0]
    live_slots = jnp.arange(slot_count, dtype=jnp.int32) < live_count
    select = (owner_row[None, :] == blocks[:, None]) & live_slots[:, None]
    slab_pos = lax.axis_index("slab")
    holder_ids = jnp.arange(owner_row.shape[0], dtype=jnp.int32)
    target = jnp.sum(jnp.where(select, holder_ids[None, :], 0), axis=1)
    distance_ids = jnp.arange(slot_count, dtype=jnp.int32)
    relative = ((target - slab_pos)[:, None] == distance_ids[None, :]) & live_slots[:, None]
    relative_float = relative.astype(jnp.float32)
    far_relative = relative[1:, 1:].astype(jnp.bfloat16)
    flat_tiles = tiles.reshape(slot_count * ray_count, voxels)
    ray_local = jnp.dot(
        flat_tiles, jnp.ones((voxels,), jnp.bfloat16), preferred_element_type=jnp.float32
    )
    ray_sends = jnp.einsum("td,tr->dr", relative_float, ray_local.reshape(slot_count, ray_count))
    ray_total = ray_sends[0]
    for distance in range(1, slot_count):
        ray_total = ray_total + from_behind(ray_sends[distance], "slab", distance)
    live_rows = jnp.repeat(live_slots, ray_count).astype(jnp.bfloat16)
    voxel_local = jnp.dot(live_rows, flat_tiles, preferred_element_type=jnp.float32)
    voxel_total = sum_angle(voxel_local.reshape(slab_depth, height), lax.axis_size("angle"))
    ray_scale = 1.0 / ray_total
    voxel_scale = (1.0 / voxel_total).reshape(1, slab_depth, height)
    lower_all = from_behind(weight_z[slab_depth - 1], "slab", 1)
    z_first = slab_pos * slab_depth
    z_total = slab_depth * lax.axis_size("slab")
    groups = lax.axis_size("angle")
    share_width = column_count // groups
    angle_pos = lax.axis_index("angle")
    share_first = angle_pos * share_width

    def share_of(array):
        part = lax.dynamic_slice_in_dim(array, share_first, share_width, array.ndim - 1)
        return jnp.moveaxis(part, -1, 0).astype(jnp.float32)

    measured = sino[0, 0].astype(jnp.float32)
    volume = share_of(volume0)
    local_z = share_of(weight_z)
    local_y = share_of(weight_y)
    local_x = share_of(weight_x)
    lower_rim = share_of(lower_all)
    left_index = jnp.maximum(share_first - 1, 0)
    left_rim = lax.dynamic_index_in_dim(weight_x, left_index, 2, keepdims=False).astype(
        jnp.float32
    ) * (angle_pos > 0).astype(jnp.float32)
    gathered = None
    residual = jnp.zeros((ray_count, column_count), jnp.float32)
    for iteration in range(ITERS):
        if gathered is None:
            flat_volume = volume0.astype(jnp.bfloat16).reshape(voxels, column_count)
            far_products = jnp.einsum(
                "trv,vn->trn", tiles[1:], flat_volume, preferred_element_type=jnp.float32
            ).astype(jnp.bfloat16)
        else:
            far_products = jnp.einsum(
                "trv,nv->trn", tiles[1:], gathered, preferred_element_type=jnp.float32
            ).astype(jnp.bfloat16)
        sends_half = jnp.einsum(
            "td,trn->drn", far_relative, far_products, preferred_element_type=jnp.float32
        ).astype(jnp.bfloat16)
        arrived = [
            from_behind(sends_half[distance - 1], "slab", distance)
            for distance in range(1, slot_count)
        ]
        if gathered is None:
            near_products = jnp.einsum(
                "rv,vn->rn", tiles[0], flat_volume, preferred_element_type=jnp.float32
            )
        else:
            near_products = jnp.einsum(
                "rv,nv->rn", tiles[0], gathered, preferred_element_type=jnp.float32
            )
        near_products = lax.optimization_barrier(near_products.astype(jnp.bfloat16))
        projected = near_products.astype(jnp.float32)
        for distance in range(1, slot_count):
            projected = projected + arrived[distance - 1].astype(jnp.float32)
        residual = (measured - projected) * ray_scale[:, None]
        residual_half = residual.astype(jnp.bfloat16)
        nearby = [
            from_behind(residual_half, "slab", -distance) for distance in range(1, slot_count)
        ]
        near_back = lax.optimization_barrier(
            jnp.einsum("rn,rv->nv", residual_half, tiles[0], preferred_element_type=jnp.float32)
        )
        picked = jnp.einsum(
            "td,drn->trn", far_relative, jnp.stack(nearby), preferred_element_type=jnp.float32
        ).astype(jnp.bfloat16)
        back_t = near_back + jnp.einsum(
            "trn,trv->nv", picked, tiles[1:], preferred_element_type=jnp.float32
        )
        back_own = scatter_angle(back_t.reshape(groups, share_width, voxels))
        volume = volume + voxel_scale * back_own.reshape(share_width, slab_depth, height)
        volume = smooth_share(
            volume,
            local_z,
            local_y,
            local_x,
            lower_rim,
            left_rim,
            z_first,
            z_total,
            share_first,
            column_count,
        )
        if iteration + 1 < ITERS:
            own_half = volume.astype(jnp.bfloat16).reshape(share_width, voxels)
            gathered = gather_angle(own_half, groups).reshape(column_count, voxels)
    volume_out = jnp.moveaxis(volume, 0, -1)
    return (volume_out, residual[None, None])


def solution(mesh):
    in_specs = (
        P("slab", None, None),
        P("slab", "angle", None, None, None),
        P("slab", "angle", None),
        P("slab", "angle"),
        P("angle", None),
        P("angle", "slab", None, None),
        P("slab", None, None),
        P("slab", None, None),
        P("slab", None, None),
    )
    out_specs = (P("slab", None, "angle"), P("angle", "slab", None, None))
    return jax.shard_map(shards, mesh=mesh, in_specs=in_specs, out_specs=out_specs, check_vma=False)
```

```python
import functools

import jax
import jax.numpy as jnp
from jax import lax
from jax.experimental import pallas as pl
from jax.experimental.pallas import tpu as pltpu
from jax.sharding import PartitionSpec as P

ITERS = 3


SMOOTH_EPS = 0.01
SMOOTH_RATE = 0.15

MESH_ID = pl.DeviceIdType.MESH


def from_behind(value, axis, steps):
    count = lax.axis_size(axis)
    first, last = (max(0, -steps), min(count, count - steps))
    return lax.ppermute(value, axis, [(source, source + steps) for source in range(first, last)])


def limiter(difference):
    return difference / jnp.sqrt(difference * difference + SMOOTH_EPS)


def _where_am_i():
    slab = lax.axis_index("slab")
    here = lax.axis_index("angle")
    chip = here // 2
    core = here % 2
    partner = here + 1 - 2 * core
    return slab, here, chip, core, partner


def _greet(slab, chip, core, partner, n_chip):
    barrier = pltpu.get_barrier_semaphore()
    pl.semaphore_signal(barrier, 1, device_id=(slab, partner), device_id_type=MESH_ID)
    for d in range(1, n_chip):
        peer = ((chip + d) % n_chip) * 2 + core
        pl.semaphore_signal(barrier, 1, device_id=(slab, peer), device_id_type=MESH_ID)
    pl.semaphore_wait(barrier, n_chip)


def _scatter_kernel(n_chip, part_ref, half_ref, out_ref, got_pair, got_ring, chip_sum,
                    send_a, recv_a, send_b, recv_b):
    slab, here, chip, core, partner = _where_am_i()
    _greet(slab, chip, core, partner, n_chip)
    order = list(range(1, n_chip)) + [0]
    pair = []
    for i, d in enumerate(order):
        dest = (chip + d) % n_chip
        copy = pltpu.make_async_remote_copy(
            src_ref=half_ref.at[2 * dest + 1 - core],
            dst_ref=got_pair.at[i],
            send_sem=send_a.at[i],
            recv_sem=recv_a.at[i],
            device_id=(slab, partner),
            device_id_type=MESH_ID,
        )
        copy.start()
        pair.append(copy)
    ring = []
    for i, d in enumerate(order[:-1]):
        dest = (chip + d) % n_chip
        pair[i].wait_recv()
        chip_sum[i] = (
            part_ref[2 * dest + core] + got_pair[i].astype(jnp.float32)
        ).astype(chip_sum.dtype)
        copy = pltpu.make_async_remote_copy(
            src_ref=chip_sum.at[i],
            dst_ref=got_ring.at[d],
            send_sem=send_b.at[d],
            recv_sem=recv_b.at[d],
            device_id=(slab, 2 * dest + core),
            device_id_type=MESH_ID,
        )
        copy.start()
        ring.append(copy)
    pair[-1].wait_recv()
    total = part_ref[here] + got_pair[n_chip - 1].astype(jnp.float32)
    for copy in pair:
        copy.wait_send()
    for copy in ring:
        copy.wait()
    for d in range(1, n_chip):
        total = total + got_ring[d].astype(jnp.float32)
    out_ref[...] = total


def scatter_angle(part):
    blocks, rows, cols = part.shape
    n_chip = blocks // 2
    link = part.dtype
    return pl.pallas_call(
        functools.partial(_scatter_kernel, n_chip),
        out_shape=jax.ShapeDtypeStruct((rows, cols), jnp.float32),
        in_specs=[pl.BlockSpec(memory_space=pltpu.VMEM)] * 2,
        out_specs=pl.BlockSpec(memory_space=pltpu.VMEM),
        scratch_shapes=[
            pltpu.VMEM((n_chip, rows, cols), link),
            pltpu.VMEM((n_chip, rows, cols), link),
            pltpu.VMEM((n_chip, rows, cols), link),
            pltpu.SemaphoreType.DMA((n_chip,)),
            pltpu.SemaphoreType.DMA((n_chip,)),
            pltpu.SemaphoreType.DMA((n_chip,)),
            pltpu.SemaphoreType.DMA((n_chip,)),
        ],
        compiler_params=pltpu.CompilerParams(collective_id=0, has_side_effects=True),
        cost_estimate=pl.CostEstimate(
            flops=2 * blocks * rows * cols, bytes_accessed=4 * 3 * blocks * rows * cols,
            transcendentals=0,
        ),
    )(part, part.astype(link))


def _sum_kernel(groups, part_ref, out_ref, got, send_sem, recv_sem):
    slab = lax.axis_index("slab")
    here = lax.axis_index("angle")
    barrier = pltpu.get_barrier_semaphore()
    for d in range(1, groups):
        peer = (here + d) % groups
        pl.semaphore_signal(barrier, 1, device_id=(slab, peer), device_id_type=MESH_ID)
    pl.semaphore_wait(barrier, groups - 1)
    copies = []
    for d in range(1, groups):
        copy = pltpu.make_async_remote_copy(
            src_ref=part_ref,
            dst_ref=got.at[d],
            send_sem=send_sem.at[d],
            recv_sem=recv_sem.at[d],
            device_id=(slab, (here + d) % groups),
            device_id_type=MESH_ID,
        )
        copy.start()
        copies.append(copy)
    total = part_ref[...]
    for copy in copies:
        copy.wait()
    for d in range(1, groups):
        total = total + got[d]
    out_ref[...] = total


def sum_angle(part, groups):
    return pl.pallas_call(
        functools.partial(_sum_kernel, groups),
        out_shape=jax.ShapeDtypeStruct(part.shape, part.dtype),
        in_specs=[pl.BlockSpec(memory_space=pltpu.VMEM)],
        out_specs=pl.BlockSpec(memory_space=pltpu.VMEM),
        scratch_shapes=[
            pltpu.VMEM((groups,) + part.shape, part.dtype),
            pltpu.SemaphoreType.DMA((groups,)),
            pltpu.SemaphoreType.DMA((groups,)),
        ],
        compiler_params=pltpu.CompilerParams(collective_id=2, has_side_effects=True),
        cost_estimate=pl.CostEstimate(
            flops=groups * part.size, bytes_accessed=4 * 2 * groups * part.size,
            transcendentals=0,
        ),
    )(part)


def _gather_kernel(n_chip, own_ref, out_ref, held, send_a, recv_a, send_b, recv_b, local_sem):
    slab, here, chip, core, partner = _where_am_i()
    _greet(slab, chip, core, partner, n_chip)
    mine = pltpu.make_async_copy(own_ref, held.at[here], local_sem.at[0])
    mine.start()
    pair = [
        pltpu.make_async_remote_copy(
            src_ref=own_ref,
            dst_ref=held.at[here],
            send_sem=send_b.at[0],
            recv_sem=recv_b.at[0],
            device_id=(slab, partner),
            device_id_type=MESH_ID,
        )
    ]
    pair[0].start()
    ring = [None]
    for d in range(1, n_chip):
        dest = (chip + d) % n_chip
        copy = pltpu.make_async_remote_copy(
            src_ref=own_ref,
            dst_ref=held.at[here],
            send_sem=send_a.at[d],
            recv_sem=recv_a.at[d],
            device_id=(slab, 2 * dest + core),
            device_id_type=MESH_ID,
        )
        copy.start()
        ring.append(copy)
    for d in range(1, n_chip):
        ring[d].wait_recv()
        block = 2 * ((chip - d + n_chip) % n_chip) + core
        copy = pltpu.make_async_remote_copy(
            src_ref=held.at[block],
            dst_ref=held.at[block],
            send_sem=send_b.at[d],
            recv_sem=recv_b.at[d],
            device_id=(slab, partner),
            device_id_type=MESH_ID,
        )
        copy.start()
        pair.append(copy)
    mine.wait()
    for d in range(1, n_chip):
        ring[d].wait_send()
    for copy in pair:
        copy.wait()
    out_ref[...] = held[...]


def gather_angle(own, groups):
    rows, cols = own.shape
    n_chip = groups // 2
    return pl.pallas_call(
        functools.partial(_gather_kernel, n_chip),
        out_shape=jax.ShapeDtypeStruct((groups, rows, cols), own.dtype),
        in_specs=[pl.BlockSpec(memory_space=pltpu.VMEM)],
        out_specs=pl.BlockSpec(memory_space=pltpu.VMEM),
        scratch_shapes=[
            pltpu.VMEM((groups, rows, cols), own.dtype),
            pltpu.SemaphoreType.DMA((n_chip,)),
            pltpu.SemaphoreType.DMA((n_chip,)),
            pltpu.SemaphoreType.DMA((n_chip,)),
            pltpu.SemaphoreType.DMA((n_chip,)),
            pltpu.SemaphoreType.DMA((1,)),
        ],
        compiler_params=pltpu.CompilerParams(collective_id=1, has_side_effects=True),
        cost_estimate=pl.CostEstimate(
            flops=0, bytes_accessed=2 * 2 * groups * rows * cols, transcendentals=0,
        ),
    )(own)


def _project_kernel(w_ref, v_ref, o_ref):
    o_ref[...] = jnp.dot(w_ref[...], v_ref[...], preferred_element_type=jnp.float32).astype(
        o_ref.dtype
    )


def project(tiles, volume, first, count, rows=256):
    ray_count, voxels = tiles.shape[1:]
    columns = volume.shape[1]
    return pl.pallas_call(
        _project_kernel,
        grid=(count, ray_count // rows),
        in_specs=[
            pl.BlockSpec((None, rows, voxels), lambda t, r: (t + first, r, 0)),
            pl.BlockSpec((voxels, columns), lambda t, r: (0, 0)),
        ],
        out_specs=pl.BlockSpec((None, rows, columns), lambda t, r: (t, r, 0)),
        out_shape=jax.ShapeDtypeStruct((count, ray_count, columns), jnp.bfloat16),
        cost_estimate=pl.CostEstimate(
            flops=2 * count * ray_count * voxels * columns,
            bytes_accessed=2 * (count * ray_count * voxels + voxels * columns),
            transcendentals=0,
        ),
    )(tiles, volume)


def _back_kernel(p_ref, w_ref, o_ref):
    @pl.when((pl.program_id(0) == 0) & (pl.program_id(1) == 0))
    def _():
        o_ref[...] = jnp.zeros_like(o_ref)

    o_ref[...] += jnp.dot(p_ref[...], w_ref[...], preferred_element_type=jnp.float32)


def back_project(picked_t, tiles, first, rows=256):
    count, columns, ray_count = picked_t.shape
    voxels = tiles.shape[2]
    return pl.pallas_call(
        _back_kernel,
        grid=(count, ray_count // rows),
        in_specs=[
            pl.BlockSpec((None, columns, rows), lambda t, r: (t, 0, r)),
            pl.BlockSpec((None, rows, voxels), lambda t, r: (t + first, r, 0)),
        ],
        out_specs=pl.BlockSpec((columns, voxels), lambda t, r: (0, 0)),
        out_shape=jax.ShapeDtypeStruct((columns, voxels), jnp.float32),
        cost_estimate=pl.CostEstimate(
            flops=2 * count * ray_count * voxels * columns,
            bytes_accessed=2 * count * ray_count * voxels + 4 * columns * voxels,
            transcendentals=0,
        ),
    )(picked_t, tiles)


def smooth_share(
    volume,
    weight_z,
    weight_y,
    weight_x,
    lower_rim,
    left_rim,
    z_first,
    z_total,
    x_first,
    x_total,
):
    upper_halo = from_behind(volume[:, 0], "slab", -1)
    lower_halo = from_behind(volume[:, -1], "slab", 1)
    right_halo = from_behind(volume[0], "angle", -1)
    left_halo = from_behind(volume[-1], "angle", 1)
    upper = jnp.concatenate([volume[:, 1:], upper_halo[:, None]], axis=1)
    inside = (z_first + lax.broadcasted_iota(jnp.int32, volume.shape, 1) + 1 < z_total).astype(
        jnp.float32
    )
    face_flux = weight_z * limiter(upper - volume) * inside
    lower_flux = lower_rim * limiter(volume[:, 0] - lower_halo)
    previous = jnp.concatenate([lower_flux[:, None], face_flux[:, :-1]], axis=1)
    change = face_flux - previous
    following = jnp.concatenate([volume[:, :, 1:], jnp.zeros_like(volume[:, :, :1])], axis=2)
    inside = (lax.broadcasted_iota(jnp.int32, volume.shape, 2) < volume.shape[2] - 1).astype(
        jnp.float32
    )
    face_flux = weight_y * limiter(following - volume) * inside
    previous = jnp.concatenate([jnp.zeros_like(face_flux[:, :, :1]), face_flux[:, :, :-1]], axis=2)
    change = change + face_flux - previous
    following = jnp.concatenate([volume[1:], right_halo[None]], axis=0)
    inside = (x_first + lax.broadcasted_iota(jnp.int32, volume.shape, 0) + 1 < x_total).astype(
        jnp.float32
    )
    face_flux = weight_x * limiter(following - volume) * inside
    lower_flux = left_rim * limiter(volume[0] - left_halo)
    previous = jnp.concatenate([lower_flux[None], face_flux[:-1]], axis=0)
    change = change + face_flux - previous
    return volume + SMOOTH_RATE * change


def shards(volume0, weights, tile_block, tile_count, owner, sino, weight_z, weight_y, weight_x):
    tiles = weights[0, 0]
    slot_count, ray_count, voxels = tiles.shape
    slab_depth, height, column_count = volume0.shape
    blocks = tile_block[0, 0]
    live_count = tile_count[0, 0]
    owner_row = owner[0]
    live_slots = jnp.arange(slot_count, dtype=jnp.int32) < live_count
    select = (owner_row[None, :] == blocks[:, None]) & live_slots[:, None]
    slab_pos = lax.axis_index("slab")
    holder_ids = jnp.arange(owner_row.shape[0], dtype=jnp.int32)
    target = jnp.sum(jnp.where(select, holder_ids[None, :], 0), axis=1)
    distance_ids = jnp.arange(slot_count, dtype=jnp.int32)
    relative = ((target - slab_pos)[:, None] == distance_ids[None, :]) & live_slots[:, None]
    relative_float = relative.astype(jnp.float32)
    far_relative = relative[1:, 1:].astype(jnp.bfloat16)
    flat_tiles = tiles.reshape(slot_count * ray_count, voxels)
    ray_local = jnp.dot(
        flat_tiles, jnp.ones((voxels,), jnp.bfloat16), preferred_element_type=jnp.float32
    )
    ray_sends = jnp.einsum("td,tr->dr", relative_float, ray_local.reshape(slot_count, ray_count))
    ray_total = ray_sends[0]
    for distance in range(1, slot_count):
        ray_total = ray_total + from_behind(ray_sends[distance], "slab", distance)
    live_rows = jnp.repeat(live_slots, ray_count).astype(jnp.bfloat16)
    voxel_local = jnp.dot(live_rows, flat_tiles, preferred_element_type=jnp.float32)
    voxel_total = sum_angle(voxel_local.reshape(slab_depth, height), lax.axis_size("angle"))
    ray_scale = 1.0 / ray_total
    voxel_scale = (1.0 / voxel_total).reshape(1, slab_depth, height)
    lower_all = from_behind(weight_z[slab_depth - 1], "slab", 1)
    z_first = slab_pos * slab_depth
    z_total = slab_depth * lax.axis_size("slab")
    groups = lax.axis_size("angle")
    share_width = column_count // groups
    angle_pos = lax.axis_index("angle")
    share_first = angle_pos * share_width

    def share_of(array):
        part = lax.dynamic_slice_in_dim(array, share_first, share_width, array.ndim - 1)
        return jnp.moveaxis(part, -1, 0).astype(jnp.float32)

    measured = sino[0, 0].astype(jnp.float32)
    volume = share_of(volume0)
    local_z = share_of(weight_z)
    local_y = share_of(weight_y)
    local_x = share_of(weight_x)
    lower_rim = share_of(lower_all)
    left_index = jnp.maximum(share_first - 1, 0)
    left_rim = lax.dynamic_index_in_dim(weight_x, left_index, 2, keepdims=False).astype(
        jnp.float32
    ) * (angle_pos > 0).astype(jnp.float32)
    gathered = None
    residual = jnp.zeros((ray_count, column_count), jnp.float32)
    for iteration in range(ITERS):
        if gathered is None:
            flat_volume = volume0.astype(jnp.bfloat16).reshape(voxels, column_count)
        else:
            flat_volume = gathered.T
        far_products = project(tiles, flat_volume, 1, slot_count - 1)
        sends_half = jnp.einsum(
            "td,trn->drn", far_relative, far_products, preferred_element_type=jnp.float32
        ).astype(jnp.bfloat16)
        arrived = [
            from_behind(sends_half[distance - 1], "slab", distance)
            for distance in range(1, slot_count)
        ]
        near_products = project(tiles, flat_volume, 0, 1)[0]
        projected = near_products.astype(jnp.float32)
        for distance in range(1, slot_count):
            projected = projected + arrived[distance - 1].astype(jnp.float32)
        residual = (measured - projected) * ray_scale[:, None]
        residual_half = residual.astype(jnp.bfloat16)
        nearby = [
            from_behind(residual_half, "slab", -distance) for distance in range(1, slot_count)
        ]
        near_back = back_project(residual_half.T[None], tiles, 0)
        picked_t = jnp.einsum(
            "td,drn->tnr", far_relative, jnp.stack(nearby), preferred_element_type=jnp.float32
        ).astype(jnp.bfloat16)
        back_t = near_back + back_project(picked_t, tiles, 1)
        back_own = scatter_angle(back_t.reshape(groups, share_width, voxels))
        volume = volume + voxel_scale * back_own.reshape(share_width, slab_depth, height)
        volume = smooth_share(
            volume,
            local_z,
            local_y,
            local_x,
            lower_rim,
            left_rim,
            z_first,
            z_total,
            share_first,
            column_count,
        )
        if iteration + 1 < ITERS:
            own_half = volume.astype(jnp.bfloat16).reshape(share_width, voxels)
            gathered = gather_angle(own_half, groups).reshape(column_count, voxels)
    volume_out = jnp.moveaxis(volume, 0, -1)
    return (volume_out, residual[None, None])


def solution(mesh):
    in_specs = (
        P("slab", None, None),
        P("slab", "angle", None, None, None),
        P("slab", "angle", None),
        P("slab", "angle"),
        P("angle", None),
        P("angle", "slab", None, None),
        P("slab", None, None),
        P("slab", None, None),
        P("slab", None, None),
    )
    out_specs = (P("slab", None, "angle"), P("angle", "slab", None, None))
    return jax.shard_map(shards, mesh=mesh, in_specs=in_specs, out_specs=out_specs, check_vma=False)
```

```python
import functools

import jax
import jax.numpy as jnp
from jax import lax
from jax.experimental import pallas as pl
from jax.experimental.pallas import tpu as pltpu
from jax.sharding import PartitionSpec as P

ITERS = 3


SMOOTH_EPS = 0.01
SMOOTH_RATE = 0.15

MESH_ID = pl.DeviceIdType.MESH


def from_behind(value, axis, steps):
    count = lax.axis_size(axis)
    first, last = (max(0, -steps), min(count, count - steps))
    return lax.ppermute(value, axis, [(source, source + steps) for source in range(first, last)])


def limiter(difference):
    return difference / jnp.sqrt(difference * difference + SMOOTH_EPS)


def _where_am_i():
    slab = lax.axis_index("slab")
    here = lax.axis_index("angle")
    chip = here // 2
    core = here % 2
    partner = here + 1 - 2 * core
    return slab, here, chip, core, partner


def _greet(slab, chip, core, partner, n_chip):
    barrier = pltpu.get_barrier_semaphore()
    pl.semaphore_signal(barrier, 1, device_id=(slab, partner), device_id_type=MESH_ID)
    for d in range(1, n_chip):
        peer = ((chip + d) % n_chip) * 2 + core
        pl.semaphore_signal(barrier, 1, device_id=(slab, peer), device_id_type=MESH_ID)
    pl.semaphore_wait(barrier, n_chip)


def _scatter_kernel(n_chip, with_extra, *refs):
    if with_extra:
        (part_ref, half_ref, extra_ref, out_ref, extra_out, got_pair, got_ring, chip_sum,
         send_a, recv_a, send_b, recv_b, extra_pair, extra_ring, extra_chip,
         send_c, recv_c) = refs
    else:
        (part_ref, half_ref, out_ref, got_pair, got_ring, chip_sum,
         send_a, recv_a, send_b, recv_b) = refs
    slab, here, chip, core, partner = _where_am_i()
    _greet(slab, chip, core, partner, n_chip)
    if with_extra:
        extra_copy = pltpu.make_async_remote_copy(
            src_ref=extra_ref,
            dst_ref=extra_pair,
            send_sem=send_c.at[0],
            recv_sem=recv_c.at[0],
            device_id=(slab, partner),
            device_id_type=MESH_ID,
        )
        extra_copy.start()
    order = list(range(1, n_chip)) + [0]
    pair = []
    for i, d in enumerate(order):
        dest = (chip + d) % n_chip
        copy = pltpu.make_async_remote_copy(
            src_ref=half_ref.at[2 * dest + 1 - core],
            dst_ref=got_pair.at[i],
            send_sem=send_a.at[i],
            recv_sem=recv_a.at[i],
            device_id=(slab, partner),
            device_id_type=MESH_ID,
        )
        copy.start()
        pair.append(copy)
    extra_sends = []
    if with_extra:
        extra_copy.wait()
        extra_chip[...] = extra_ref[...] + extra_pair[...]
        for d in range(1, n_chip):
            dest = (chip + d) % n_chip
            copy = pltpu.make_async_remote_copy(
                src_ref=extra_chip,
                dst_ref=extra_ring.at[d],
                send_sem=send_c.at[d],
                recv_sem=recv_c.at[d],
                device_id=(slab, 2 * dest + core),
                device_id_type=MESH_ID,
            )
            copy.start()
            extra_sends.append(copy)
    ring = []
    for i, d in enumerate(order[:-1]):
        dest = (chip + d) % n_chip
        pair[i].wait_recv()
        chip_sum[i] = (
            part_ref[2 * dest + core] + got_pair[i].astype(jnp.float32)
        ).astype(chip_sum.dtype)
        copy = pltpu.make_async_remote_copy(
            src_ref=chip_sum.at[i],
            dst_ref=got_ring.at[d],
            send_sem=send_b.at[d],
            recv_sem=recv_b.at[d],
            device_id=(slab, 2 * dest + core),
            device_id_type=MESH_ID,
        )
        copy.start()
        ring.append(copy)
    pair[-1].wait_recv()
    total = part_ref[here] + got_pair[n_chip - 1].astype(jnp.float32)
    for copy in pair:
        copy.wait_send()
    for copy in ring:
        copy.wait()
    for d in range(1, n_chip):
        total = total + got_ring[d].astype(jnp.float32)
    out_ref[...] = total
    if with_extra:
        for copy in extra_sends:
            copy.wait()
        extra_total = extra_chip[...]
        for d in range(1, n_chip):
            extra_total = extra_total + extra_ring[d]
        extra_out[...] = extra_total


def scatter_angle(part, extra=None):
    blocks, rows, cols = part.shape
    n_chip = blocks // 2
    link = part.dtype
    with_extra = extra is not None
    scratch = [
        pltpu.VMEM((n_chip, rows, cols), link),
        pltpu.VMEM((n_chip, rows, cols), link),
        pltpu.VMEM((n_chip, rows, cols), link),
        pltpu.SemaphoreType.DMA((n_chip,)),
        pltpu.SemaphoreType.DMA((n_chip,)),
        pltpu.SemaphoreType.DMA((n_chip,)),
        pltpu.SemaphoreType.DMA((n_chip,)),
    ]
    operands = [part, part.astype(link)]
    out_shape = [jax.ShapeDtypeStruct((rows, cols), jnp.float32)]
    if with_extra:
        scratch += [
            pltpu.VMEM(extra.shape, extra.dtype),
            pltpu.VMEM((n_chip,) + extra.shape, extra.dtype),
            pltpu.VMEM(extra.shape, extra.dtype),
            pltpu.SemaphoreType.DMA((n_chip,)),
            pltpu.SemaphoreType.DMA((n_chip,)),
        ]
        operands.append(extra)
        out_shape.append(jax.ShapeDtypeStruct(extra.shape, extra.dtype))
    result = pl.pallas_call(
        functools.partial(_scatter_kernel, n_chip, with_extra),
        out_shape=tuple(out_shape),
        in_specs=[pl.BlockSpec(memory_space=pltpu.VMEM)] * len(operands),
        out_specs=tuple(pl.BlockSpec(memory_space=pltpu.VMEM) for _ in out_shape),
        scratch_shapes=scratch,
        compiler_params=pltpu.CompilerParams(
            collective_id=5 if with_extra else 0, has_side_effects=True
        ),
        cost_estimate=pl.CostEstimate(
            flops=2 * blocks * rows * cols, bytes_accessed=4 * 3 * blocks * rows * cols,
            transcendentals=0,
        ),
    )(*operands)
    return result if with_extra else result[0]


def _sum_kernel(groups, part_ref, out_ref, got, send_sem, recv_sem):
    slab = lax.axis_index("slab")
    here = lax.axis_index("angle")
    barrier = pltpu.get_barrier_semaphore()
    for d in range(1, groups):
        peer = (here + d) % groups
        pl.semaphore_signal(barrier, 1, device_id=(slab, peer), device_id_type=MESH_ID)
    pl.semaphore_wait(barrier, groups - 1)
    copies = []
    for d in range(1, groups):
        copy = pltpu.make_async_remote_copy(
            src_ref=part_ref,
            dst_ref=got.at[d],
            send_sem=send_sem.at[d],
            recv_sem=recv_sem.at[d],
            device_id=(slab, (here + d) % groups),
            device_id_type=MESH_ID,
        )
        copy.start()
        copies.append(copy)
    total = part_ref[...]
    for copy in copies:
        copy.wait()
    for d in range(1, groups):
        total = total + got[d]
    out_ref[...] = total


def sum_angle(part, groups):
    return pl.pallas_call(
        functools.partial(_sum_kernel, groups),
        out_shape=jax.ShapeDtypeStruct(part.shape, part.dtype),
        in_specs=[pl.BlockSpec(memory_space=pltpu.VMEM)],
        out_specs=pl.BlockSpec(memory_space=pltpu.VMEM),
        scratch_shapes=[
            pltpu.VMEM((groups,) + part.shape, part.dtype),
            pltpu.SemaphoreType.DMA((groups,)),
            pltpu.SemaphoreType.DMA((groups,)),
        ],
        compiler_params=pltpu.CompilerParams(collective_id=2, has_side_effects=True),
        cost_estimate=pl.CostEstimate(
            flops=groups * part.size, bytes_accessed=4 * 2 * groups * part.size,
            transcendentals=0,
        ),
    )(part)


def _gather_kernel(n_chip, own_ref, out_ref, held, send_a, recv_a, send_b, recv_b, local_sem):
    slab, here, chip, core, partner = _where_am_i()
    _greet(slab, chip, core, partner, n_chip)
    mine = pltpu.make_async_copy(own_ref, held.at[here], local_sem.at[0])
    mine.start()
    pair = [
        pltpu.make_async_remote_copy(
            src_ref=own_ref,
            dst_ref=held.at[here],
            send_sem=send_b.at[0],
            recv_sem=recv_b.at[0],
            device_id=(slab, partner),
            device_id_type=MESH_ID,
        )
    ]
    pair[0].start()
    ring = [None]
    for d in range(1, n_chip):
        dest = (chip + d) % n_chip
        copy = pltpu.make_async_remote_copy(
            src_ref=own_ref,
            dst_ref=held.at[here],
            send_sem=send_a.at[d],
            recv_sem=recv_a.at[d],
            device_id=(slab, 2 * dest + core),
            device_id_type=MESH_ID,
        )
        copy.start()
        ring.append(copy)
    for d in range(1, n_chip):
        ring[d].wait_recv()
        block = 2 * ((chip - d + n_chip) % n_chip) + core
        copy = pltpu.make_async_remote_copy(
            src_ref=held.at[block],
            dst_ref=held.at[block],
            send_sem=send_b.at[d],
            recv_sem=recv_b.at[d],
            device_id=(slab, partner),
            device_id_type=MESH_ID,
        )
        copy.start()
        pair.append(copy)
    mine.wait()
    for d in range(1, n_chip):
        ring[d].wait_send()
    for copy in pair:
        copy.wait()
    out_ref[...] = held[...]


def gather_angle(own, groups):
    rows, cols = own.shape
    n_chip = groups // 2
    return pl.pallas_call(
        functools.partial(_gather_kernel, n_chip),
        out_shape=jax.ShapeDtypeStruct((groups, rows, cols), own.dtype),
        in_specs=[pl.BlockSpec(memory_space=pltpu.VMEM)],
        out_specs=pl.BlockSpec(memory_space=pltpu.VMEM),
        scratch_shapes=[
            pltpu.VMEM((groups, rows, cols), own.dtype),
            pltpu.SemaphoreType.DMA((n_chip,)),
            pltpu.SemaphoreType.DMA((n_chip,)),
            pltpu.SemaphoreType.DMA((n_chip,)),
            pltpu.SemaphoreType.DMA((n_chip,)),
            pltpu.SemaphoreType.DMA((1,)),
        ],
        compiler_params=pltpu.CompilerParams(collective_id=1, has_side_effects=True),
        cost_estimate=pl.CostEstimate(
            flops=0, bytes_accessed=2 * 2 * groups * rows * cols, transcendentals=0,
        ),
    )(own)


def smooth_share(
    volume,
    weight_z,
    weight_y,
    weight_x,
    lower_rim,
    left_rim,
    z_first,
    z_total,
    x_first,
    x_total,
):
    upper_halo = from_behind(volume[:, 0], "slab", -1)
    lower_halo = from_behind(volume[:, -1], "slab", 1)
    right_halo = from_behind(volume[0], "angle", -1)
    left_halo = from_behind(volume[-1], "angle", 1)
    upper = jnp.concatenate([volume[:, 1:], upper_halo[:, None]], axis=1)
    inside = (z_first + lax.broadcasted_iota(jnp.int32, volume.shape, 1) + 1 < z_total).astype(
        jnp.float32
    )
    face_flux = weight_z * limiter(upper - volume) * inside
    lower_flux = lower_rim * limiter(volume[:, 0] - lower_halo)
    previous = jnp.concatenate([lower_flux[:, None], face_flux[:, :-1]], axis=1)
    change = face_flux - previous
    following = jnp.concatenate([volume[:, :, 1:], jnp.zeros_like(volume[:, :, :1])], axis=2)
    inside = (lax.broadcasted_iota(jnp.int32, volume.shape, 2) < volume.shape[2] - 1).astype(
        jnp.float32
    )
    face_flux = weight_y * limiter(following - volume) * inside
    previous = jnp.concatenate([jnp.zeros_like(face_flux[:, :, :1]), face_flux[:, :, :-1]], axis=2)
    change = change + face_flux - previous
    following = jnp.concatenate([volume[1:], right_halo[None]], axis=0)
    inside = (x_first + lax.broadcasted_iota(jnp.int32, volume.shape, 0) + 1 < x_total).astype(
        jnp.float32
    )
    face_flux = weight_x * limiter(following - volume) * inside
    lower_flux = left_rim * limiter(volume[0] - left_halo)
    previous = jnp.concatenate([lower_flux[None], face_flux[:-1]], axis=0)
    change = change + face_flux - previous
    return volume + SMOOTH_RATE * change


def shards(volume0, weights, tile_block, tile_count, owner, sino, weight_z, weight_y, weight_x):
    tiles = weights[0, 0]
    slot_count, ray_count, voxels = tiles.shape
    slab_depth, height, column_count = volume0.shape
    blocks = tile_block[0, 0]
    live_count = tile_count[0, 0]
    owner_row = owner[0]
    live_slots = jnp.arange(slot_count, dtype=jnp.int32) < live_count
    select = (owner_row[None, :] == blocks[:, None]) & live_slots[:, None]
    slab_pos = lax.axis_index("slab")
    holder_ids = jnp.arange(owner_row.shape[0], dtype=jnp.int32)
    target = jnp.sum(jnp.where(select, holder_ids[None, :], 0), axis=1)
    distance_ids = jnp.arange(slot_count, dtype=jnp.int32)
    relative = ((target - slab_pos)[:, None] == distance_ids[None, :]) & live_slots[:, None]
    relative_float = relative.astype(jnp.float32)
    far_relative = relative[1:, 1:].astype(jnp.bfloat16)
    flat_tiles = tiles.reshape(slot_count * ray_count, voxels)
    ray_local = jnp.dot(
        flat_tiles, jnp.ones((voxels,), jnp.bfloat16), preferred_element_type=jnp.float32
    )
    ray_sends = jnp.einsum("td,tr->dr", relative_float, ray_local.reshape(slot_count, ray_count))
    ray_total = ray_sends[0]
    for distance in range(1, slot_count):
        ray_total = ray_total + from_behind(ray_sends[distance], "slab", distance)
    live_rows = jnp.repeat(live_slots, ray_count).astype(jnp.bfloat16)
    voxel_local = jnp.dot(live_rows, flat_tiles, preferred_element_type=jnp.float32)
    ray_scale = 1.0 / ray_total
    lower_all = from_behind(weight_z[slab_depth - 1], "slab", 1)
    z_first = slab_pos * slab_depth
    z_total = slab_depth * lax.axis_size("slab")
    groups = lax.axis_size("angle")
    share_width = column_count // groups
    angle_pos = lax.axis_index("angle")
    share_first = angle_pos * share_width

    def share_of(array):
        part = lax.dynamic_slice_in_dim(array, share_first, share_width, array.ndim - 1)
        return jnp.moveaxis(part, -1, 0).astype(jnp.float32)

    measured = sino[0, 0].astype(jnp.float32)
    volume = share_of(volume0)
    local_z = share_of(weight_z)
    local_y = share_of(weight_y)
    local_x = share_of(weight_x)
    lower_rim = share_of(lower_all)
    left_index = jnp.maximum(share_first - 1, 0)
    left_rim = lax.dynamic_index_in_dim(weight_x, left_index, 2, keepdims=False).astype(
        jnp.float32
    ) * (angle_pos > 0).astype(jnp.float32)
    gathered = None
    residual = jnp.zeros((ray_count, column_count), jnp.float32)
    for iteration in range(ITERS):
        if gathered is None:
            flat_volume = volume0.astype(jnp.bfloat16).reshape(voxels, column_count)
            far_products = jnp.einsum(
                "trv,vn->trn", tiles[1:], flat_volume, preferred_element_type=jnp.float32
            ).astype(jnp.bfloat16)
        else:
            far_products = jnp.einsum(
                "trv,nv->trn", tiles[1:], gathered, preferred_element_type=jnp.float32
            ).astype(jnp.bfloat16)
        sends_half = jnp.einsum(
            "td,trn->drn", far_relative, far_products, preferred_element_type=jnp.float32
        ).astype(jnp.bfloat16)
        arrived = [
            from_behind(sends_half[distance - 1], "slab", distance)
            for distance in range(1, slot_count)
        ]
        if gathered is None:
            near_products = jnp.einsum(
                "rv,vn->rn", tiles[0], flat_volume, preferred_element_type=jnp.float32
            )
        else:
            near_products = jnp.einsum(
                "rv,nv->rn", tiles[0], gathered, preferred_element_type=jnp.float32
            )
        near_products = lax.optimization_barrier(near_products.astype(jnp.bfloat16))
        projected = near_products.astype(jnp.float32)
        for distance in range(1, slot_count):
            projected = projected + arrived[distance - 1].astype(jnp.float32)
        residual = (measured - projected) * ray_scale[:, None]
        residual_half = residual.astype(jnp.bfloat16)
        nearby = [
            from_behind(residual_half, "slab", -distance) for distance in range(1, slot_count)
        ]
        near_back = lax.optimization_barrier(
            jnp.einsum("rn,rv->nv", residual_half, tiles[0], preferred_element_type=jnp.float32)
        )
        picked = jnp.einsum(
            "td,drn->trn", far_relative, jnp.stack(nearby), preferred_element_type=jnp.float32
        ).astype(jnp.bfloat16)
        back_t = near_back + jnp.einsum(
            "trn,trv->nv", picked, tiles[1:], preferred_element_type=jnp.float32
        )
        if iteration == 0:
            back_own, voxel_total = scatter_angle(
                back_t.reshape(groups, share_width, voxels),
                voxel_local.reshape(slab_depth, height),
            )
            voxel_scale = (1.0 / voxel_total).reshape(1, slab_depth, height)
        else:
            back_own = scatter_angle(back_t.reshape(groups, share_width, voxels))
        volume = volume + voxel_scale * back_own.reshape(share_width, slab_depth, height)
        volume = smooth_share(
            volume,
            local_z,
            local_y,
            local_x,
            lower_rim,
            left_rim,
            z_first,
            z_total,
            share_first,
            column_count,
        )
        if iteration + 1 < ITERS:
            own_half = volume.astype(jnp.bfloat16).reshape(share_width, voxels)
            gathered = gather_angle(own_half, groups).reshape(column_count, voxels)
    volume_out = jnp.moveaxis(volume, 0, -1)
    return (volume_out, residual[None, None])


def solution(mesh):
    in_specs = (
        P("slab", None, None),
        P("slab", "angle", None, None, None),
        P("slab", "angle", None),
        P("slab", "angle"),
        P("angle", None),
        P("angle", "slab", None, None),
        P("slab", None, None),
        P("slab", None, None),
        P("slab", None, None),
    )
    out_specs = (P("slab", None, "angle"), P("angle", "slab", None, None))
    return jax.shard_map(shards, mesh=mesh, in_specs=in_specs, out_specs=out_specs, check_vma=False)
```

```python
import functools

import jax
import jax.numpy as jnp
from jax import lax
from jax.experimental import pallas as pl
from jax.experimental.pallas import tpu as pltpu
from jax.sharding import PartitionSpec as P

ITERS = 3


SMOOTH_EPS = 0.01
SMOOTH_RATE = 0.15

MESH_ID = pl.DeviceIdType.MESH


def from_behind(value, axis, steps):
    count = lax.axis_size(axis)
    first, last = (max(0, -steps), min(count, count - steps))
    return lax.ppermute(value, axis, [(source, source + steps) for source in range(first, last)])


def limiter(difference):
    return difference / jnp.sqrt(difference * difference + SMOOTH_EPS)


def _where_am_i():
    slab = lax.axis_index("slab")
    here = lax.axis_index("angle")
    chip = here // 2
    core = here % 2
    partner = here + 1 - 2 * core
    return slab, here, chip, core, partner


def _greet(slab, chip, core, partner, n_chip):
    barrier = pltpu.get_barrier_semaphore()
    pl.semaphore_signal(barrier, 1, device_id=(slab, partner), device_id_type=MESH_ID)
    for d in range(1, n_chip):
        peer = ((chip + d) % n_chip) * 2 + core
        pl.semaphore_signal(barrier, 1, device_id=(slab, peer), device_id_type=MESH_ID)
    pl.semaphore_wait(barrier, n_chip)


def _scatter_kernel(n_chip, with_extra, *refs):
    if with_extra:
        (part_ref, half_ref, extra_ref, out_ref, extra_out, got_pair, got_ring, chip_sum,
         send_a, recv_a, send_b, recv_b, extra_pair, extra_ring, extra_chip,
         send_c, recv_c) = refs
    else:
        (part_ref, half_ref, out_ref, got_pair, got_ring, chip_sum,
         send_a, recv_a, send_b, recv_b) = refs
    slab, here, chip, core, partner = _where_am_i()
    _greet(slab, chip, core, partner, n_chip)
    if with_extra:
        extra_copy = pltpu.make_async_remote_copy(
            src_ref=extra_ref,
            dst_ref=extra_pair,
            send_sem=send_c.at[0],
            recv_sem=recv_c.at[0],
            device_id=(slab, partner),
            device_id_type=MESH_ID,
        )
        extra_copy.start()
    order = list(range(1, n_chip)) + [0]
    pair = []
    for i, d in enumerate(order):
        dest = (chip + d) % n_chip
        copy = pltpu.make_async_remote_copy(
            src_ref=half_ref.at[2 * dest + 1 - core],
            dst_ref=got_pair.at[i],
            send_sem=send_a.at[i],
            recv_sem=recv_a.at[i],
            device_id=(slab, partner),
            device_id_type=MESH_ID,
        )
        copy.start()
        pair.append(copy)
    extra_sends = []
    if with_extra:
        extra_copy.wait()
        extra_chip[...] = extra_ref[...] + extra_pair[...]
        for d in range(1, n_chip):
            dest = (chip + d) % n_chip
            copy = pltpu.make_async_remote_copy(
                src_ref=extra_chip,
                dst_ref=extra_ring.at[d],
                send_sem=send_c.at[d],
                recv_sem=recv_c.at[d],
                device_id=(slab, 2 * dest + core),
                device_id_type=MESH_ID,
            )
            copy.start()
            extra_sends.append(copy)
    ring = []
    for i, d in enumerate(order[:-1]):
        dest = (chip + d) % n_chip
        pair[i].wait_recv()
        chip_sum[i] = (
            part_ref[2 * dest + core] + got_pair[i].astype(jnp.float32)
        ).astype(chip_sum.dtype)
        copy = pltpu.make_async_remote_copy(
            src_ref=chip_sum.at[i],
            dst_ref=got_ring.at[d],
            send_sem=send_b.at[d],
            recv_sem=recv_b.at[d],
            device_id=(slab, 2 * dest + core),
            device_id_type=MESH_ID,
        )
        copy.start()
        ring.append(copy)
    pair[-1].wait_recv()
    total = part_ref[here] + got_pair[n_chip - 1].astype(jnp.float32)
    for copy in pair:
        copy.wait_send()
    for copy in ring:
        copy.wait()
    for d in range(1, n_chip):
        total = total + got_ring[d].astype(jnp.float32)
    out_ref[...] = total
    if with_extra:
        for copy in extra_sends:
            copy.wait()
        extra_total = extra_chip[...]
        for d in range(1, n_chip):
            extra_total = extra_total + extra_ring[d]
        extra_out[...] = extra_total


def scatter_angle(part, extra=None):
    blocks, rows, cols = part.shape
    n_chip = blocks // 2
    link = part.dtype
    with_extra = extra is not None
    scratch = [
        pltpu.VMEM((n_chip, rows, cols), link),
        pltpu.VMEM((n_chip, rows, cols), link),
        pltpu.VMEM((n_chip, rows, cols), link),
        pltpu.SemaphoreType.DMA((n_chip,)),
        pltpu.SemaphoreType.DMA((n_chip,)),
        pltpu.SemaphoreType.DMA((n_chip,)),
        pltpu.SemaphoreType.DMA((n_chip,)),
    ]
    operands = [part, part.astype(link)]
    out_shape = [jax.ShapeDtypeStruct((rows, cols), jnp.float32)]
    if with_extra:
        scratch += [
            pltpu.VMEM(extra.shape, extra.dtype),
            pltpu.VMEM((n_chip,) + extra.shape, extra.dtype),
            pltpu.VMEM(extra.shape, extra.dtype),
            pltpu.SemaphoreType.DMA((n_chip,)),
            pltpu.SemaphoreType.DMA((n_chip,)),
        ]
        operands.append(extra)
        out_shape.append(jax.ShapeDtypeStruct(extra.shape, extra.dtype))
    result = pl.pallas_call(
        functools.partial(_scatter_kernel, n_chip, with_extra),
        out_shape=tuple(out_shape),
        in_specs=[pl.BlockSpec(memory_space=pltpu.VMEM)] * len(operands),
        out_specs=tuple(pl.BlockSpec(memory_space=pltpu.VMEM) for _ in out_shape),
        scratch_shapes=scratch,
        compiler_params=pltpu.CompilerParams(
            collective_id=5 if with_extra else 0, has_side_effects=True
        ),
        cost_estimate=pl.CostEstimate(
            flops=2 * blocks * rows * cols, bytes_accessed=4 * 3 * blocks * rows * cols,
            transcendentals=0,
        ),
    )(*operands)
    return result if with_extra else result[0]


def _sum_kernel(groups, part_ref, out_ref, got, send_sem, recv_sem):
    slab = lax.axis_index("slab")
    here = lax.axis_index("angle")
    barrier = pltpu.get_barrier_semaphore()
    for d in range(1, groups):
        peer = (here + d) % groups
        pl.semaphore_signal(barrier, 1, device_id=(slab, peer), device_id_type=MESH_ID)
    pl.semaphore_wait(barrier, groups - 1)
    copies = []
    for d in range(1, groups):
        copy = pltpu.make_async_remote_copy(
            src_ref=part_ref,
            dst_ref=got.at[d],
            send_sem=send_sem.at[d],
            recv_sem=recv_sem.at[d],
            device_id=(slab, (here + d) % groups),
            device_id_type=MESH_ID,
        )
        copy.start()
        copies.append(copy)
    total = part_ref[...]
    for copy in copies:
        copy.wait()
    for d in range(1, groups):
        total = total + got[d]
    out_ref[...] = total


def sum_angle(part, groups):
    return pl.pallas_call(
        functools.partial(_sum_kernel, groups),
        out_shape=jax.ShapeDtypeStruct(part.shape, part.dtype),
        in_specs=[pl.BlockSpec(memory_space=pltpu.VMEM)],
        out_specs=pl.BlockSpec(memory_space=pltpu.VMEM),
        scratch_shapes=[
            pltpu.VMEM((groups,) + part.shape, part.dtype),
            pltpu.SemaphoreType.DMA((groups,)),
            pltpu.SemaphoreType.DMA((groups,)),
        ],
        compiler_params=pltpu.CompilerParams(collective_id=2, has_side_effects=True),
        cost_estimate=pl.CostEstimate(
            flops=groups * part.size, bytes_accessed=4 * 2 * groups * part.size,
            transcendentals=0,
        ),
    )(part)


def _gather_kernel(n_chip, own_ref, out_ref, held, send_a, recv_a, send_b, recv_b, local_sem):
    slab, here, chip, core, partner = _where_am_i()
    _greet(slab, chip, core, partner, n_chip)
    mine = pltpu.make_async_copy(own_ref, held.at[here], local_sem.at[0])
    mine.start()
    pair = [
        pltpu.make_async_remote_copy(
            src_ref=own_ref,
            dst_ref=held.at[here],
            send_sem=send_b.at[0],
            recv_sem=recv_b.at[0],
            device_id=(slab, partner),
            device_id_type=MESH_ID,
        )
    ]
    pair[0].start()
    ring = [None]
    for d in range(1, n_chip):
        dest = (chip + d) % n_chip
        copy = pltpu.make_async_remote_copy(
            src_ref=own_ref,
            dst_ref=held.at[here],
            send_sem=send_a.at[d],
            recv_sem=recv_a.at[d],
            device_id=(slab, 2 * dest + core),
            device_id_type=MESH_ID,
        )
        copy.start()
        ring.append(copy)
    for d in range(1, n_chip):
        ring[d].wait_recv()
        block = 2 * ((chip - d + n_chip) % n_chip) + core
        copy = pltpu.make_async_remote_copy(
            src_ref=held.at[block],
            dst_ref=held.at[block],
            send_sem=send_b.at[d],
            recv_sem=recv_b.at[d],
            device_id=(slab, partner),
            device_id_type=MESH_ID,
        )
        copy.start()
        pair.append(copy)
    mine.wait()
    for d in range(1, n_chip):
        ring[d].wait_send()
    for copy in pair:
        copy.wait()
    out_ref[...] = held[...]


def gather_angle(own, groups):
    rows, cols = own.shape
    n_chip = groups // 2
    return pl.pallas_call(
        functools.partial(_gather_kernel, n_chip),
        out_shape=jax.ShapeDtypeStruct((groups, rows, cols), own.dtype),
        in_specs=[pl.BlockSpec(memory_space=pltpu.VMEM)],
        out_specs=pl.BlockSpec(memory_space=pltpu.VMEM),
        scratch_shapes=[
            pltpu.VMEM((groups, rows, cols), own.dtype),
            pltpu.SemaphoreType.DMA((n_chip,)),
            pltpu.SemaphoreType.DMA((n_chip,)),
            pltpu.SemaphoreType.DMA((n_chip,)),
            pltpu.SemaphoreType.DMA((n_chip,)),
            pltpu.SemaphoreType.DMA((1,)),
        ],
        compiler_params=pltpu.CompilerParams(collective_id=1, has_side_effects=True),
        cost_estimate=pl.CostEstimate(
            flops=0, bytes_accessed=2 * 2 * groups * rows * cols, transcendentals=0,
        ),
    )(own)


def smooth_share(
    volume,
    weight_z,
    weight_y,
    weight_x,
    lower_rim,
    left_rim,
    z_first,
    z_total,
    x_first,
    x_total,
):
    upper_halo = from_behind(volume[:, 0], "slab", -1)
    lower_halo = from_behind(volume[:, -1], "slab", 1)
    right_halo = from_behind(volume[0], "angle", -1)
    left_halo = from_behind(volume[-1], "angle", 1)
    upper = jnp.concatenate([volume[:, 1:], upper_halo[:, None]], axis=1)
    inside = (z_first + lax.broadcasted_iota(jnp.int32, volume.shape, 1) + 1 < z_total).astype(
        jnp.float32
    )
    face_flux = weight_z * limiter(upper - volume) * inside
    lower_flux = lower_rim * limiter(volume[:, 0] - lower_halo)
    previous = jnp.concatenate([lower_flux[:, None], face_flux[:, :-1]], axis=1)
    change = face_flux - previous
    following = jnp.concatenate([volume[:, :, 1:], jnp.zeros_like(volume[:, :, :1])], axis=2)
    inside = (lax.broadcasted_iota(jnp.int32, volume.shape, 2) < volume.shape[2] - 1).astype(
        jnp.float32
    )
    face_flux = weight_y * limiter(following - volume) * inside
    previous = jnp.concatenate([jnp.zeros_like(face_flux[:, :, :1]), face_flux[:, :, :-1]], axis=2)
    change = change + face_flux - previous
    following = jnp.concatenate([volume[1:], right_halo[None]], axis=0)
    inside = (x_first + lax.broadcasted_iota(jnp.int32, volume.shape, 0) + 1 < x_total).astype(
        jnp.float32
    )
    face_flux = weight_x * limiter(following - volume) * inside
    lower_flux = left_rim * limiter(volume[0] - left_halo)
    previous = jnp.concatenate([lower_flux[None], face_flux[:-1]], axis=0)
    change = change + face_flux - previous
    return volume + SMOOTH_RATE * change


def shards(volume0, weights, tile_block, tile_count, owner, sino, weight_z, weight_y, weight_x):
    tiles = weights[0, 0]
    slot_count, ray_count, voxels = tiles.shape
    slab_depth, height, column_count = volume0.shape
    blocks = tile_block[0, 0]
    live_count = tile_count[0, 0]
    owner_row = owner[0]
    live_slots = jnp.arange(slot_count, dtype=jnp.int32) < live_count
    select = (owner_row[None, :] == blocks[:, None]) & live_slots[:, None]
    slab_pos = lax.axis_index("slab")
    holder_ids = jnp.arange(owner_row.shape[0], dtype=jnp.int32)
    target = jnp.sum(jnp.where(select, holder_ids[None, :], 0), axis=1)
    distance_ids = jnp.arange(slot_count, dtype=jnp.int32)
    relative = ((target - slab_pos)[:, None] == distance_ids[None, :]) & live_slots[:, None]
    relative_float = relative.astype(jnp.float32)
    far_relative = relative[1:, 1:].astype(jnp.bfloat16)
    flat_tiles = tiles.reshape(slot_count * ray_count, voxels)
    ray_local = jnp.dot(
        flat_tiles, jnp.ones((voxels,), jnp.bfloat16), preferred_element_type=jnp.float32
    )
    ray_sends = jnp.einsum("td,tr->dr", relative_float, ray_local.reshape(slot_count, ray_count))
    ray_high = ray_sends.astype(jnp.bfloat16)
    ray_low = (ray_sends - ray_high.astype(jnp.float32)).astype(jnp.bfloat16)
    live_rows = jnp.repeat(live_slots, ray_count).astype(jnp.bfloat16)
    voxel_local = jnp.dot(live_rows, flat_tiles, preferred_element_type=jnp.float32)
    z_first = slab_pos * slab_depth
    z_total = slab_depth * lax.axis_size("slab")
    groups = lax.axis_size("angle")
    share_width = column_count // groups
    angle_pos = lax.axis_index("angle")
    share_first = angle_pos * share_width

    def share_of(array):
        part = lax.dynamic_slice_in_dim(array, share_first, share_width, array.ndim - 1)
        return jnp.moveaxis(part, -1, 0).astype(jnp.float32)

    measured = sino[0, 0].astype(jnp.float32)
    volume = share_of(volume0)
    local_z = share_of(weight_z)
    local_y = share_of(weight_y)
    local_x = share_of(weight_x)
    left_index = jnp.maximum(share_first - 1, 0)
    left_rim = lax.dynamic_index_in_dim(weight_x, left_index, 2, keepdims=False).astype(
        jnp.float32
    ) * (angle_pos > 0).astype(jnp.float32)
    gathered = None
    residual = jnp.zeros((ray_count, column_count), jnp.float32)
    for iteration in range(ITERS):
        if gathered is None:
            flat_volume = volume0.astype(jnp.bfloat16).reshape(voxels, column_count)
            far_products = jnp.einsum(
                "trv,vn->trn", tiles[1:], flat_volume, preferred_element_type=jnp.float32
            ).astype(jnp.bfloat16)
        else:
            far_products = jnp.einsum(
                "trv,nv->trn", tiles[1:], gathered, preferred_element_type=jnp.float32
            ).astype(jnp.bfloat16)
        sends_half = jnp.einsum(
            "td,trn->drn", far_relative, far_products, preferred_element_type=jnp.float32
        ).astype(jnp.bfloat16)
        if iteration == 0:
            lanes = sends_half.shape[2]
            arrived = []
            ray_total = ray_sends[0]
            for distance in range(1, slot_count):
                pieces = [
                    sends_half[distance - 1],
                    ray_high[distance].reshape(-1, lanes),
                    ray_low[distance].reshape(-1, lanes),
                ]
                if distance == 1:
                    pieces.append(weight_z[slab_depth - 1])
                payload = from_behind(jnp.concatenate(pieces, axis=0), "slab", distance)
                arrived.append(payload[:ray_count])
                ray_rows = ray_count // lanes
                ray_high_in = payload[ray_count:ray_count + ray_rows].reshape(ray_count)
                ray_low_in = payload[ray_count + ray_rows:ray_count + 2 * ray_rows].reshape(
                    ray_count
                )
                ray_total = ray_total + (
                    ray_high_in.astype(jnp.float32) + ray_low_in.astype(jnp.float32)
                )
                if distance == 1:
                    lower_all = payload[ray_count + 2 * ray_rows:]
            ray_scale = 1.0 / ray_total
            lower_rim = share_of(lower_all)
        else:
            arrived = [
                from_behind(sends_half[distance - 1], "slab", distance)
                for distance in range(1, slot_count)
            ]
        if gathered is None:
            near_products = jnp.einsum(
                "rv,vn->rn", tiles[0], flat_volume, preferred_element_type=jnp.float32
            )
        else:
            near_products = jnp.einsum(
                "rv,nv->rn", tiles[0], gathered, preferred_element_type=jnp.float32
            )
        near_products = lax.optimization_barrier(near_products.astype(jnp.bfloat16))
        projected = near_products.astype(jnp.float32)
        for distance in range(1, slot_count):
            projected = projected + arrived[distance - 1].astype(jnp.float32)
        residual = (measured - projected) * ray_scale[:, None]
        residual_half = residual.astype(jnp.bfloat16)
        nearby = [
            from_behind(residual_half, "slab", -distance) for distance in range(1, slot_count)
        ]
        near_back = lax.optimization_barrier(
            jnp.einsum("rn,rv->nv", residual_half, tiles[0], preferred_element_type=jnp.float32)
        )
        picked = jnp.einsum(
            "td,drn->trn", far_relative, jnp.stack(nearby), preferred_element_type=jnp.float32
        ).astype(jnp.bfloat16)
        back_t = near_back + jnp.einsum(
            "trn,trv->nv", picked, tiles[1:], preferred_element_type=jnp.float32
        )
        if iteration == 0:
            back_own, voxel_total = scatter_angle(
                back_t.reshape(groups, share_width, voxels),
                voxel_local.reshape(slab_depth, height),
            )
            voxel_scale = (1.0 / voxel_total).reshape(1, slab_depth, height)
        else:
            back_own = scatter_angle(back_t.reshape(groups, share_width, voxels))
        volume = volume + voxel_scale * back_own.reshape(share_width, slab_depth, height)
        volume = smooth_share(
            volume,
            local_z,
            local_y,
            local_x,
            lower_rim,
            left_rim,
            z_first,
            z_total,
            share_first,
            column_count,
        )
        if iteration + 1 < ITERS:
            own_half = volume.astype(jnp.bfloat16).reshape(share_width, voxels)
            gathered = gather_angle(own_half, groups).reshape(column_count, voxels)
    volume_out = jnp.moveaxis(volume, 0, -1)
    return (volume_out, residual[None, None])


def solution(mesh):
    in_specs = (
        P("slab", None, None),
        P("slab", "angle", None, None, None),
        P("slab", "angle", None),
        P("slab", "angle"),
        P("angle", None),
        P("angle", "slab", None, None),
        P("slab", None, None),
        P("slab", None, None),
        P("slab", None, None),
    )
    out_specs = (P("slab", None, "angle"), P("angle", "slab", None, None))
    return jax.shard_map(shards, mesh=mesh, in_specs=in_specs, out_specs=out_specs, check_vma=False)
```

```python
import functools

import jax
import jax.numpy as jnp
from jax import lax
from jax.experimental import pallas as pl
from jax.experimental.pallas import tpu as pltpu
from jax.sharding import PartitionSpec as P

ITERS = 3


SMOOTH_EPS = 0.01
SMOOTH_RATE = 0.15

MESH_ID = pl.DeviceIdType.MESH


def from_behind(value, axis, steps):
    count = lax.axis_size(axis)
    first, last = (max(0, -steps), min(count, count - steps))
    return lax.ppermute(value, axis, [(source, source + steps) for source in range(first, last)])


def limiter(difference):
    return difference / jnp.sqrt(difference * difference + SMOOTH_EPS)


def _where_am_i():
    slab = lax.axis_index("slab")
    here = lax.axis_index("angle")
    chip = here // 2
    core = here % 2
    partner = here + 1 - 2 * core
    return slab, here, chip, core, partner


def _greet(slab, chip, core, partner, n_chip):
    barrier = pltpu.get_barrier_semaphore()
    pl.semaphore_signal(barrier, 1, device_id=(slab, partner), device_id_type=MESH_ID)
    for d in range(1, n_chip):
        peer = ((chip + d) % n_chip) * 2 + core
        pl.semaphore_signal(barrier, 1, device_id=(slab, peer), device_id_type=MESH_ID)
    pl.semaphore_wait(barrier, n_chip)


def _scatter_kernel(n_chip, with_extra, *refs):
    if with_extra:
        (part_ref, half_ref, extra_ref, out_ref, extra_out, got_pair, got_ring, chip_sum,
         send_a, recv_a, send_b, recv_b, extra_pair, extra_ring, extra_chip,
         send_c, recv_c) = refs
    else:
        (part_ref, half_ref, out_ref, got_pair, got_ring, chip_sum,
         send_a, recv_a, send_b, recv_b) = refs
    slab, here, chip, core, partner = _where_am_i()
    _greet(slab, chip, core, partner, n_chip)
    if with_extra:
        extra_copy = pltpu.make_async_remote_copy(
            src_ref=extra_ref,
            dst_ref=extra_pair,
            send_sem=send_c.at[0],
            recv_sem=recv_c.at[0],
            device_id=(slab, partner),
            device_id_type=MESH_ID,
        )
        extra_copy.start()
    order = list(range(1, n_chip)) + [0]
    pair = []
    for i, d in enumerate(order):
        dest = (chip + d) % n_chip
        copy = pltpu.make_async_remote_copy(
            src_ref=half_ref.at[2 * dest + 1 - core],
            dst_ref=got_pair.at[i],
            send_sem=send_a.at[i],
            recv_sem=recv_a.at[i],
            device_id=(slab, partner),
            device_id_type=MESH_ID,
        )
        copy.start()
        pair.append(copy)
    extra_sends = []
    if with_extra:
        extra_copy.wait()
        extra_chip[...] = extra_ref[...] + extra_pair[...]
        for d in range(1, n_chip):
            dest = (chip + d) % n_chip
            copy = pltpu.make_async_remote_copy(
                src_ref=extra_chip,
                dst_ref=extra_ring.at[d],
                send_sem=send_c.at[d],
                recv_sem=recv_c.at[d],
                device_id=(slab, 2 * dest + core),
                device_id_type=MESH_ID,
            )
            copy.start()
            extra_sends.append(copy)
    ring = []
    for i, d in enumerate(order[:-1]):
        dest = (chip + d) % n_chip
        pair[i].wait_recv()
        chip_sum[i] = (
            part_ref[2 * dest + core] + got_pair[i].astype(jnp.float32)
        ).astype(chip_sum.dtype)
        copy = pltpu.make_async_remote_copy(
            src_ref=chip_sum.at[i],
            dst_ref=got_ring.at[d],
            send_sem=send_b.at[d],
            recv_sem=recv_b.at[d],
            device_id=(slab, 2 * dest + core),
            device_id_type=MESH_ID,
        )
        copy.start()
        ring.append(copy)
    pair[-1].wait_recv()
    total = part_ref[here] + got_pair[n_chip - 1].astype(jnp.float32)
    for copy in pair:
        copy.wait_send()
    for copy in ring:
        copy.wait()
    for d in range(1, n_chip):
        total = total + got_ring[d].astype(jnp.float32)
    out_ref[...] = total
    if with_extra:
        for copy in extra_sends:
            copy.wait()
        extra_total = extra_chip[...]
        for d in range(1, n_chip):
            extra_total = extra_total + extra_ring[d]
        extra_out[...] = extra_total


def scatter_angle(part, extra=None):
    blocks, rows, cols = part.shape
    n_chip = blocks // 2
    link = part.dtype
    with_extra = extra is not None
    scratch = [
        pltpu.VMEM((n_chip, rows, cols), link),
        pltpu.VMEM((n_chip, rows, cols), link),
        pltpu.VMEM((n_chip, rows, cols), link),
        pltpu.SemaphoreType.DMA((n_chip,)),
        pltpu.SemaphoreType.DMA((n_chip,)),
        pltpu.SemaphoreType.DMA((n_chip,)),
        pltpu.SemaphoreType.DMA((n_chip,)),
    ]
    operands = [part, part.astype(link)]
    out_shape = [jax.ShapeDtypeStruct((rows, cols), jnp.float32)]
    if with_extra:
        scratch += [
            pltpu.VMEM(extra.shape, extra.dtype),
            pltpu.VMEM((n_chip,) + extra.shape, extra.dtype),
            pltpu.VMEM(extra.shape, extra.dtype),
            pltpu.SemaphoreType.DMA((n_chip,)),
            pltpu.SemaphoreType.DMA((n_chip,)),
        ]
        operands.append(extra)
        out_shape.append(jax.ShapeDtypeStruct(extra.shape, extra.dtype))
    result = pl.pallas_call(
        functools.partial(_scatter_kernel, n_chip, with_extra),
        out_shape=tuple(out_shape),
        in_specs=[pl.BlockSpec(memory_space=pltpu.VMEM)] * len(operands),
        out_specs=tuple(pl.BlockSpec(memory_space=pltpu.VMEM) for _ in out_shape),
        scratch_shapes=scratch,
        compiler_params=pltpu.CompilerParams(
            collective_id=5 if with_extra else 0, has_side_effects=True
        ),
        cost_estimate=pl.CostEstimate(
            flops=2 * blocks * rows * cols, bytes_accessed=4 * 3 * blocks * rows * cols,
            transcendentals=0,
        ),
    )(*operands)
    return result if with_extra else result[0]


def _sum_kernel(groups, part_ref, out_ref, got, send_sem, recv_sem):
    slab = lax.axis_index("slab")
    here = lax.axis_index("angle")
    barrier = pltpu.get_barrier_semaphore()
    for d in range(1, groups):
        peer = (here + d) % groups
        pl.semaphore_signal(barrier, 1, device_id=(slab, peer), device_id_type=MESH_ID)
    pl.semaphore_wait(barrier, groups - 1)
    copies = []
    for d in range(1, groups):
        copy = pltpu.make_async_remote_copy(
            src_ref=part_ref,
            dst_ref=got.at[d],
            send_sem=send_sem.at[d],
            recv_sem=recv_sem.at[d],
            device_id=(slab, (here + d) % groups),
            device_id_type=MESH_ID,
        )
        copy.start()
        copies.append(copy)
    total = part_ref[...]
    for copy in copies:
        copy.wait()
    for d in range(1, groups):
        total = total + got[d]
    out_ref[...] = total


def sum_angle(part, groups):
    return pl.pallas_call(
        functools.partial(_sum_kernel, groups),
        out_shape=jax.ShapeDtypeStruct(part.shape, part.dtype),
        in_specs=[pl.BlockSpec(memory_space=pltpu.VMEM)],
        out_specs=pl.BlockSpec(memory_space=pltpu.VMEM),
        scratch_shapes=[
            pltpu.VMEM((groups,) + part.shape, part.dtype),
            pltpu.SemaphoreType.DMA((groups,)),
            pltpu.SemaphoreType.DMA((groups,)),
        ],
        compiler_params=pltpu.CompilerParams(collective_id=2, has_side_effects=True),
        cost_estimate=pl.CostEstimate(
            flops=groups * part.size, bytes_accessed=4 * 2 * groups * part.size,
            transcendentals=0,
        ),
    )(part)


def _gather_kernel(n_chip, own_ref, out_ref, held, send_a, recv_a, send_b, recv_b, local_sem):
    slab, here, chip, core, partner = _where_am_i()
    _greet(slab, chip, core, partner, n_chip)
    mine = pltpu.make_async_copy(own_ref, held.at[here], local_sem.at[0])
    mine.start()
    pair = [
        pltpu.make_async_remote_copy(
            src_ref=own_ref,
            dst_ref=held.at[here],
            send_sem=send_b.at[0],
            recv_sem=recv_b.at[0],
            device_id=(slab, partner),
            device_id_type=MESH_ID,
        )
    ]
    pair[0].start()
    ring = [None]
    for d in range(1, n_chip):
        dest = (chip + d) % n_chip
        copy = pltpu.make_async_remote_copy(
            src_ref=own_ref,
            dst_ref=held.at[here],
            send_sem=send_a.at[d],
            recv_sem=recv_a.at[d],
            device_id=(slab, 2 * dest + core),
            device_id_type=MESH_ID,
        )
        copy.start()
        ring.append(copy)
    for d in range(1, n_chip):
        ring[d].wait_recv()
        block = 2 * ((chip - d + n_chip) % n_chip) + core
        copy = pltpu.make_async_remote_copy(
            src_ref=held.at[block],
            dst_ref=held.at[block],
            send_sem=send_b.at[d],
            recv_sem=recv_b.at[d],
            device_id=(slab, partner),
            device_id_type=MESH_ID,
        )
        copy.start()
        pair.append(copy)
    mine.wait()
    for d in range(1, n_chip):
        ring[d].wait_send()
    for copy in pair:
        copy.wait()
    out_ref[...] = held[...]


def gather_angle(own, groups):
    rows, cols = own.shape
    n_chip = groups // 2
    return pl.pallas_call(
        functools.partial(_gather_kernel, n_chip),
        out_shape=jax.ShapeDtypeStruct((groups, rows, cols), own.dtype),
        in_specs=[pl.BlockSpec(memory_space=pltpu.VMEM)],
        out_specs=pl.BlockSpec(memory_space=pltpu.VMEM),
        scratch_shapes=[
            pltpu.VMEM((groups, rows, cols), own.dtype),
            pltpu.SemaphoreType.DMA((n_chip,)),
            pltpu.SemaphoreType.DMA((n_chip,)),
            pltpu.SemaphoreType.DMA((n_chip,)),
            pltpu.SemaphoreType.DMA((n_chip,)),
            pltpu.SemaphoreType.DMA((1,)),
        ],
        compiler_params=pltpu.CompilerParams(collective_id=1, has_side_effects=True),
        cost_estimate=pl.CostEstimate(
            flops=0, bytes_accessed=2 * 2 * groups * rows * cols, transcendentals=0,
        ),
    )(own)


def smooth_share(
    volume,
    weight_z,
    weight_y,
    weight_x,
    lower_rim,
    left_rim,
    z_first,
    z_total,
    x_first,
    x_total,
):
    upper_halo = from_behind(volume[:, 0], "slab", -1)
    lower_halo = from_behind(volume[:, -1], "slab", 1)
    right_halo = from_behind(volume[0], "angle", -1)
    left_halo = from_behind(volume[-1], "angle", 1)
    upper = jnp.concatenate([volume[:, 1:], upper_halo[:, None]], axis=1)
    inside = (z_first + lax.broadcasted_iota(jnp.int32, volume.shape, 1) + 1 < z_total).astype(
        jnp.float32
    )
    face_flux = weight_z * limiter(upper - volume) * inside
    lower_flux = lower_rim * limiter(volume[:, 0] - lower_halo)
    previous = jnp.concatenate([lower_flux[:, None], face_flux[:, :-1]], axis=1)
    change = face_flux - previous
    following = jnp.concatenate([volume[:, :, 1:], jnp.zeros_like(volume[:, :, :1])], axis=2)
    inside = (lax.broadcasted_iota(jnp.int32, volume.shape, 2) < volume.shape[2] - 1).astype(
        jnp.float32
    )
    face_flux = weight_y * limiter(following - volume) * inside
    previous = jnp.concatenate([jnp.zeros_like(face_flux[:, :, :1]), face_flux[:, :, :-1]], axis=2)
    change = change + face_flux - previous
    following = jnp.concatenate([volume[1:], right_halo[None]], axis=0)
    inside = (x_first + lax.broadcasted_iota(jnp.int32, volume.shape, 0) + 1 < x_total).astype(
        jnp.float32
    )
    face_flux = weight_x * limiter(following - volume) * inside
    lower_flux = left_rim * limiter(volume[0] - left_halo)
    previous = jnp.concatenate([lower_flux[None], face_flux[:-1]], axis=0)
    change = change + face_flux - previous
    return volume + SMOOTH_RATE * change


def shards(volume0, weights, tile_block, tile_count, owner, sino, weight_z, weight_y, weight_x):
    tiles = weights[0, 0]
    slot_count, ray_count, voxels = tiles.shape
    slab_depth, height, column_count = volume0.shape
    blocks = tile_block[0, 0]
    live_count = tile_count[0, 0]
    owner_row = owner[0]
    live_slots = jnp.arange(slot_count, dtype=jnp.int32) < live_count
    select = (owner_row[None, :] == blocks[:, None]) & live_slots[:, None]
    slab_pos = lax.axis_index("slab")
    holder_ids = jnp.arange(owner_row.shape[0], dtype=jnp.int32)
    target = jnp.sum(jnp.where(select, holder_ids[None, :], 0), axis=1)
    distance_ids = jnp.arange(slot_count, dtype=jnp.int32)
    relative = ((target - slab_pos)[:, None] == distance_ids[None, :]) & live_slots[:, None]
    relative_float = relative.astype(jnp.float32)
    far_relative = relative[1:, 1:].astype(jnp.bfloat16)
    flat_tiles = tiles.reshape(slot_count * ray_count, voxels)
    ray_local = jnp.dot(
        flat_tiles, jnp.ones((voxels,), jnp.bfloat16), preferred_element_type=jnp.float32
    )
    ray_sends = jnp.einsum("td,tr->dr", relative_float, ray_local.reshape(slot_count, ray_count))
    ray_total = ray_sends[0]
    for distance in range(1, slot_count):
        ray_total = ray_total + from_behind(ray_sends[distance], "slab", distance)
    live_rows = jnp.repeat(live_slots, ray_count).astype(jnp.bfloat16)
    voxel_local = jnp.dot(live_rows, flat_tiles, preferred_element_type=jnp.float32)
    ray_scale = 1.0 / ray_total
    lower_all = from_behind(weight_z[slab_depth - 1], "slab", 1)
    z_first = slab_pos * slab_depth
    z_total = slab_depth * lax.axis_size("slab")
    groups = lax.axis_size("angle")
    share_width = column_count // groups
    angle_pos = lax.axis_index("angle")
    share_first = angle_pos * share_width

    def share_of(array):
        part = lax.dynamic_slice_in_dim(array, share_first, share_width, array.ndim - 1)
        return jnp.moveaxis(part, -1, 0)

    measured = sino[0, 0].astype(jnp.float32)
    volume = share_of(volume0).astype(jnp.float32)
    local_z = share_of(weight_z)
    local_y = share_of(weight_y)
    local_x = share_of(weight_x)
    lower_rim = share_of(lower_all)
    left_index = jnp.maximum(share_first - 1, 0)
    left_rim = lax.dynamic_index_in_dim(weight_x, left_index, 2, keepdims=False).astype(
        jnp.float32
    ) * (angle_pos > 0).astype(jnp.float32)
    gathered = None
    residual = jnp.zeros((ray_count, column_count), jnp.float32)
    for iteration in range(ITERS):
        if gathered is None:
            flat_volume = volume0.astype(jnp.bfloat16).reshape(voxels, column_count)
            far_products = jnp.einsum(
                "trv,vn->trn", tiles[1:], flat_volume, preferred_element_type=jnp.float32
            ).astype(jnp.bfloat16)
        else:
            far_products = jnp.einsum(
                "trv,nv->trn", tiles[1:], gathered, preferred_element_type=jnp.float32
            ).astype(jnp.bfloat16)
        sends_half = jnp.einsum(
            "td,trn->drn", far_relative, far_products, preferred_element_type=jnp.float32
        ).astype(jnp.bfloat16)
        arrived = [
            from_behind(sends_half[distance - 1], "slab", distance)
            for distance in range(1, slot_count)
        ]
        if gathered is None:
            near_products = jnp.einsum(
                "rv,vn->rn", tiles[0], flat_volume, preferred_element_type=jnp.float32
            )
        else:
            near_products = jnp.einsum(
                "rv,nv->rn", tiles[0], gathered, preferred_element_type=jnp.float32
            )
        near_products = lax.optimization_barrier(near_products.astype(jnp.bfloat16))
        projected = near_products.astype(jnp.float32)
        for distance in range(1, slot_count):
            projected = projected + arrived[distance - 1].astype(jnp.float32)
        residual = (measured - projected) * ray_scale[:, None]
        residual_half = residual.astype(jnp.bfloat16)
        nearby = [
            from_behind(residual_half, "slab", -distance) for distance in range(1, slot_count)
        ]
        near_back = lax.optimization_barrier(
            jnp.einsum("rn,rv->nv", residual_half, tiles[0], preferred_element_type=jnp.float32)
        )
        picked = jnp.einsum(
            "td,drn->trn", far_relative, jnp.stack(nearby), preferred_element_type=jnp.float32
        ).astype(jnp.bfloat16)
        back_t = near_back + jnp.einsum(
            "trn,trv->nv", picked, tiles[1:], preferred_element_type=jnp.float32
        )
        if iteration == 0:
            back_own, voxel_total = scatter_angle(
                back_t.reshape(groups, share_width, voxels),
                voxel_local.reshape(slab_depth, height),
            )
            voxel_scale = (1.0 / voxel_total).reshape(1, slab_depth, height)
        else:
            back_own = scatter_angle(back_t.reshape(groups, share_width, voxels))
        volume = volume + voxel_scale * back_own.reshape(share_width, slab_depth, height)
        volume = smooth_share(
            volume,
            local_z,
            local_y,
            local_x,
            lower_rim,
            left_rim,
            z_first,
            z_total,
            share_first,
            column_count,
        )
        if iteration + 1 < ITERS:
            own_half = volume.astype(jnp.bfloat16).reshape(share_width, voxels)
            gathered = gather_angle(own_half, groups).reshape(column_count, voxels)
    volume_out = jnp.moveaxis(volume, 0, -1)
    return (volume_out, residual[None, None])


def solution(mesh):
    in_specs = (
        P("slab", None, None),
        P("slab", "angle", None, None, None),
        P("slab", "angle", None),
        P("slab", "angle"),
        P("angle", None),
        P("angle", "slab", None, None),
        P("slab", None, None),
        P("slab", None, None),
        P("slab", None, None),
    )
    out_specs = (P("slab", None, "angle"), P("angle", "slab", None, None))
    return jax.shard_map(shards, mesh=mesh, in_specs=in_specs, out_specs=out_specs, check_vma=False)
```

```python
import functools

import jax
import jax.numpy as jnp
from jax import lax
from jax.experimental import pallas as pl
from jax.experimental.pallas import tpu as pltpu
from jax.sharding import PartitionSpec as P

ITERS = 3


SMOOTH_EPS = 0.01
SMOOTH_RATE = 0.15

MESH_ID = pl.DeviceIdType.MESH


def from_behind(value, axis, steps):
    count = lax.axis_size(axis)
    first, last = (max(0, -steps), min(count, count - steps))
    return lax.ppermute(value, axis, [(source, source + steps) for source in range(first, last)])


def limiter(difference):
    return difference / jnp.sqrt(difference * difference + SMOOTH_EPS)


def _where_am_i():
    slab = lax.axis_index("slab")
    here = lax.axis_index("angle")
    chip = here // 2
    core = here % 2
    partner = here + 1 - 2 * core
    return slab, here, chip, core, partner


def _greet(slab, chip, core, partner, n_chip):
    barrier = pltpu.get_barrier_semaphore()
    pl.semaphore_signal(barrier, 1, device_id=(slab, partner), device_id_type=MESH_ID)
    for d in range(1, n_chip):
        peer = ((chip + d) % n_chip) * 2 + core
        pl.semaphore_signal(barrier, 1, device_id=(slab, peer), device_id_type=MESH_ID)
    pl.semaphore_wait(barrier, n_chip)


def _scatter_kernel(n_chip, with_extra, *refs):
    if with_extra:
        (part_ref, half_ref, extra_ref, out_ref, extra_out, got_pair, got_ring, chip_sum,
         send_a, recv_a, send_b, recv_b, extra_pair, extra_ring, extra_chip,
         send_c, recv_c) = refs
    else:
        (part_ref, half_ref, out_ref, got_pair, got_ring, chip_sum,
         send_a, recv_a, send_b, recv_b) = refs
    slab, here, chip, core, partner = _where_am_i()
    _greet(slab, chip, core, partner, n_chip)
    if with_extra:
        extra_copy = pltpu.make_async_remote_copy(
            src_ref=extra_ref,
            dst_ref=extra_pair,
            send_sem=send_c.at[0],
            recv_sem=recv_c.at[0],
            device_id=(slab, partner),
            device_id_type=MESH_ID,
        )
        extra_copy.start()
    order = list(range(1, n_chip)) + [0]
    pair = []
    for i, d in enumerate(order):
        dest = (chip + d) % n_chip
        copy = pltpu.make_async_remote_copy(
            src_ref=half_ref.at[2 * dest + 1 - core],
            dst_ref=got_pair.at[i],
            send_sem=send_a.at[i],
            recv_sem=recv_a.at[i],
            device_id=(slab, partner),
            device_id_type=MESH_ID,
        )
        copy.start()
        pair.append(copy)
    extra_sends = []
    if with_extra:
        extra_copy.wait()
        extra_chip[...] = extra_ref[...] + extra_pair[...]
        for d in range(1, n_chip):
            dest = (chip + d) % n_chip
            copy = pltpu.make_async_remote_copy(
                src_ref=extra_chip,
                dst_ref=extra_ring.at[d],
                send_sem=send_c.at[d],
                recv_sem=recv_c.at[d],
                device_id=(slab, 2 * dest + core),
                device_id_type=MESH_ID,
            )
            copy.start()
            extra_sends.append(copy)
    ring = []
    for i, d in enumerate(order[:-1]):
        dest = (chip + d) % n_chip
        pair[i].wait_recv()
        chip_sum[i] = (
            part_ref[2 * dest + core] + got_pair[i].astype(jnp.float32)
        ).astype(chip_sum.dtype)
        copy = pltpu.make_async_remote_copy(
            src_ref=chip_sum.at[i],
            dst_ref=got_ring.at[d],
            send_sem=send_b.at[d],
            recv_sem=recv_b.at[d],
            device_id=(slab, 2 * dest + core),
            device_id_type=MESH_ID,
        )
        copy.start()
        ring.append(copy)
    pair[-1].wait_recv()
    total = part_ref[here] + got_pair[n_chip - 1].astype(jnp.float32)
    for copy in pair:
        copy.wait_send()
    for copy in ring:
        copy.wait()
    for d in range(1, n_chip):
        total = total + got_ring[d].astype(jnp.float32)
    out_ref[...] = total
    if with_extra:
        for copy in extra_sends:
            copy.wait()
        extra_total = extra_chip[...]
        for d in range(1, n_chip):
            extra_total = extra_total + extra_ring[d]
        extra_out[...] = extra_total


def scatter_angle(part, extra=None):
    blocks, rows, cols = part.shape
    n_chip = blocks // 2
    link = part.dtype
    with_extra = extra is not None
    scratch = [
        pltpu.VMEM((n_chip, rows, cols), link),
        pltpu.VMEM((n_chip, rows, cols), link),
        pltpu.VMEM((n_chip, rows, cols), link),
        pltpu.SemaphoreType.DMA((n_chip,)),
        pltpu.SemaphoreType.DMA((n_chip,)),
        pltpu.SemaphoreType.DMA((n_chip,)),
        pltpu.SemaphoreType.DMA((n_chip,)),
    ]
    operands = [part, part.astype(link)]
    out_shape = [jax.ShapeDtypeStruct((rows, cols), jnp.float32)]
    if with_extra:
        scratch += [
            pltpu.VMEM(extra.shape, extra.dtype),
            pltpu.VMEM((n_chip,) + extra.shape, extra.dtype),
            pltpu.VMEM(extra.shape, extra.dtype),
            pltpu.SemaphoreType.DMA((n_chip,)),
            pltpu.SemaphoreType.DMA((n_chip,)),
        ]
        operands.append(extra)
        out_shape.append(jax.ShapeDtypeStruct(extra.shape, extra.dtype))
    result = pl.pallas_call(
        functools.partial(_scatter_kernel, n_chip, with_extra),
        out_shape=tuple(out_shape),
        in_specs=[pl.BlockSpec(memory_space=pltpu.VMEM)] * len(operands),
        out_specs=tuple(pl.BlockSpec(memory_space=pltpu.VMEM) for _ in out_shape),
        scratch_shapes=scratch,
        compiler_params=pltpu.CompilerParams(
            collective_id=5 if with_extra else 0, has_side_effects=True
        ),
        cost_estimate=pl.CostEstimate(
            flops=2 * blocks * rows * cols, bytes_accessed=4 * 3 * blocks * rows * cols,
            transcendentals=0,
        ),
    )(*operands)
    return result if with_extra else result[0]


def _sum_kernel(groups, part_ref, out_ref, got, send_sem, recv_sem):
    slab = lax.axis_index("slab")
    here = lax.axis_index("angle")
    barrier = pltpu.get_barrier_semaphore()
    for d in range(1, groups):
        peer = (here + d) % groups
        pl.semaphore_signal(barrier, 1, device_id=(slab, peer), device_id_type=MESH_ID)
    pl.semaphore_wait(barrier, groups - 1)
    copies = []
    for d in range(1, groups):
        copy = pltpu.make_async_remote_copy(
            src_ref=part_ref,
            dst_ref=got.at[d],
            send_sem=send_sem.at[d],
            recv_sem=recv_sem.at[d],
            device_id=(slab, (here + d) % groups),
            device_id_type=MESH_ID,
        )
        copy.start()
        copies.append(copy)
    total = part_ref[...]
    for copy in copies:
        copy.wait()
    for d in range(1, groups):
        total = total + got[d]
    out_ref[...] = total


def sum_angle(part, groups):
    return pl.pallas_call(
        functools.partial(_sum_kernel, groups),
        out_shape=jax.ShapeDtypeStruct(part.shape, part.dtype),
        in_specs=[pl.BlockSpec(memory_space=pltpu.VMEM)],
        out_specs=pl.BlockSpec(memory_space=pltpu.VMEM),
        scratch_shapes=[
            pltpu.VMEM((groups,) + part.shape, part.dtype),
            pltpu.SemaphoreType.DMA((groups,)),
            pltpu.SemaphoreType.DMA((groups,)),
        ],
        compiler_params=pltpu.CompilerParams(collective_id=2, has_side_effects=True),
        cost_estimate=pl.CostEstimate(
            flops=groups * part.size, bytes_accessed=4 * 2 * groups * part.size,
            transcendentals=0,
        ),
    )(part)


def _gather_kernel(n_chip, own_ref, out_ref, held, send_a, recv_a, send_b, recv_b, local_sem):
    slab, here, chip, core, partner = _where_am_i()
    _greet(slab, chip, core, partner, n_chip)
    mine = pltpu.make_async_copy(own_ref, held.at[here], local_sem.at[0])
    mine.start()
    pair = [
        pltpu.make_async_remote_copy(
            src_ref=own_ref,
            dst_ref=held.at[here],
            send_sem=send_b.at[0],
            recv_sem=recv_b.at[0],
            device_id=(slab, partner),
            device_id_type=MESH_ID,
        )
    ]
    pair[0].start()
    ring = [None]
    for d in range(1, n_chip):
        dest = (chip + d) % n_chip
        copy = pltpu.make_async_remote_copy(
            src_ref=own_ref,
            dst_ref=held.at[here],
            send_sem=send_a.at[d],
            recv_sem=recv_a.at[d],
            device_id=(slab, 2 * dest + core),
            device_id_type=MESH_ID,
        )
        copy.start()
        ring.append(copy)
    for d in range(1, n_chip):
        ring[d].wait_recv()
        block = 2 * ((chip - d + n_chip) % n_chip) + core
        copy = pltpu.make_async_remote_copy(
            src_ref=held.at[block],
            dst_ref=held.at[block],
            send_sem=send_b.at[d],
            recv_sem=recv_b.at[d],
            device_id=(slab, partner),
            device_id_type=MESH_ID,
        )
        copy.start()
        pair.append(copy)
    mine.wait()
    for d in range(1, n_chip):
        ring[d].wait_send()
    for copy in pair:
        copy.wait()
    out_ref[...] = held[...]


def gather_angle(own, groups):
    rows, cols = own.shape
    n_chip = groups // 2
    return pl.pallas_call(
        functools.partial(_gather_kernel, n_chip),
        out_shape=jax.ShapeDtypeStruct((groups, rows, cols), own.dtype),
        in_specs=[pl.BlockSpec(memory_space=pltpu.VMEM)],
        out_specs=pl.BlockSpec(memory_space=pltpu.VMEM),
        scratch_shapes=[
            pltpu.VMEM((groups, rows, cols), own.dtype),
            pltpu.SemaphoreType.DMA((n_chip,)),
            pltpu.SemaphoreType.DMA((n_chip,)),
            pltpu.SemaphoreType.DMA((n_chip,)),
            pltpu.SemaphoreType.DMA((n_chip,)),
            pltpu.SemaphoreType.DMA((1,)),
        ],
        compiler_params=pltpu.CompilerParams(collective_id=1, has_side_effects=True),
        cost_estimate=pl.CostEstimate(
            flops=0, bytes_accessed=2 * 2 * groups * rows * cols, transcendentals=0,
        ),
    )(own)


def smooth_share(
    volume,
    weight_z,
    weight_y,
    weight_x,
    lower_rim,
    left_rim,
    z_first,
    z_total,
    x_first,
    x_total,
):
    upper_halo = from_behind(volume[:, 0], "slab", -1)
    lower_halo = from_behind(volume[:, -1], "slab", 1)
    right_halo = from_behind(volume[0], "angle", -1)
    left_halo = from_behind(volume[-1], "angle", 1)
    upper = jnp.concatenate([volume[:, 1:], upper_halo[:, None]], axis=1)
    inside = (z_first + lax.broadcasted_iota(jnp.int32, volume.shape, 1) + 1 < z_total).astype(
        jnp.float32
    )
    face_flux = weight_z * limiter(upper - volume) * inside
    lower_flux = lower_rim * limiter(volume[:, 0] - lower_halo)
    previous = jnp.concatenate([lower_flux[:, None], face_flux[:, :-1]], axis=1)
    change = face_flux - previous
    following = jnp.concatenate([volume[:, :, 1:], jnp.zeros_like(volume[:, :, :1])], axis=2)
    inside = (lax.broadcasted_iota(jnp.int32, volume.shape, 2) < volume.shape[2] - 1).astype(
        jnp.float32
    )
    face_flux = weight_y * limiter(following - volume) * inside
    previous = jnp.concatenate([jnp.zeros_like(face_flux[:, :, :1]), face_flux[:, :, :-1]], axis=2)
    change = change + face_flux - previous
    following = jnp.concatenate([volume[1:], right_halo[None]], axis=0)
    inside = (x_first + lax.broadcasted_iota(jnp.int32, volume.shape, 0) + 1 < x_total).astype(
        jnp.float32
    )
    face_flux = weight_x * limiter(following - volume) * inside
    lower_flux = left_rim * limiter(volume[0] - left_halo)
    previous = jnp.concatenate([lower_flux[None], face_flux[:-1]], axis=0)
    change = change + face_flux - previous
    return volume + SMOOTH_RATE * change


def shards(volume0, weights, tile_block, tile_count, owner, sino, weight_z, weight_y, weight_x):
    tiles = weights[0, 0]
    slot_count, ray_count, voxels = tiles.shape
    slab_depth, height, column_count = volume0.shape
    blocks = tile_block[0, 0]
    live_count = tile_count[0, 0]
    owner_row = owner[0]
    live_slots = jnp.arange(slot_count, dtype=jnp.int32) < live_count
    select = (owner_row[None, :] == blocks[:, None]) & live_slots[:, None]
    slab_pos = lax.axis_index("slab")
    holder_ids = jnp.arange(owner_row.shape[0], dtype=jnp.int32)
    target = jnp.sum(jnp.where(select, holder_ids[None, :], 0), axis=1)
    distance_ids = jnp.arange(slot_count, dtype=jnp.int32)
    relative = ((target - slab_pos)[:, None] == distance_ids[None, :]) & live_slots[:, None]
    relative_float = relative.astype(jnp.float32)
    far_relative = relative[1:, 1:].astype(jnp.bfloat16)
    flat_tiles = tiles.reshape(slot_count * ray_count, voxels)
    ray_local = jnp.dot(
        flat_tiles, jnp.ones((voxels,), jnp.bfloat16), preferred_element_type=jnp.float32
    )
    ray_sends = jnp.einsum("td,tr->dr", relative_float, ray_local.reshape(slot_count, ray_count))
    ray_total = ray_sends[0]
    for distance in range(1, slot_count):
        ray_total = ray_total + from_behind(ray_sends[distance], "slab", distance)
    live_rows = jnp.repeat(live_slots, ray_count).astype(jnp.bfloat16)
    voxel_local = jnp.dot(live_rows, flat_tiles, preferred_element_type=jnp.float32)
    ray_scale = 1.0 / ray_total
    lower_all = from_behind(weight_z[slab_depth - 1], "slab", 1)
    z_first = slab_pos * slab_depth
    z_total = slab_depth * lax.axis_size("slab")
    groups = lax.axis_size("angle")
    share_width = column_count // groups
    angle_pos = lax.axis_index("angle")
    share_first = angle_pos * share_width

    def share_of(array):
        part = lax.dynamic_slice_in_dim(array, share_first, share_width, array.ndim - 1)
        return jnp.moveaxis(part, -1, 0)

    measured = sino[0, 0].astype(jnp.float32)
    left_index = jnp.maximum(share_first - 1, 0)
    left_rim = lax.dynamic_index_in_dim(weight_x, left_index, 2, keepdims=False).astype(
        jnp.float32
    ) * (angle_pos > 0).astype(jnp.float32)
    gathered = None
    residual = jnp.zeros((ray_count, column_count), jnp.float32)
    for iteration in range(ITERS):
        if gathered is None:
            flat_volume = volume0.astype(jnp.bfloat16).reshape(voxels, column_count)
            far_products = jnp.einsum(
                "trv,vn->trn", tiles[1:], flat_volume, preferred_element_type=jnp.float32
            ).astype(jnp.bfloat16)
        else:
            far_products = jnp.einsum(
                "trv,nv->trn", tiles[1:], gathered, preferred_element_type=jnp.float32
            ).astype(jnp.bfloat16)
        sends_half = jnp.einsum(
            "td,trn->drn", far_relative, far_products, preferred_element_type=jnp.float32
        ).astype(jnp.bfloat16)
        arrived = [
            from_behind(sends_half[distance - 1], "slab", distance)
            for distance in range(1, slot_count)
        ]
        if gathered is None:
            near_products = jnp.einsum(
                "rv,vn->rn", tiles[0], flat_volume, preferred_element_type=jnp.float32
            )
        else:
            near_products = jnp.einsum(
                "rv,nv->rn", tiles[0], gathered, preferred_element_type=jnp.float32
            )
        near_products = lax.optimization_barrier(near_products.astype(jnp.bfloat16))
        projected = near_products.astype(jnp.float32)
        for distance in range(1, slot_count):
            projected = projected + arrived[distance - 1].astype(jnp.float32)
        residual = (measured - projected) * ray_scale[:, None]
        residual_half = residual.astype(jnp.bfloat16)
        if iteration == 0:
            residual_half, late = lax.optimization_barrier(
                (residual_half, (volume0, weight_z, weight_y, weight_x, lower_all))
            )
            volume = share_of(late[0]).astype(jnp.float32)
            local_z = share_of(late[1])
            local_y = share_of(late[2])
            local_x = share_of(late[3])
            lower_rim = share_of(late[4])
        nearby = [
            from_behind(residual_half, "slab", -distance) for distance in range(1, slot_count)
        ]
        near_back = lax.optimization_barrier(
            jnp.einsum("rn,rv->nv", residual_half, tiles[0], preferred_element_type=jnp.float32)
        )
        picked = jnp.einsum(
            "td,drn->trn", far_relative, jnp.stack(nearby), preferred_element_type=jnp.float32
        ).astype(jnp.bfloat16)
        back_t = near_back + jnp.einsum(
            "trn,trv->nv", picked, tiles[1:], preferred_element_type=jnp.float32
        )
        if iteration == 0:
            back_own, voxel_total = scatter_angle(
                back_t.reshape(groups, share_width, voxels),
                voxel_local.reshape(slab_depth, height),
            )
            voxel_scale = (1.0 / voxel_total).reshape(1, slab_depth, height)
        else:
            back_own = scatter_angle(back_t.reshape(groups, share_width, voxels))
        volume = volume + voxel_scale * back_own.reshape(share_width, slab_depth, height)
        volume = smooth_share(
            volume,
            local_z,
            local_y,
            local_x,
            lower_rim,
            left_rim,
            z_first,
            z_total,
            share_first,
            column_count,
        )
        if iteration + 1 < ITERS:
            own_half = volume.astype(jnp.bfloat16).reshape(share_width, voxels)
            gathered = gather_angle(own_half, groups).reshape(column_count, voxels)
    volume_out = jnp.moveaxis(volume, 0, -1)
    return (volume_out, residual[None, None])


def solution(mesh):
    in_specs = (
        P("slab", None, None),
        P("slab", "angle", None, None, None),
        P("slab", "angle", None),
        P("slab", "angle"),
        P("angle", None),
        P("angle", "slab", None, None),
        P("slab", None, None),
        P("slab", None, None),
        P("slab", None, None),
    )
    out_specs = (P("slab", None, "angle"), P("angle", "slab", None, None))
    return jax.shard_map(shards, mesh=mesh, in_specs=in_specs, out_specs=out_specs, check_vma=False)
```

```python
import functools

import jax
import jax.numpy as jnp
from jax import lax
from jax.experimental import pallas as pl
from jax.experimental.pallas import tpu as pltpu
from jax.sharding import PartitionSpec as P

ITERS = 3


SMOOTH_EPS = 0.01
SMOOTH_RATE = 0.15

MESH_ID = pl.DeviceIdType.MESH


def from_behind(value, axis, steps):
    count = lax.axis_size(axis)
    first, last = (max(0, -steps), min(count, count - steps))
    return lax.ppermute(value, axis, [(source, source + steps) for source in range(first, last)])


def limiter(difference):
    return difference / jnp.sqrt(difference * difference + SMOOTH_EPS)


def _where_am_i():
    slab = lax.axis_index("slab")
    here = lax.axis_index("angle")
    chip = here // 2
    core = here % 2
    partner = here + 1 - 2 * core
    return slab, here, chip, core, partner


def _greet(slab, chip, core, partner, n_chip):
    barrier = pltpu.get_barrier_semaphore()
    pl.semaphore_signal(barrier, 1, device_id=(slab, partner), device_id_type=MESH_ID)
    for d in range(1, n_chip):
        peer = ((chip + d) % n_chip) * 2 + core
        pl.semaphore_signal(barrier, 1, device_id=(slab, peer), device_id_type=MESH_ID)
    pl.semaphore_wait(barrier, n_chip)


def _scatter_kernel(n_chip, with_extra, *refs):
    if with_extra:
        (part_ref, half_ref, extra_ref, out_ref, extra_out, got_pair, got_ring, chip_sum,
         send_a, recv_a, send_b, recv_b, extra_pair, extra_ring, extra_chip,
         send_c, recv_c) = refs
    else:
        (part_ref, half_ref, out_ref, got_pair, got_ring, chip_sum,
         send_a, recv_a, send_b, recv_b) = refs
    slab, here, chip, core, partner = _where_am_i()
    _greet(slab, chip, core, partner, n_chip)
    if with_extra:
        extra_copy = pltpu.make_async_remote_copy(
            src_ref=extra_ref,
            dst_ref=extra_pair,
            send_sem=send_c.at[0],
            recv_sem=recv_c.at[0],
            device_id=(slab, partner),
            device_id_type=MESH_ID,
        )
        extra_copy.start()
    order = list(range(1, n_chip)) + [0]
    pair = []
    for i, d in enumerate(order):
        dest = (chip + d) % n_chip
        copy = pltpu.make_async_remote_copy(
            src_ref=half_ref.at[2 * dest + 1 - core],
            dst_ref=got_pair.at[i],
            send_sem=send_a.at[i],
            recv_sem=recv_a.at[i],
            device_id=(slab, partner),
            device_id_type=MESH_ID,
        )
        copy.start()
        pair.append(copy)
    extra_sends = []
    if with_extra:
        extra_copy.wait()
        extra_chip[...] = extra_ref[...] + extra_pair[...]
        for d in range(1, n_chip):
            dest = (chip + d) % n_chip
            copy = pltpu.make_async_remote_copy(
                src_ref=extra_chip,
                dst_ref=extra_ring.at[d],
                send_sem=send_c.at[d],
                recv_sem=recv_c.at[d],
                device_id=(slab, 2 * dest + core),
                device_id_type=MESH_ID,
            )
            copy.start()
            extra_sends.append(copy)
    ring = []
    for i, d in enumerate(order[:-1]):
        dest = (chip + d) % n_chip
        pair[i].wait_recv()
        chip_sum[i] = (
            part_ref[2 * dest + core] + got_pair[i].astype(jnp.float32)
        ).astype(chip_sum.dtype)
        copy = pltpu.make_async_remote_copy(
            src_ref=chip_sum.at[i],
            dst_ref=got_ring.at[d],
            send_sem=send_b.at[d],
            recv_sem=recv_b.at[d],
            device_id=(slab, 2 * dest + core),
            device_id_type=MESH_ID,
        )
        copy.start()
        ring.append(copy)
    pair[-1].wait_recv()
    total = part_ref[here] + got_pair[n_chip - 1].astype(jnp.float32)
    for copy in pair:
        copy.wait_send()
    for copy in ring:
        copy.wait()
    for d in range(1, n_chip):
        total = total + got_ring[d].astype(jnp.float32)
    out_ref[...] = total
    if with_extra:
        for copy in extra_sends:
            copy.wait()
        extra_total = extra_chip[...]
        for d in range(1, n_chip):
            extra_total = extra_total + extra_ring[d]
        extra_out[...] = extra_total


def scatter_angle(part, extra=None):
    blocks, rows, cols = part.shape
    n_chip = blocks // 2
    link = part.dtype
    with_extra = extra is not None
    scratch = [
        pltpu.VMEM((n_chip, rows, cols), link),
        pltpu.VMEM((n_chip, rows, cols), link),
        pltpu.VMEM((n_chip, rows, cols), link),
        pltpu.SemaphoreType.DMA((n_chip,)),
        pltpu.SemaphoreType.DMA((n_chip,)),
        pltpu.SemaphoreType.DMA((n_chip,)),
        pltpu.SemaphoreType.DMA((n_chip,)),
    ]
    operands = [part, part.astype(link)]
    out_shape = [jax.ShapeDtypeStruct((rows, cols), jnp.float32)]
    if with_extra:
        scratch += [
            pltpu.VMEM(extra.shape, extra.dtype),
            pltpu.VMEM((n_chip,) + extra.shape, extra.dtype),
            pltpu.VMEM(extra.shape, extra.dtype),
            pltpu.SemaphoreType.DMA((n_chip,)),
            pltpu.SemaphoreType.DMA((n_chip,)),
        ]
        operands.append(extra)
        out_shape.append(jax.ShapeDtypeStruct(extra.shape, extra.dtype))
    result = pl.pallas_call(
        functools.partial(_scatter_kernel, n_chip, with_extra),
        out_shape=tuple(out_shape),
        in_specs=[pl.BlockSpec(memory_space=pltpu.VMEM)] * len(operands),
        out_specs=tuple(pl.BlockSpec(memory_space=pltpu.VMEM) for _ in out_shape),
        scratch_shapes=scratch,
        compiler_params=pltpu.CompilerParams(
            collective_id=5 if with_extra else 0, has_side_effects=True
        ),
        cost_estimate=pl.CostEstimate(
            flops=2 * blocks * rows * cols, bytes_accessed=4 * 3 * blocks * rows * cols,
            transcendentals=0,
        ),
    )(*operands)
    return result if with_extra else result[0]


def _sum_kernel(groups, part_ref, out_ref, got, send_sem, recv_sem):
    slab = lax.axis_index("slab")
    here = lax.axis_index("angle")
    barrier = pltpu.get_barrier_semaphore()
    for d in range(1, groups):
        peer = (here + d) % groups
        pl.semaphore_signal(barrier, 1, device_id=(slab, peer), device_id_type=MESH_ID)
    pl.semaphore_wait(barrier, groups - 1)
    copies = []
    for d in range(1, groups):
        copy = pltpu.make_async_remote_copy(
            src_ref=part_ref,
            dst_ref=got.at[d],
            send_sem=send_sem.at[d],
            recv_sem=recv_sem.at[d],
            device_id=(slab, (here + d) % groups),
            device_id_type=MESH_ID,
        )
        copy.start()
        copies.append(copy)
    total = part_ref[...]
    for copy in copies:
        copy.wait()
    for d in range(1, groups):
        total = total + got[d]
    out_ref[...] = total


def sum_angle(part, groups):
    return pl.pallas_call(
        functools.partial(_sum_kernel, groups),
        out_shape=jax.ShapeDtypeStruct(part.shape, part.dtype),
        in_specs=[pl.BlockSpec(memory_space=pltpu.VMEM)],
        out_specs=pl.BlockSpec(memory_space=pltpu.VMEM),
        scratch_shapes=[
            pltpu.VMEM((groups,) + part.shape, part.dtype),
            pltpu.SemaphoreType.DMA((groups,)),
            pltpu.SemaphoreType.DMA((groups,)),
        ],
        compiler_params=pltpu.CompilerParams(collective_id=2, has_side_effects=True),
        cost_estimate=pl.CostEstimate(
            flops=groups * part.size, bytes_accessed=4 * 2 * groups * part.size,
            transcendentals=0,
        ),
    )(part)


def _gather_kernel(n_chip, own_ref, out_ref, held, send_a, recv_a, send_b, recv_b, local_sem):
    slab, here, chip, core, partner = _where_am_i()
    _greet(slab, chip, core, partner, n_chip)
    mine = pltpu.make_async_copy(own_ref, held.at[here], local_sem.at[0])
    mine.start()
    pair = [
        pltpu.make_async_remote_copy(
            src_ref=own_ref,
            dst_ref=held.at[here],
            send_sem=send_b.at[0],
            recv_sem=recv_b.at[0],
            device_id=(slab, partner),
            device_id_type=MESH_ID,
        )
    ]
    pair[0].start()
    ring = [None]
    for d in range(1, n_chip):
        dest = (chip + d) % n_chip
        copy = pltpu.make_async_remote_copy(
            src_ref=own_ref,
            dst_ref=held.at[here],
            send_sem=send_a.at[d],
            recv_sem=recv_a.at[d],
            device_id=(slab, 2 * dest + core),
            device_id_type=MESH_ID,
        )
        copy.start()
        ring.append(copy)
    for d in range(1, n_chip):
        ring[d].wait_recv()
        block = 2 * ((chip - d + n_chip) % n_chip) + core
        copy = pltpu.make_async_remote_copy(
            src_ref=held.at[block],
            dst_ref=held.at[block],
            send_sem=send_b.at[d],
            recv_sem=recv_b.at[d],
            device_id=(slab, partner),
            device_id_type=MESH_ID,
        )
        copy.start()
        pair.append(copy)
    mine.wait()
    for d in range(1, n_chip):
        ring[d].wait_send()
    for copy in pair:
        copy.wait()
    out_ref[...] = held[...]


def gather_angle(own, groups):
    rows, cols = own.shape
    n_chip = groups // 2
    return pl.pallas_call(
        functools.partial(_gather_kernel, n_chip),
        out_shape=jax.ShapeDtypeStruct((groups, rows, cols), own.dtype),
        in_specs=[pl.BlockSpec(memory_space=pltpu.VMEM)],
        out_specs=pl.BlockSpec(memory_space=pltpu.VMEM),
        scratch_shapes=[
            pltpu.VMEM((groups, rows, cols), own.dtype),
            pltpu.SemaphoreType.DMA((n_chip,)),
            pltpu.SemaphoreType.DMA((n_chip,)),
            pltpu.SemaphoreType.DMA((n_chip,)),
            pltpu.SemaphoreType.DMA((n_chip,)),
            pltpu.SemaphoreType.DMA((1,)),
        ],
        compiler_params=pltpu.CompilerParams(collective_id=1, has_side_effects=True),
        cost_estimate=pl.CostEstimate(
            flops=0, bytes_accessed=2 * 2 * groups * rows * cols, transcendentals=0,
        ),
    )(own)


def smooth_share(
    volume,
    weight_z,
    weight_y,
    weight_x,
    lower_rim,
    left_rim,
    z_first,
    z_total,
    x_first,
    x_total,
):
    upper_halo = from_behind(volume[:, 0], "slab", -1)
    lower_halo = from_behind(volume[:, -1], "slab", 1)
    right_halo = from_behind(volume[0], "angle", -1)
    left_halo = from_behind(volume[-1], "angle", 1)
    upper = jnp.concatenate([volume[:, 1:], upper_halo[:, None]], axis=1)
    inside = (z_first + lax.broadcasted_iota(jnp.int32, volume.shape, 1) + 1 < z_total).astype(
        jnp.float32
    )
    face_flux = weight_z * limiter(upper - volume) * inside
    lower_flux = lower_rim * limiter(volume[:, 0] - lower_halo)
    previous = jnp.concatenate([lower_flux[:, None], face_flux[:, :-1]], axis=1)
    change = face_flux - previous
    following = jnp.concatenate([volume[:, :, 1:], jnp.zeros_like(volume[:, :, :1])], axis=2)
    inside = (lax.broadcasted_iota(jnp.int32, volume.shape, 2) < volume.shape[2] - 1).astype(
        jnp.float32
    )
    face_flux = weight_y * limiter(following - volume) * inside
    previous = jnp.concatenate([jnp.zeros_like(face_flux[:, :, :1]), face_flux[:, :, :-1]], axis=2)
    change = change + face_flux - previous
    following = jnp.concatenate([volume[1:], right_halo[None]], axis=0)
    inside = (x_first + lax.broadcasted_iota(jnp.int32, volume.shape, 0) + 1 < x_total).astype(
        jnp.float32
    )
    face_flux = weight_x * limiter(following - volume) * inside
    lower_flux = left_rim * limiter(volume[0] - left_halo)
    previous = jnp.concatenate([lower_flux[None], face_flux[:-1]], axis=0)
    change = change + face_flux - previous
    return volume + SMOOTH_RATE * change


def shards(volume0, weights, tile_block, tile_count, owner, sino, weight_z, weight_y, weight_x):
    tiles = weights[0, 0]
    slot_count, ray_count, voxels = tiles.shape
    slab_depth, height, column_count = volume0.shape
    blocks = tile_block[0, 0]
    live_count = tile_count[0, 0]
    owner_row = owner[0]
    live_slots = jnp.arange(slot_count, dtype=jnp.int32) < live_count
    select = (owner_row[None, :] == blocks[:, None]) & live_slots[:, None]
    slab_pos = lax.axis_index("slab")
    holder_ids = jnp.arange(owner_row.shape[0], dtype=jnp.int32)
    target = jnp.sum(jnp.where(select, holder_ids[None, :], 0), axis=1)
    distance_ids = jnp.arange(slot_count, dtype=jnp.int32)
    relative = ((target - slab_pos)[:, None] == distance_ids[None, :]) & live_slots[:, None]
    relative_float = relative.astype(jnp.float32)
    far_relative = relative[1:, 1:].astype(jnp.bfloat16)
    flat_tiles = tiles.reshape(slot_count * ray_count, voxels)
    ray_local = jnp.dot(
        flat_tiles, jnp.ones((voxels,), jnp.bfloat16), preferred_element_type=jnp.float32
    )
    ray_sends = jnp.einsum("td,tr->dr", relative_float, ray_local.reshape(slot_count, ray_count))
    ray_total = ray_sends[0]
    for distance in range(1, slot_count):
        ray_total = ray_total + from_behind(ray_sends[distance], "slab", distance)
    live_rows = jnp.repeat(live_slots, ray_count).astype(jnp.bfloat16)
    voxel_local = jnp.dot(live_rows, flat_tiles, preferred_element_type=jnp.float32)
    ray_scale = 1.0 / ray_total
    lower_all = from_behind(weight_z[slab_depth - 1], "slab", 1)
    z_first = slab_pos * slab_depth
    z_total = slab_depth * lax.axis_size("slab")
    groups = lax.axis_size("angle")
    share_width = column_count // groups
    angle_pos = lax.axis_index("angle")
    share_first = angle_pos * share_width

    def share_of(array):
        part = lax.dynamic_slice_in_dim(array, share_first, share_width, array.ndim - 1)
        return jnp.moveaxis(part, -1, 0)

    measured = sino[0, 0].astype(jnp.float32)
    left_index = jnp.maximum(share_first - 1, 0)
    gathered = None
    residual = jnp.zeros((ray_count, column_count), jnp.float32)
    for iteration in range(ITERS):
        if gathered is None:
            flat_volume = volume0.astype(jnp.bfloat16).reshape(voxels, column_count)
            far_products = jnp.einsum(
                "trv,vn->trn", tiles[1:], flat_volume, preferred_element_type=jnp.float32
            ).astype(jnp.bfloat16)
        else:
            far_products = jnp.einsum(
                "trv,nv->trn", tiles[1:], gathered, preferred_element_type=jnp.float32
            ).astype(jnp.bfloat16)
        sends_half = jnp.einsum(
            "td,trn->drn", far_relative, far_products, preferred_element_type=jnp.float32
        ).astype(jnp.bfloat16)
        arrived = [
            from_behind(sends_half[distance - 1], "slab", distance)
            for distance in range(1, slot_count)
        ]
        if gathered is None:
            near_products = jnp.einsum(
                "rv,vn->rn", tiles[0], flat_volume, preferred_element_type=jnp.float32
            )
        else:
            near_products = jnp.einsum(
                "rv,nv->rn", tiles[0], gathered, preferred_element_type=jnp.float32
            )
        near_products = lax.optimization_barrier(near_products.astype(jnp.bfloat16))
        projected = near_products.astype(jnp.float32)
        for distance in range(1, slot_count):
            projected = projected + arrived[distance - 1].astype(jnp.float32)
        residual = (measured - projected) * ray_scale[:, None]
        residual_half = residual.astype(jnp.bfloat16)
        if iteration == 0:
            residual_half, late = lax.optimization_barrier(
                (residual_half, (volume0, weight_z, weight_y, weight_x, lower_all))
            )
            volume = share_of(late[0]).astype(jnp.float32)
            local_z = share_of(late[1])
            local_y = share_of(late[2])
            local_x = share_of(late[3])
            lower_rim = share_of(late[4])
            left_rim = lax.dynamic_index_in_dim(late[3], left_index, 2, keepdims=False).astype(
                jnp.float32
            ) * (angle_pos > 0).astype(jnp.float32)
        nearby = [
            from_behind(residual_half, "slab", -distance) for distance in range(1, slot_count)
        ]
        near_back = lax.optimization_barrier(
            jnp.einsum("rn,rv->nv", residual_half, tiles[0], preferred_element_type=jnp.float32)
        )
        picked = jnp.einsum(
            "td,drn->trn", far_relative, jnp.stack(nearby), preferred_element_type=jnp.float32
        ).astype(jnp.bfloat16)
        back_t = near_back + jnp.einsum(
            "trn,trv->nv", picked, tiles[1:], preferred_element_type=jnp.float32
        )
        if iteration == 0:
            back_own, voxel_total = scatter_angle(
                back_t.reshape(groups, share_width, voxels),
                voxel_local.reshape(slab_depth, height),
            )
            voxel_scale = (1.0 / voxel_total).reshape(1, slab_depth, height)
        else:
            back_own = scatter_angle(back_t.reshape(groups, share_width, voxels))
        volume = volume + voxel_scale * back_own.reshape(share_width, slab_depth, height)
        volume = smooth_share(
            volume,
            local_z,
            local_y,
            local_x,
            lower_rim,
            left_rim,
            z_first,
            z_total,
            share_first,
            column_count,
        )
        if iteration + 1 < ITERS:
            own_half = volume.astype(jnp.bfloat16).reshape(share_width, voxels)
            gathered = gather_angle(own_half, groups).reshape(column_count, voxels)
    volume_out = jnp.moveaxis(volume, 0, -1)
    return (volume_out, residual[None, None])


def solution(mesh):
    in_specs = (
        P("slab", None, None),
        P("slab", "angle", None, None, None),
        P("slab", "angle", None),
        P("slab", "angle"),
        P("angle", None),
        P("angle", "slab", None, None),
        P("slab", None, None),
        P("slab", None, None),
        P("slab", None, None),
    )
    out_specs = (P("slab", None, "angle"), P("angle", "slab", None, None))
    return jax.shard_map(shards, mesh=mesh, in_specs=in_specs, out_specs=out_specs, check_vma=False)
```
